32 devices in a mesh: groups: 2 (over x), tm: 8 (over z, y), tile: 2 (over core).
Axes of the slice: x: 2, y: 2, z: 4, core: 2. Of those that a mesh axis runs over, the one named last changes fastest.
Arguments:
- movie: bfloat16 [4, 2304, 4096], P(('groups', 'tile'), None, 'tm'), parts along dimension 0, may hold values from 0 to 4
- cycle_weights: bfloat16 [4, 2304, 56], P(('groups', 'tile')), parts along dimension 0, may hold values from -0.75 to 0.75
- footprints: bfloat16 [4, 2304, 384], P(('groups', 'tile')), parts along dimension 0, may hold values from 0.19921875 to 1
- traces: bfloat16 [4, 384, 4096], P(('groups', 'tile'), None, 'tm'), parts along dimension 0, may hold values from 0 to 1.5
- centre_row: int32 [4, 384], P(('groups', 'tile')), parts along dimension 0, may hold values from 0 to 47
- centre_col: int32 [4, 384], P(('groups', 'tile')), parts along dimension 0, may hold values from 0 to 47
- radius: int32 [4, 384], P(('groups', 'tile')), parts along dimension 0, may hold values from 4 to 9
- comp_count: int32 [4], P(('groups', 'tile')), parts along dimension 0, may hold values from 64 to 384
Outputs:
- new_footprints: bfloat16 [4, 2304, 384], P(('groups', 'tile')), parts along dimension 0
- new_traces: bfloat16 [4, 384, 4096], P(('groups', 'tile'), None, 'tm'), parts along dimension 0
The draws below stay inside these ranges and needn't reach their ends.
There are 2 independent parts, one for each index of `groups`. The reference program is written for one: setup_inputs(seed, part) draws one part's arguments, and reference() takes and returns one part's arrays. A program takes and returns all parts, laid end to end along the dimension named above; each array names one. Nothing has to cross between parts.
All inputs are finite; a program needn't handle non-finite values.
Results may differ from the reference program's by a relative error of at most 0.0034.
Values may be sent and summed in bfloat16 or wider, within the bound.
No kernel may reach another device: no remote copies, remote signals or barrier semaphores. Data moves between devices by JAX's collectives and lax.ppermute only.
A program may use at most 64 MiB of HBM per device.

```python
import math
import jax
import jax.numpy as jnp
from jax import lax

TILE_SIDE = 48
CYCLE = 8
OFFS = 56
KMAX = 384
PASSES = 2
PIX = 2304
TILES = 2
FRAMES = 4096


def draw_traces(key, part):
    first_key = jax.random.fold_in(jax.random.fold_in(key, 17), 0)
    ramp = 1.0 + 2.0 * jnp.arange(FRAMES, dtype=jnp.float32) / FRAMES
    logs = jax.random.uniform(first_key, (TILES, KMAX, FRAMES), jnp.float32, math.log(0.05), math.log(0.5))
    values = jnp.exp(logs) * ramp[None, None, :]
    return values.astype(jnp.bfloat16)


def place_ends(entries, stream_key, low, largest):
    dims = entries.shape
    index_at = [jax.random.randint(jax.random.fold_in(stream_key, axis), (), 0, dims[axis]) for axis in range(len(dims))]
    entries = entries.at[tuple(index_at)].set(low)
    longest = dims.index(max(dims))
    index_at[longest] = (index_at[longest] + 1) % dims[longest]
    return entries.at[tuple(index_at)].set(largest)


def steps_of(key, extent, shards, least, largest):
    gain, own = 1.0, jax.random.fold_in(key, 6)
    for position, blocks in shards:
        steps = jnp.exp(jax.random.uniform(jax.random.fold_in(own, position), (blocks,), jnp.float32, least / len(shards), largest / len(shards)))
        gain = gain * jnp.repeat(steps, extent[position] // blocks).reshape([-1 if axis == position else 1 for axis in range(len(extent))])
    return gain


def bell_draw(own_key, dims, spread, bound, pieces=(), held_as=jnp.bfloat16):
    array = jax.random.normal(own_key, dims, jnp.float32) * spread
    if len(pieces) > 0:
        array = steps_of(own_key, dims, pieces, -0.22, 0.18) * array
    return jnp.clip(array, min=-bound, max=bound).astype(held_as)


def setup_inputs(seed: int = 0, part: int = 0) -> dict:
    splits = jax.random.split(jax.random.key(seed), 9)
    own_keys = jax.random.split(jax.random.fold_in(splits[8], part), 9)
    return {
        "movie": jnp.clip(4.0 * jax.random.uniform(own_keys[0], (TILES, PIX, FRAMES), jnp.float32) ** steps_of(own_keys[0], (TILES, PIX, FRAMES), ((0, 2), (2, 8)), -0.2, 0.2), 0.0, 4.0).astype(jnp.bfloat16),
        "cycle_weights": bell_draw(own_keys[1], (TILES, PIX, OFFS), OFFS ** -0.5, 0.75, ((0, 2),)),
        "footprints": jnp.clip(0.19921875 + 0.80078125 * jax.random.uniform(own_keys[2], (TILES, PIX, KMAX), jnp.float32) ** steps_of(own_keys[2], (TILES, PIX, KMAX), ((0, 2),), -0.2, 0.2), 0.19921875, 1.0).astype(jnp.bfloat16),
        "traces": draw_traces(jax.random.fold_in(jax.random.fold_in(splits[8], part), 71), part),
        "centre_row": place_ends(jax.random.randint(own_keys[4], (TILES, KMAX), 0, TILE_SIDE), jax.random.fold_in(own_keys[4], 1), 0, TILE_SIDE - 1).astype(jnp.int32),
        "centre_col": place_ends(jax.random.randint(own_keys[5], (TILES, KMAX), 0, TILE_SIDE), jax.random.fold_in(own_keys[5], 1), 0, TILE_SIDE - 1).astype(jnp.int32),
        "radius": place_ends(jax.random.randint(own_keys[6], (TILES, KMAX), TILE_SIDE // 12, TILE_SIDE // 5 + 1), jax.random.fold_in(own_keys[6], 1), TILE_SIDE // 12, (TILE_SIDE // 5 + 1) - 1).astype(jnp.int32),
        "comp_count": jax.random.randint(own_keys[7], (TILES,), KMAX // 6, KMAX + 1).astype(jnp.int32),
    }


RIDGE_TERM = 1.0


def cycle_offsets():
    found = []
    for row_step in range(-CYCLE, CYCLE + 1):
        for col_step in range(-CYCLE, CYCLE + 1):
            dist_sq = row_step * row_step + col_step * col_step
            if CYCLE * CYCLE <= dist_sq < (CYCLE + 1) * (CYCLE + 1):
                found.append((row_step, col_step))
    return found


def cycle_back(weights, window):
    frames = window.shape[2]
    grid_w = weights.reshape(TILE_SIDE, TILE_SIDE, -1)
    total = jnp.zeros((TILE_SIDE, TILE_SIDE, frames), jnp.float32)
    for index, (row_step, col_step) in enumerate(cycle_offsets()):
        top = CYCLE + row_step
        left = CYCLE + col_step
        piece = window[top:top + TILE_SIDE, left:left + TILE_SIDE, :].astype(jnp.float32)
        total = total + grid_w[:, :, index:index + 1].astype(jnp.float32) * piece
    return total.reshape(TILE_SIDE * TILE_SIDE, frames).astype(jnp.bfloat16)


def keep_mask(row_at, col_at, reach, count):
    pixel = jnp.arange(TILE_SIDE * TILE_SIDE, dtype=jnp.int32)
    row_gap = (pixel // TILE_SIDE)[:, None] - row_at[None, :]
    col_gap = (pixel % TILE_SIDE)[:, None] - col_at[None, :]
    inside = row_gap * row_gap + col_gap * col_gap <= (reach * reach)[None, :]
    live = jnp.arange(KMAX, dtype=jnp.int32) < count
    return inside & live[None, :], live


def pad_tiles(resid):
    frames = resid.shape[2]
    blocks = resid.reshape(TILES, TILE_SIDE, TILE_SIDE, frames)
    field = jnp.transpose(blocks, (1, 0, 2, 3)).reshape(TILE_SIDE, TILES * TILE_SIDE, frames)
    padded = jnp.pad(field, ((CYCLE, CYCLE), (CYCLE, CYCLE), (0, 0)))
    pad_len = TILE_SIDE + 2 * CYCLE
    return [padded[:, tile_idx * TILE_SIDE:tile_idx * TILE_SIDE + pad_len, :] for tile_idx in range(TILES)]


def reference(movie, cycle_weights, footprints, traces, centre_row, centre_col, radius, comp_count):
    zero = jnp.zeros((), jnp.bfloat16)
    feet, lives, keeps, trace_now, den_a = [], [], [], [], []
    for tile_idx in range(TILES):
        keep, live = keep_mask(centre_row[tile_idx], centre_col[tile_idx], radius[tile_idx], comp_count[tile_idx])
        foot = jnp.where(keep, footprints[tile_idx], zero)
        feet.append(foot)
        keeps.append(keep)
        lives.append(live)
        trace_now.append(jnp.where(live[:, None], traces[tile_idx], zero))
        den_a.append(jnp.sum(jnp.square(foot.astype(jnp.float32)), axis=0) + RIDGE_TERM)
    movie_f = movie.astype(jnp.float32)
    backs = None
    for sweep in range(PASSES):
        prods = [jnp.dot(feet[tile_idx], trace_now[tile_idx], preferred_element_type=jnp.float32) for tile_idx in range(TILES)]
        resid = jnp.stack([(movie_f[tile_idx] - prods[tile_idx]).astype(jnp.bfloat16) for tile_idx in range(TILES)])
        windows = pad_tiles(resid)
        backs = [cycle_back(cycle_weights[tile_idx], windows[tile_idx]) for tile_idx in range(TILES)]
        updated = []
        for tile_idx in range(TILES):
            err = (prods[tile_idx] + backs[tile_idx].astype(jnp.float32) - movie_f[tile_idx]).astype(jnp.bfloat16)
            grad = lax.dot_general(feet[tile_idx], err, (((0,), (0,)), ((), ())), preferred_element_type=jnp.float32)
            moved = jnp.maximum(trace_now[tile_idx].astype(jnp.float32) - grad / den_a[tile_idx][:, None], 0.0)
            updated.append(jnp.where(lives[tile_idx][:, None], moved, 0.0).astype(jnp.bfloat16))
        trace_now = updated
    outs_a = []
    for tile_idx in range(TILES):
        prod = jnp.dot(feet[tile_idx], trace_now[tile_idx], preferred_element_type=jnp.float32)
        ferr = (prod + backs[tile_idx].astype(jnp.float32) - movie_f[tile_idx]).astype(jnp.bfloat16)
        grad_a = lax.dot_general(ferr, trace_now[tile_idx], (((1,), (1,)), ((), ())), preferred_element_type=jnp.float32)
        den_c = jnp.sum(jnp.square(trace_now[tile_idx].astype(jnp.float32)), axis=1) + RIDGE_TERM
        moved = jnp.maximum(feet[tile_idx].astype(jnp.float32) - grad_a / den_c[None, :], 0.0)
        outs_a.append(jnp.where(keeps[tile_idx], moved, 0.0).astype(jnp.bfloat16))
    return jnp.stack(outs_a), jnp.stack(trace_now)
```

```python
import functools

import jax
import jax.numpy as jnp
import numpy as np
from jax import lax
from jax.experimental import pallas as pl
from jax.experimental.pallas import tpu as pltpu
from jax.sharding import PartitionSpec as P

SIDE = 48
CYCLE = 8
PASSES = 2
RIDGE = 1.0
MAX_RADIUS = 9
BAND = 8
LANES = 128

FOLD_R = 16
FOLD_C = 19
FOLD_SHIFT = 9
SLOTS = FOLD_R * FOLD_C

f32 = jnp.float32
bf16 = jnp.bfloat16
i32 = jnp.int32


def cycle_offsets():
    found = []
    for dy in range(-CYCLE, CYCLE + 1):
        for dx in range(-CYCLE, CYCLE + 1):
            if CYCLE * CYCLE <= dy * dy + dx * dx < (CYCLE + 1) * (CYCLE + 1):
                found.append((dy, dx))
    return found


def band_tables():
    offsets = cycle_offsets()
    none = len(offsets)
    own = np.full((BAND, SIDE, BAND + 2 * CYCLE, SIDE), none, np.int32)
    for o, (dy, dx) in enumerate(offsets):
        for i in range(BAND):
            for c in range(max(0, -dx), min(SIDE, SIDE - dx)):
                own[i, c, i + CYCLE + dy, c + dx] = o
    own = own.reshape(BAND * SIDE, (BAND + 2 * CYCLE) * SIDE)
    beside = np.full((2, BAND, CYCLE, 32, CYCLE), none, np.int32)
    for o, (dy, dx) in enumerate(offsets):
        for i in range(BAND):
            for q in range(CYCLE):
                h = q + dx - CYCLE
                if 0 <= h < CYCLE:
                    beside[0, i, q, i + CYCLE + dy, h] = o
                h = q + dx + CYCLE
                if 0 <= h < CYCLE:
                    beside[1, i, q, i + CYCLE + dy, h] = o
    return own, beside.reshape(2, BAND * CYCLE, 32 * CYCLE)


def fold_rows(parts):
    share = -(-SLOTS // parts)
    block = -(-(share + 2) // 8) * 8
    row, col = np.arange(SIDE * SIDE) // SIDE, np.arange(SIDE * SIDE) % SIDE
    slot = (row % FOLD_R) * FOLD_C + (col + FOLD_SHIFT * (row // FOLD_R)) % FOLD_C
    return (slot // share * block + slot % share).astype(np.int32), share, block


def params(mib=24):
    return pltpu.CompilerParams(vmem_limit_bytes=mib * 2**20)


VM = pl.BlockSpec(memory_space=pltpu.VMEM)
SM = pl.BlockSpec(memory_space=pltpu.SMEM)


def dot(a, b):
    return jnp.dot(a, b, preferred_element_type=f32)


def disc_limit(centre_row, radius, count, row):
    gap = row - centre_row
    live = lax.broadcasted_iota(i32, centre_row.shape, 1) < count
    return jnp.where(live, radius * radius - gap * gap, -1)


def col_gap_sq(centre_col):
    gap = lax.broadcasted_iota(i32, (SIDE, centre_col.shape[1]), 0) - centre_col
    return gap * gap


def resid_band(g, tile, movie_ref, foot, trace, d_ref, r_ref, pay_ref):
    band = BAND * SIDE
    rows = pl.ds(g * band, band)
    d = movie_ref[rows, :].astype(f32) - dot(foot, trace)
    d_ref[rows, :] = d
    r_ref[rows, :] = d.astype(bf16)
    d3 = d.reshape(BAND, SIDE, d.shape[1])
    edge = jnp.where(tile == 0, d3[:, SIDE - CYCLE :], d3[:, :CYCLE])
    pay_ref[pl.ds(g * BAND * CYCLE, BAND * CYCLE), :] = edge.reshape(BAND * CYCLE, d.shape[1]).astype(bf16)


def start_kernel(tile_ref, count_ref, movie_ref, fp_ref, tr_ref, cr_ref, cc_ref, rad_ref,
                 foot_ref, trace_ref, den_ref, d_ref, r_ref, pay_ref):
    count, tile = count_ref[0], tile_ref[0]
    comps = tr_ref.shape[0]
    live = lax.broadcasted_iota(i32, (comps, 1), 0) < count
    trace = jnp.where(live, tr_ref[...].astype(f32), 0.0).astype(bf16)
    trace_ref[...] = trace
    gap_sq = col_gap_sq(cc_ref[...])
    cr, rad = cr_ref[...], rad_ref[...]
    total = jnp.zeros((8, comps), f32)
    for g in range(SIDE // BAND):
        for i in range(BAND):
            row = g * BAND + i
            keep = gap_sq <= disc_limit(cr, rad, count, row)
            foot = jnp.where(keep, fp_ref[pl.ds(row * SIDE, SIDE), :].astype(f32), 0.0)
            foot_ref[pl.ds(row * SIDE, SIDE), :] = foot.astype(bf16)
            total = total + jnp.sum((foot * foot).reshape(SIDE // 8, 8, comps), axis=0)
        resid_band(g, tile, movie_ref, foot_ref[pl.ds(g * BAND * SIDE, BAND * SIDE), :], trace,
                   d_ref, r_ref, pay_ref)
    energy = jnp.sum(total, axis=0, keepdims=True) + RIDGE
    den_ref[...] = jnp.transpose(jnp.broadcast_to(energy, (LANES, comps)))


def banded(bands_ref, r_ref, x_ref):
    band = BAND * SIDE
    for g in range(SIDE // BAND):
        low = max(0, CYCLE - g * BAND)
        high = min(BAND + 2 * CYCLE, SIDE + CYCLE - g * BAND)
        first = (g * BAND + low - CYCLE) * SIDE
        x_ref[pl.ds(g * band, band), :] = dot(
            bands_ref[g, :, low * SIDE : high * SIDE], r_ref[pl.ds(first, (high - low) * SIDE), :])


def build_kernel(tile_ref, w_ref, own_ref, beside_ref, foot_ref, r_ref,
                 bands_ref, sides_ref, footT_ref, x_ref, wide):
    tile = tile_ref[0]
    wide[...] = jnp.zeros_like(wide)
    wide[:, : w_ref.shape[1]] = w_ref[...].astype(f32)
    reach = own_ref.shape[1]
    pick = beside_ref[tile]

    def one(g, carry):
        base = pl.multiple_of(g * (BAND * SIDE), BAND * SIDE)
        edges = []
        for i in range(BAND):
            w = wide[pl.ds(base + i * SIDE, SIDE), :]
            edges.append(jnp.where(tile == 0, w[SIDE - CYCLE :], w[:CYCLE]))
            for v in range(reach // LANES):
                lanes = slice(v * LANES, (v + 1) * LANES)
                if lanes.stop <= i * SIDE or lanes.start >= (i + 2 * CYCLE + 1) * SIDE:
                    block = jnp.zeros((SIDE, LANES), bf16)
                else:
                    index = own_ref[i * SIDE : (i + 1) * SIDE, lanes]
                    block = jnp.take_along_axis(w, index, axis=1).astype(bf16)
                bands_ref[g, i * SIDE : (i + 1) * SIDE, lanes] = block
        edge = jnp.concatenate(edges, axis=0)
        for v in range(2):
            lanes = slice(v * LANES, (v + 1) * LANES)
            sides_ref[g, :, lanes] = jnp.take_along_axis(edge, pick[:, lanes], axis=1).astype(bf16)
        return carry

    lax.fori_loop(0, SIDE // BAND, one, 0)
    footT_ref[...] = jnp.transpose(foot_ref[...])
    banded(bands_ref, r_ref, x_ref)


def banded_kernel(bands_ref, r_ref, x_ref):
    banded(bands_ref, r_ref, x_ref)


def trace_step(tile, count, halo_ref, sides_ref, x_ref, d_ref, footT_ref, trace_ref, den_ref,
               wide_halo, err, back_ref=None):
    frames = x_ref.shape[1]
    band, edge = BAND * SIDE, CYCLE * SIDE
    pad = CYCLE * CYCLE
    wide_halo[:pad, :] = jnp.zeros((pad, frames), bf16)
    wide_halo[pl.ds(pad, edge), :] = halo_ref[...]
    tail = wide_halo.shape[0] - pad - edge
    wide_halo[pl.ds(pad + edge, tail), :] = jnp.zeros((tail, frames), bf16)
    for g in range(SIDE // BAND):
        rows = pl.ds(g * band, band)
        reach = sides_ref.shape[2]
        side = dot(sides_ref[g], wide_halo[pl.ds(g * BAND * CYCLE, reach), :]).reshape(BAND, CYCLE, frames)
        left = jnp.where(tile == 0, 0.0, side)
        right = jnp.where(tile == 0, side, 0.0)
        x = x_ref[rows, :].reshape(BAND, SIDE, frames)
        x = jnp.concatenate(
            [x[:, :CYCLE] + left, x[:, CYCLE : SIDE - CYCLE], x[:, SIDE - CYCLE :] + right], axis=1)
        back = x.reshape(band, frames).astype(bf16)
        if back_ref is not None:
            back_ref[rows, :] = back
        err[rows, :] = (back.astype(f32) - d_ref[rows, :]).astype(bf16)
    grad = dot(footT_ref[...], err[...])
    comps = grad.shape[0]
    live = lax.broadcasted_iota(i32, (comps, 1), 0) < count
    moved = jnp.maximum(trace_ref[...].astype(f32) - grad / den_ref[:, :1], 0.0)
    return jnp.where(live, moved, 0.0)


def pass_kernel(tile_ref, count_ref, halo_ref, sides_ref, x_ref, d_ref, footT_ref, foot_ref, trace_ref, den_ref,
                movie_ref, new_trace_ref, new_d_ref, new_r_ref, pay_ref, wide_halo, err):
    tile, count = tile_ref[0], count_ref[0]
    trace = trace_step(tile, count, halo_ref, sides_ref, x_ref, d_ref, footT_ref, trace_ref, den_ref,
                       wide_halo, err).astype(bf16)
    new_trace_ref[...] = trace
    for g in range(SIDE // BAND):
        resid_band(g, tile, movie_ref, foot_ref[pl.ds(g * BAND * SIDE, BAND * SIDE), :], trace,
                   new_d_ref, new_r_ref, pay_ref)


def last_kernel(block, share, tile_ref, count_ref, halo_ref, sides_ref, x_ref, d_ref, footT_ref, foot_ref, trace_ref,
                den_ref, movie_ref, cr_ref, cc_ref, rad_ref, slot_ref,
                new_trace_ref, part_ref, ffold_ref, wide_halo, err, back, masked):
    tile, count = tile_ref[0], count_ref[0]
    trace = trace_step(tile, count, halo_ref, sides_ref, x_ref, d_ref, footT_ref, trace_ref, den_ref,
                       wide_halo, err, back).astype(bf16)
    new_trace_ref[...] = trace
    comps = trace.shape[0]
    tf = trace.astype(f32)
    energy = jnp.sum(tf * tf, axis=1, keepdims=True)
    energy = jnp.transpose(jnp.broadcast_to(energy, (comps, LANES)))[:1]
    high = energy.astype(bf16).astype(f32)
    low = energy - high
    gap_sq = col_gap_sq(cc_ref[...])
    cr, rad = cr_ref[...], rad_ref[...]
    band = BAND * SIDE
    for g in range(SIDE // BAND):
        rows = pl.ds(g * band, band)
        prod = dot(foot_ref[rows, :], trace)
        ferr = (prod + back[rows, :].astype(f32) - movie_ref[rows, :].astype(f32)).astype(bf16)
        grad = lax.dot_general(ferr, trace, (((1,), (1,)), ((), ())), preferred_element_type=f32)
        for i in range(BAND):
            row = g * BAND + i
            keep = gap_sq <= disc_limit(cr, rad, count, row)
            masked[pl.ds(row * SIDE, SIDE), :] = jnp.where(keep, grad[i * SIDE : (i + 1) * SIDE], 0.0).astype(bf16)
    packed = part_ref.shape[0]
    at = lax.broadcasted_iota(i32, (packed, slot_ref.shape[1]), 0)
    fold = jnp.where(at == slot_ref[...], 1.0, 0.0).astype(bf16)
    inner = lax.rem(lax.broadcasted_iota(i32, (packed, comps), 0), block)
    part = dot(fold, masked[...])
    part = jnp.where(inner == share, high, jnp.where(inner == share + 1, low, part))
    part_ref[...] = part.astype(bf16)
    ffold_ref[...] = dot(fold, foot_ref[...])


def share_kernel(share, me_ref, parts_ref, ffold_ref, out_ref):
    parts, block, comps = parts_ref.shape
    total = jnp.zeros((block, comps), f32)
    for j in range(parts):
        total = total + parts_ref[j].astype(f32)
    den = total[share : share + 1] + total[share + 1 : share + 2] + RIDGE
    foot = ffold_ref[pl.ds(pl.multiple_of(me_ref[0] * block, 8), block), :]
    moved = jnp.maximum(foot - total / den, 0.0).astype(bf16)
    for j in range(parts):
        out_ref[j] = moved


def unfold_kernel(count_ref, all_ref, slot_ref, cr_ref, cc_ref, rad_ref, out_ref):
    count = count_ref[0]
    rows_in = all_ref.shape[0]
    gap_sq = col_gap_sq(cc_ref[...])
    cr, rad = cr_ref[...], rad_ref[...]
    band = BAND * SIDE
    every = all_ref[...]
    for g in range(SIDE // BAND):
        at = lax.broadcasted_iota(i32, (band, rows_in), 1)
        unfold = jnp.where(at == slot_ref[pl.ds(g * band, band), :1], 1.0, 0.0).astype(bf16)
        wide = dot(unfold, every)
        for i in range(BAND):
            row = g * BAND + i
            keep = gap_sq <= disc_limit(cr, rad, count, row)
            out_ref[pl.ds(row * SIDE, SIDE), :] = jnp.where(keep, wide[i * SIDE : (i + 1) * SIDE], 0.0).astype(bf16)


def swap(x):
    count = lax.axis_size("tile")
    return lax.ppermute(x, "tile", [(i, count - 1 - i) for i in range(count)])


def shards(movie, cycle_weights, footprints, traces, centre_row, centre_col, radius, comp_count):
    assert lax.axis_size("tile") == 2
    parts = lax.axis_size("tm")
    movie, weights, fp, tr = movie[0], cycle_weights[0], footprints[0], traces[0]
    pixels, frames = movie.shape
    comps = tr.shape[0]
    band = BAND * SIDE
    bands = SIDE // BAND
    edge = SIDE * CYCLE
    tile = lax.axis_index("tile").astype(i32).reshape(1)
    me = lax.axis_index("tm").astype(i32).reshape(1)
    own, beside = band_tables()
    slots, share, block = fold_rows(parts)
    packed = parts * block
    sds = jax.ShapeDtypeStruct
    halo_pad = pltpu.VMEM((edge + 3 * CYCLE * CYCLE, frames), bf16)
    err_buf = pltpu.VMEM((pixels, frames), bf16)

    foot, trace, den, d, r, pay = pl.pallas_call(
        start_kernel,
        out_shape=(sds((pixels, comps), bf16), sds((comps, frames), bf16), sds((comps, LANES), f32),
                   sds((pixels, frames), f32), sds((pixels, frames), bf16), sds((edge, frames), bf16)),
        in_specs=[SM, SM] + [VM] * 6, out_specs=[VM] * 6, compiler_params=params(),
    )(tile, comp_count, movie, fp, tr, centre_row, centre_col, radius)
    halo = swap(pay)
    band_w, side_w, footT, x = pl.pallas_call(
        build_kernel,
        out_shape=(sds((bands, band, own.shape[1]), bf16), sds((bands, CYCLE * BAND, beside.shape[2]), bf16),
                   sds((comps, pixels), bf16), sds((pixels, frames), f32)),
        in_specs=[SM] + [VM] * 5, out_specs=[VM] * 4,
        scratch_shapes=[pltpu.VMEM((pixels, LANES), f32)], compiler_params=params(),
        cost_estimate=pl.CostEstimate(flops=4_000_000_000, bytes_accessed=20_000_000, transcendentals=0),
    )(tile, weights, jnp.asarray(own), jnp.asarray(beside), foot, r)
    trace, d, r, pay = pl.pallas_call(
        pass_kernel,
        out_shape=(sds((comps, frames), bf16), sds((pixels, frames), f32), sds((pixels, frames), bf16),
                   sds((edge, frames), bf16)),
        in_specs=[SM, SM] + [VM] * 9, out_specs=[VM] * 4,
        scratch_shapes=[halo_pad, err_buf], compiler_params=params(),
    )(tile, comp_count, halo, side_w, x, d, footT, foot, trace, den, movie)
    halo = swap(pay)
    x = pl.pallas_call(
        banded_kernel,
        out_shape=sds((pixels, frames), f32),
        in_specs=[VM, VM], out_specs=VM, compiler_params=params(),
        cost_estimate=pl.CostEstimate(flops=4_000_000_000, bytes_accessed=20_000_000, transcendentals=0),
    )(band_w, r)
    slot_lane = jnp.asarray(slots.reshape(1, pixels))
    slot_col = jnp.asarray(slots.reshape(pixels, 1))
    trace, part, ffold = pl.pallas_call(
        functools.partial(last_kernel, block, share),
        out_shape=(sds((comps, frames), bf16), sds((packed, comps), bf16), sds((packed, comps), f32)),
        in_specs=[SM, SM] + [VM] * 13, out_specs=[VM] * 3,
        scratch_shapes=[halo_pad, err_buf, pltpu.VMEM((pixels, frames), bf16), pltpu.VMEM((pixels, comps), bf16)],
        compiler_params=params(32),
    )(tile, comp_count, halo, side_w, x, d, footT, foot, trace, den, movie, centre_row, centre_col, radius, slot_lane)
    received = lax.all_to_all(part.reshape(parts, block, comps), "tm", 0, 0, tiled=False)
    moved = pl.pallas_call(
        functools.partial(share_kernel, share),
        out_shape=sds((parts, block, comps), bf16),
        in_specs=[SM, VM, VM], out_specs=VM, compiler_params=params(),
    )(me, received, ffold)
    every = lax.all_to_all(moved, "tm", 0, 0, tiled=False).reshape(packed, comps)
    new_foot = pl.pallas_call(
        unfold_kernel,
        out_shape=sds((pixels, comps), bf16),
        in_specs=[SM] + [VM] * 5, out_specs=VM, compiler_params=params(),
    )(comp_count, every, slot_col, centre_row, centre_col, radius)
    return (new_foot[None], trace[None])


def solution(mesh):
    in_specs = (
        P(("groups", "tile"), None, "tm"),
        P(("groups", "tile"), None, None),
        P(("groups", "tile"), None, None),
        P(("groups", "tile"), None, "tm"),
        P(("groups", "tile"), None),
        P(("groups", "tile"), None),
        P(("groups", "tile"), None),
        P(("groups", "tile")),
    )
    out_specs = (P(("groups", "tile"), None, None), P(("groups", "tile"), None, "tm"))
    return jax.shard_map(shards, mesh=mesh, in_specs=in_specs, out_specs=out_specs, check_vma=False)
```

```python
import functools

import jax
import jax.numpy as jnp
import numpy as np
from jax import lax
from jax.experimental import pallas as pl
from jax.experimental.pallas import tpu as pltpu
from jax.sharding import PartitionSpec as P

SIDE = 48
CYCLE = 8
PASSES = 2
RIDGE = 1.0
MAX_RADIUS = 9
BAND = 8
LANES = 128
OFFS_PAD = 64

FOLD_R = 16
FOLD_C = 19
FOLD_SHIFT = 9
SLOTS = FOLD_R * FOLD_C

f32 = jnp.float32
bf16 = jnp.bfloat16
i32 = jnp.int32


def cycle_offsets():
    found = []
    for dy in range(-CYCLE, CYCLE + 1):
        for dx in range(-CYCLE, CYCLE + 1):
            if CYCLE * CYCLE <= dy * dy + dx * dx < (CYCLE + 1) * (CYCLE + 1):
                found.append((dy, dx))
    return found


def band_tables():
    offsets = cycle_offsets()
    none = len(offsets)
    reach = (BAND + 2 * CYCLE) * SIDE
    own = np.full((OFFS_PAD, 1), -1, np.int32)
    beside = np.full((2, BAND, CYCLE, 32, CYCLE), none, np.int32)
    for o, (dy, dx) in enumerate(offsets):
        own[o, 0] = ((CYCLE + dy) * SIDE + dx) % reach
        for i in range(BAND):
            for q in range(CYCLE):
                h = q + dx - CYCLE
                if 0 <= h < CYCLE:
                    beside[0, i, q, i + CYCLE + dy, h] = o
                h = q + dx + CYCLE
                if 0 <= h < CYCLE:
                    beside[1, i, q, i + CYCLE + dy, h] = o
    return own, beside.reshape(2, BAND * CYCLE, 32 * CYCLE)


def fold_rows(parts):
    share = -(-SLOTS // parts)
    block = -(-(share + 2) // 8) * 8
    assert SLOTS // 2 % share == 0 and FOLD_R == 2 * BAND
    low = np.arange(SIDE // FOLD_R)[:, None, None]
    row, col = np.arange(BAND)[:, None], np.arange(SIDE)
    slot = row * FOLD_C + (col + FOLD_SHIFT * low) % FOLD_C
    return (slot // share * block + slot % share).astype(np.int32).reshape(1, -1), share, block


def params(mib=12):
    return pltpu.CompilerParams(vmem_limit_bytes=mib * 2**20)


VM = pl.BlockSpec(memory_space=pltpu.VMEM)
HB = pl.BlockSpec(memory_space=pltpu.HBM)
SM = pl.BlockSpec(memory_space=pltpu.SMEM)


def dot(a, b):
    return jnp.dot(a, b, preferred_element_type=f32)


def disc_limit(centre_row, radius, count, row):
    gap = row - centre_row
    live = lax.broadcasted_iota(i32, centre_row.shape, 1) < count
    return jnp.where(live, radius * radius - gap * gap, -1)


def col_gap_sq(centre_col):
    gap = lax.broadcasted_iota(i32, (SIDE, centre_col.shape[1]), 0) - centre_col
    return gap * gap


def resid_band(g, tile, movie_ref, foot, trace, d_ref, r_ref, pay_ref):
    band = BAND * SIDE
    rows = pl.ds(g * band, band)
    d = movie_ref[rows, :].astype(f32) - dot(foot, trace)
    d_ref[rows, :] = d
    r_ref[rows, :] = d.astype(bf16)
    d3 = d.reshape(BAND, SIDE, d.shape[1])
    edge = jnp.where(tile == 0, d3[:, SIDE - CYCLE :], d3[:, :CYCLE])
    pay_ref[pl.ds(g * BAND * CYCLE, BAND * CYCLE), :] = edge.reshape(BAND * CYCLE, d.shape[1]).astype(bf16)


def start_kernel(tile_ref, count_ref, movie_hbm, fp_hbm, tr_hbm, cr_hbm, cc_hbm, rad_hbm,
                 foot_ref, trace_ref, den_ref, d_ref, r_ref, pay_ref, movie_ref,
                 fp_ref, tr_ref, cr_ref, cc_ref, rad_ref, sems):
    count, tile = count_ref[0], tile_ref[0]
    comps = tr_ref.shape[0]
    band = BAND * SIDE
    bands = SIDE // BAND
    small = [pltpu.make_async_copy(src, dst, sems.at[2 * bands + n]) for n, (src, dst) in enumerate(
        ((cr_hbm, cr_ref), (cc_hbm, cc_ref), (rad_hbm, rad_ref), (tr_hbm, tr_ref)))]
    fps, movies = [], []
    for g in range(bands):
        rows = pl.ds(g * band, band)
        fps.append(pltpu.make_async_copy(fp_hbm.at[rows, :], fp_ref.at[rows, :], sems.at[g]))
        movies.append(pltpu.make_async_copy(movie_hbm.at[rows, :], movie_ref.at[rows, :], sems.at[bands + g]))
    for n, copy in enumerate(small):
        copy.start()
    for g in range(bands):
        fps[g].start()
        movies[g].start()
    for copy in small:
        copy.wait()
    live = lax.broadcasted_iota(i32, (comps, 1), 0) < count
    trace = jnp.where(live, tr_ref[...].astype(f32), 0.0).astype(bf16)
    trace_ref[...] = trace
    gap_sq = col_gap_sq(cc_ref[...])
    cr, rad = cr_ref[...], rad_ref[...]
    total = jnp.zeros((8, comps), f32)
    for g in range(bands):
        fps[g].wait()
        for i in range(BAND):
            row = g * BAND + i
            keep = gap_sq <= disc_limit(cr, rad, count, row)
            foot = jnp.where(keep, fp_ref[pl.ds(row * SIDE, SIDE), :].astype(f32), 0.0)
            foot_ref[pl.ds(row * SIDE, SIDE), :] = foot.astype(bf16)
            total = total + jnp.sum((foot * foot).reshape(SIDE // 8, 8, comps), axis=0)
        movies[g].wait()
        resid_band(g, tile, movie_ref, foot_ref[pl.ds(g * band, band), :], trace, d_ref, r_ref, pay_ref)
    energy = jnp.sum(total, axis=0, keepdims=True) + RIDGE
    den_ref[...] = jnp.transpose(jnp.broadcast_to(energy, (LANES, comps)))


def banded(bands_ref, r_ref, x_ref):
    band = BAND * SIDE
    for g in range(SIDE // BAND):
        low = max(0, CYCLE - g * BAND)
        high = min(BAND + 2 * CYCLE, SIDE + CYCLE - g * BAND)
        first = (g * BAND + low - CYCLE) * SIDE
        x_ref[pl.ds(g * band, band), :] = dot(
            bands_ref[g, :, low * SIDE : high * SIDE], r_ref[pl.ds(first, (high - low) * SIDE), :])


def build_kernel(tile_ref, w_ref, own_ref, beside_ref, r_ref, bands_ref, sides_ref, x_ref, weights, wide):
    tile = tile_ref[0]
    bands = SIDE // BAND
    reach = bands_ref.shape[2]
    blocks = reach // LANES
    offs = w_ref.shape[0]
    eye = lax.broadcasted_iota(i32, (offs, LANES), 0) == lax.broadcasted_iota(i32, (offs, LANES), 1)
    weights[...] = lax.dot_general(w_ref[...], jnp.where(eye, 1.0, 0.0).astype(bf16), (((0,), (0,)), ((), ())),
                                   preferred_element_type=f32)
    pixel = lax.broadcasted_iota(i32, (SIDE, LANES), 0)
    lane = lax.broadcasted_iota(i32, (SIDE, LANES), 1)
    carried = lane < pixel
    period = 3
    inside = [jnp.abs(lax.rem(lane + v * LANES, SIDE) - pixel) <= CYCLE for v in range(period)]
    at = own_ref[...]
    target = lax.broadcasted_iota(i32, (OFFS_PAD, reach), 1)
    for i in range(BAND):
        moved = at + i * SIDE
        moved = jnp.where(moved >= reach, moved - reach, moved)
        pick = jnp.where(target == jnp.where(at < 0, -1, moved), 1.0, 0.0).astype(bf16)
        w = jnp.concatenate(
            [weights[(g * BAND + i) * SIDE : (g * BAND + i + 1) * SIDE, :OFFS_PAD] for g in range(bands)], axis=0)
        wide[...] = dot(w.astype(bf16), pick)
        for g in range(bands):
            turned = [pltpu.roll(wide[g * SIDE : (g + 1) * SIDE, v * LANES : (v + 1) * LANES], 0, 1,
                                 stride=1, stride_axis=0) for v in range(blocks)]
            for v in range(blocks):
                block = jnp.where(carried, turned[v - 1], turned[v])
                bands_ref[g, i * SIDE : (i + 1) * SIDE, v * LANES : (v + 1) * LANES] = jnp.where(
                    inside[v % period], block, 0.0).astype(bf16)
    beside = beside_ref[tile]
    for g in range(bands):
        edges = []
        for i in range(BAND):
            base = (g * BAND + i) * SIDE
            edges.append(jnp.where(tile == 0, weights[base + SIDE - CYCLE : base + SIDE, :],
                                   weights[base : base + CYCLE, :]))
        edge = jnp.concatenate(edges, axis=0)
        for v in range(2):
            lanes = slice(v * LANES, (v + 1) * LANES)
            sides_ref[g, :, lanes] = jnp.take_along_axis(edge, beside[:, lanes], axis=1).astype(bf16)
    banded(bands_ref, r_ref, x_ref)


def banded_kernel(bands_ref, r_ref, x_ref):
    banded(bands_ref, r_ref, x_ref)


def trace_step(tile, count, halo_ref, sides_ref, x_ref, d_ref, foot_ref, trace_ref, den_ref,
               wide_halo, err, back_ref=None):
    frames = x_ref.shape[1]
    band, edge = BAND * SIDE, CYCLE * SIDE
    pad = CYCLE * CYCLE
    wide_halo[:pad, :] = jnp.zeros((pad, frames), bf16)
    wide_halo[pl.ds(pad, edge), :] = halo_ref[...]
    tail = wide_halo.shape[0] - pad - edge
    wide_halo[pl.ds(pad + edge, tail), :] = jnp.zeros((tail, frames), bf16)
    for g in range(SIDE // BAND):
        rows = pl.ds(g * band, band)
        reach = sides_ref.shape[2]
        side = dot(sides_ref[g], wide_halo[pl.ds(g * BAND * CYCLE, reach), :]).reshape(BAND, CYCLE, frames)
        left = jnp.where(tile == 0, 0.0, side)
        right = jnp.where(tile == 0, side, 0.0)
        x = x_ref[rows, :].reshape(BAND, SIDE, frames)
        x = jnp.concatenate(
            [x[:, :CYCLE] + left, x[:, CYCLE : SIDE - CYCLE], x[:, SIDE - CYCLE :] + right], axis=1)
        back = x.reshape(band, frames).astype(bf16)
        if back_ref is not None:
            back_ref[rows, :] = back
        err[rows, :] = (back.astype(f32) - d_ref[rows, :]).astype(bf16)
    grad = lax.dot_general(foot_ref[...], err[...], (((0,), (0,)), ((), ())), preferred_element_type=f32)
    comps = grad.shape[0]
    live = lax.broadcasted_iota(i32, (comps, 1), 0) < count
    moved = jnp.maximum(trace_ref[...].astype(f32) - grad / den_ref[:, :1], 0.0)
    return jnp.where(live, moved, 0.0)


def pass_kernel(tile_ref, count_ref, halo_ref, sides_ref, x_ref, d_ref, foot_ref, trace_ref, den_ref,
                movie_ref, new_trace_ref, new_d_ref, new_r_ref, pay_ref, wide_halo, err):
    tile, count = tile_ref[0], count_ref[0]
    trace = trace_step(tile, count, halo_ref, sides_ref, x_ref, d_ref, foot_ref, trace_ref, den_ref,
                       wide_halo, err).astype(bf16)
    new_trace_ref[...] = trace
    for g in range(SIDE // BAND):
        resid_band(g, tile, movie_ref, foot_ref[pl.ds(g * BAND * SIDE, BAND * SIDE), :], trace,
                   new_d_ref, new_r_ref, pay_ref)


def last_kernel(block, share, tile_ref, count_ref, halo_ref, sides_ref, x_ref, d_ref, foot_ref, trace_ref,
                den_ref, movie_ref, cr_ref, cc_ref, rad_ref, slot_ref,
                trace_hbm, part_ref, fold_ref, wide_halo, err, back, masked, new_trace, sem):
    tile, count = tile_ref[0], count_ref[0]
    trace = trace_step(tile, count, halo_ref, sides_ref, x_ref, d_ref, foot_ref, trace_ref, den_ref,
                       wide_halo, err, back).astype(bf16)
    new_trace[...] = trace
    store = pltpu.make_async_copy(new_trace, trace_hbm, sem)
    store.start()
    comps = trace.shape[0]
    tf = trace.astype(f32)
    energy = jnp.sum(tf * tf, axis=1, keepdims=True)
    energy = jnp.transpose(jnp.broadcast_to(energy, (comps, LANES)))[:1]
    high = energy.astype(bf16).astype(f32)
    low = energy - high
    gap_sq = col_gap_sq(cc_ref[...])
    cr, rad = cr_ref[...], rad_ref[...]
    band = BAND * SIDE
    for g in range(SIDE // BAND):
        rows = pl.ds(g * band, band)
        prod = dot(foot_ref[rows, :], trace)
        ferr = (prod + back[rows, :].astype(f32) - movie_ref[rows, :].astype(f32)).astype(bf16)
        grad = lax.dot_general(ferr, trace, (((1,), (1,)), ((), ())), preferred_element_type=f32)
        for i in range(BAND):
            row = g * BAND + i
            keep = gap_sq <= disc_limit(cr, rad, count, row)
            masked[g % 2, pl.ds(g // 2 * band + i * SIDE, SIDE), :] = jnp.where(
                keep, grad[i * SIDE : (i + 1) * SIDE], 0.0).astype(bf16)
    half, taken = fold_ref.shape
    at = lax.broadcasted_iota(i32, (half, taken), 0)
    fold = jnp.where(at == slot_ref[...], 1.0, 0.0).astype(bf16)
    fold_ref[...] = fold
    inner = lax.rem(lax.broadcasted_iota(i32, (half, comps), 0), block)
    for h in range(2):
        part = dot(fold, masked[h])
        part = jnp.where(inner == share, high, jnp.where(inner == share + 1, low, part))
        part_ref[h * half : (h + 1) * half, :] = part.astype(bf16)
    store.wait()


def foot_fold_kernel(fold_ref, foot_ref, out_ref):
    half = fold_ref.shape[0]
    band = BAND * SIDE
    for h in range(2):
        foot = jnp.concatenate(
            [foot_ref[g * band : (g + 1) * band, :] for g in range(h, SIDE // BAND, 2)], axis=0)
        out_ref[h * half : (h + 1) * half, :] = dot(fold_ref[...], foot)


def share_kernel(share, me_ref, parts_ref, ffold_ref, out_ref):
    parts, block, comps = parts_ref.shape
    total = jnp.zeros((block, comps), f32)
    for j in range(parts):
        total = total + parts_ref[j].astype(f32)
    den = total[share : share + 1] + total[share + 1 : share + 2] + RIDGE
    foot = ffold_ref[pl.ds(pl.multiple_of(me_ref[0] * block, 8), block), :]
    moved = jnp.maximum(foot - total / den, 0.0).astype(bf16)
    for j in range(parts):
        out_ref[j] = moved


def unfold_kernel(count_ref, all_ref, fold_ref, cr_ref, cc_ref, rad_ref, out_hbm, buf, sems):
    count = count_ref[0]
    half = fold_ref.shape[0]
    gap_sq = col_gap_sq(cc_ref[...])
    cr, rad = cr_ref[...], rad_ref[...]
    band = BAND * SIDE
    stores = []
    for g in range(SIDE // BAND):
        h, b = g % 2, g // 2
        wide = lax.dot_general(fold_ref[:, b * band : (b + 1) * band], all_ref[h * half : (h + 1) * half, :],
                               (((0,), (0,)), ((), ())), preferred_element_type=f32)
        for i in range(BAND):
            row = g * BAND + i
            keep = gap_sq <= disc_limit(cr, rad, count, row)
            buf[pl.ds(row * SIDE, SIDE), :] = jnp.where(keep, wide[i * SIDE : (i + 1) * SIDE], 0.0).astype(bf16)
        rows = pl.ds(g * band, band)
        stores.append(pltpu.make_async_copy(buf.at[rows, :], out_hbm.at[rows, :], sems.at[g]))
        stores[-1].start()
    for store in stores:
        store.wait()


def swap(x):
    count = lax.axis_size("tile")
    return lax.ppermute(x, "tile", [(i, count - 1 - i) for i in range(count)])


def shards(movie, cycle_weights, footprints, traces, centre_row, centre_col, radius, comp_count):
    assert lax.axis_size("tile") == 2
    parts = lax.axis_size("tm")
    movie, fp, tr = movie[0], footprints[0], traces[0]
    weights = jnp.swapaxes(cycle_weights[0], 0, 1)
    pixels, frames = movie.shape
    comps = tr.shape[0]
    band = BAND * SIDE
    bands = SIDE // BAND
    edge = SIDE * CYCLE
    reach = (BAND + 2 * CYCLE) * SIDE
    tile = lax.axis_index("tile").astype(i32).reshape(1)
    me = lax.axis_index("tm").astype(i32).reshape(1)
    own, beside = band_tables()
    slots, share, block = fold_rows(parts)
    packed = parts * block
    sds = jax.ShapeDtypeStruct
    halo_pad = pltpu.VMEM((edge + 3 * CYCLE * CYCLE, frames), bf16)
    err_buf = pltpu.VMEM((pixels, frames), bf16)
    one_row = pltpu.VMEM((1, comps), i32)

    foot, trace, den, d, r, pay, movie = pl.pallas_call(
        start_kernel,
        out_shape=(sds((pixels, comps), bf16), sds((comps, frames), bf16), sds((comps, LANES), f32),
                   sds((pixels, frames), f32), sds((pixels, frames), bf16), sds((edge, frames), bf16),
                   sds((pixels, frames), bf16)),
        in_specs=[SM, SM] + [HB] * 6, out_specs=[VM] * 7,
        scratch_shapes=[pltpu.VMEM((pixels, comps), bf16), pltpu.VMEM((comps, frames), bf16),
                        one_row, one_row, one_row, pltpu.SemaphoreType.DMA((2 * bands + 4,))],
        compiler_params=params(),
    )(tile, comp_count, movie, fp, tr, centre_row, centre_col, radius)
    halo = swap(pay)
    banded_cost = pl.CostEstimate(flops=4_000_000_000, bytes_accessed=20_000_000, transcendentals=0)
    band_w, side_w, x = pl.pallas_call(
        build_kernel,
        out_shape=(sds((bands, band, reach), bf16), sds((bands, CYCLE * BAND, beside.shape[2]), bf16),
                   sds((pixels, frames), f32)),
        in_specs=[SM] + [VM] * 4, out_specs=[VM] * 3,
        scratch_shapes=[pltpu.VMEM((pixels, LANES), f32), pltpu.VMEM((bands * SIDE, reach), f32)],
        compiler_params=params(), cost_estimate=banded_cost,
    )(tile, weights, jnp.asarray(own), jnp.asarray(beside), r)
    trace, d, r, pay = pl.pallas_call(
        pass_kernel,
        out_shape=(sds((comps, frames), bf16), sds((pixels, frames), f32), sds((pixels, frames), bf16),
                   sds((edge, frames), bf16)),
        in_specs=[SM, SM] + [VM] * 8, out_specs=[VM] * 4,
        scratch_shapes=[halo_pad, err_buf], compiler_params=params(),
    )(tile, comp_count, halo, side_w, x, d, foot, trace, den, movie)
    halo = swap(pay)
    x = pl.pallas_call(
        banded_kernel,
        out_shape=sds((pixels, frames), f32),
        in_specs=[VM, VM], out_specs=VM, compiler_params=params(), cost_estimate=banded_cost,
    )(band_w, r)
    trace, part, fold = pl.pallas_call(
        functools.partial(last_kernel, block, share),
        out_shape=(sds((comps, frames), bf16), sds((packed, comps), bf16), sds((packed // 2, slots.shape[1]), bf16)),
        in_specs=[SM, SM] + [VM] * 12, out_specs=[HB, VM, VM],
        scratch_shapes=[halo_pad, err_buf, pltpu.VMEM((pixels, frames), bf16), pltpu.VMEM((2, pixels // 2, comps), bf16),
                        pltpu.VMEM((comps, frames), bf16), pltpu.SemaphoreType.DMA],
        compiler_params=params(14),
    )(tile, comp_count, halo, side_w, x, d, foot, trace, den, movie, centre_row, centre_col, radius, jnp.asarray(slots))
    received = lax.all_to_all(part.reshape(parts, block, comps), "tm", 0, 0, tiled=False)
    ffold = pl.pallas_call(
        foot_fold_kernel,
        out_shape=sds((packed, comps), f32),
        in_specs=[VM, VM], out_specs=VM, compiler_params=params(),
    )(fold, foot)
    moved = pl.pallas_call(
        functools.partial(share_kernel, share),
        out_shape=sds((parts, block, comps), bf16),
        in_specs=[SM, VM, VM], out_specs=VM, compiler_params=params(),
    )(me, received, ffold)
    every = lax.all_to_all(moved, "tm", 0, 0, tiled=False).reshape(packed, comps)
    new_foot = pl.pallas_call(
        unfold_kernel,
        out_shape=sds((pixels, comps), bf16),
        in_specs=[SM] + [VM] * 5, out_specs=HB,
        scratch_shapes=[pltpu.VMEM((pixels, comps), bf16), pltpu.SemaphoreType.DMA((bands,))],
        compiler_params=params(),
    )(comp_count, every, fold, centre_row, centre_col, radius)
    return (new_foot[None], trace[None])


def solution(mesh):
    in_specs = (
        P(("groups", "tile"), None, "tm"),
        P(("groups", "tile"), None, None),
        P(("groups", "tile"), None, None),
        P(("groups", "tile"), None, "tm"),
        P(("groups", "tile"), None),
        P(("groups", "tile"), None),
        P(("groups", "tile"), None),
        P(("groups", "tile")),
    )
    out_specs = (P(("groups", "tile"), None, None), P(("groups", "tile"), None, "tm"))
    return jax.shard_map(shards, mesh=mesh, in_specs=in_specs, out_specs=out_specs, check_vma=False)
```

```python
import functools

import jax
import jax.numpy as jnp
import numpy as np
from jax import lax
from jax.experimental import pallas as pl
from jax.experimental.pallas import tpu as pltpu
from jax.sharding import PartitionSpec as P

SIDE = 48
CYCLE = 8
PASSES = 2
RIDGE = 1.0
MAX_RADIUS = 9
BAND = 8
LANES = 128
OFFS_PAD = 64

FOLD_R = 16
FOLD_C = 19
FOLD_SHIFT = 9
SLOTS = FOLD_R * FOLD_C

f32 = jnp.float32
bf16 = jnp.bfloat16
i32 = jnp.int32


def cycle_offsets():
    found = []
    for dy in range(-CYCLE, CYCLE + 1):
        for dx in range(-CYCLE, CYCLE + 1):
            if CYCLE * CYCLE <= dy * dy + dx * dx < (CYCLE + 1) * (CYCLE + 1):
                found.append((dy, dx))
    return found


def band_tables():
    offsets = cycle_offsets()
    none = len(offsets)
    reach = (BAND + 2 * CYCLE) * SIDE
    own = np.full((OFFS_PAD, 1), -1, np.int32)
    beside = np.full((2, BAND, CYCLE, 32, CYCLE), none, np.int32)
    for o, (dy, dx) in enumerate(offsets):
        own[o, 0] = ((CYCLE + dy) * SIDE + dx) % reach
        for i in range(BAND):
            for q in range(CYCLE):
                h = q + dx - CYCLE
                if 0 <= h < CYCLE:
                    beside[0, i, q, i + CYCLE + dy, h] = o
                h = q + dx + CYCLE
                if 0 <= h < CYCLE:
                    beside[1, i, q, i + CYCLE + dy, h] = o
    return own, beside.reshape(2, BAND * CYCLE, 32 * CYCLE)


def fold_rows(parts):
    share = -(-SLOTS // parts)
    block = -(-(share + 2) // 8) * 8
    assert SLOTS // 2 % share == 0 and FOLD_R == 2 * BAND
    low = np.arange(SIDE // FOLD_R)[:, None, None]
    row, col = np.arange(BAND)[:, None], np.arange(SIDE)
    slot = row * FOLD_C + (col + FOLD_SHIFT * low) % FOLD_C
    return (slot // share * block + slot % share).astype(np.int32).reshape(1, -1), share, block


def params(mib=12):
    return pltpu.CompilerParams(vmem_limit_bytes=mib * 2**20)


VM = pl.BlockSpec(memory_space=pltpu.VMEM)
HB = pl.BlockSpec(memory_space=pltpu.HBM)
SM = pl.BlockSpec(memory_space=pltpu.SMEM)


def dot(a, b):
    return jnp.dot(a, b, preferred_element_type=f32)


def disc_limit(centre_row, radius, count, row):
    gap = row - centre_row
    live = lax.broadcasted_iota(i32, centre_row.shape, 1) < count
    return jnp.where(live, radius * radius - gap * gap, -1)


def col_gap_sq(centre_col):
    gap = lax.broadcasted_iota(i32, (SIDE, centre_col.shape[1]), 0) - centre_col
    return gap * gap


def resid_band(g, tile, movie_ref, foot, trace, d_ref, r_ref, pay_ref):
    band = BAND * SIDE
    rows = pl.ds(g * band, band)
    d = movie_ref[rows, :].astype(f32) - dot(foot, trace)
    d_ref[rows, :] = d
    r_ref[rows, :] = d.astype(bf16)
    d3 = d.reshape(BAND, SIDE, d.shape[1])
    edge = jnp.where(tile == 0, d3[:, SIDE - CYCLE :], d3[:, :CYCLE])
    pay_ref[pl.ds(g * BAND * CYCLE, BAND * CYCLE), :] = edge.reshape(BAND * CYCLE, d.shape[1]).astype(bf16)


def start_kernel(tile_ref, count_ref, movie_hbm, fp_hbm, tr_hbm, cr_hbm, cc_hbm, rad_hbm,
                 foot_ref, trace_ref, den_ref, d_ref, r_ref, pay_ref, movie_ref,
                 fp_ref, tr_ref, cr_ref, cc_ref, rad_ref, sems):
    count, tile = count_ref[0], tile_ref[0]
    comps = tr_ref.shape[0]
    band = BAND * SIDE
    bands = SIDE // BAND
    small = [pltpu.make_async_copy(src, dst, sems.at[2 * bands + n]) for n, (src, dst) in enumerate(
        ((cr_hbm, cr_ref), (cc_hbm, cc_ref), (rad_hbm, rad_ref), (tr_hbm, tr_ref)))]
    fps, movies = [], []
    for g in range(bands):
        rows = pl.ds(g * band, band)
        fps.append(pltpu.make_async_copy(fp_hbm.at[rows, :], fp_ref.at[rows, :], sems.at[g]))
        movies.append(pltpu.make_async_copy(movie_hbm.at[rows, :], movie_ref.at[rows, :], sems.at[bands + g]))
    for n, copy in enumerate(small):
        copy.start()
    for g in range(bands):
        fps[g].start()
        movies[g].start()
    for copy in small:
        copy.wait()
    live = lax.broadcasted_iota(i32, (comps, 1), 0) < count
    trace = jnp.where(live, tr_ref[...].astype(f32), 0.0).astype(bf16)
    trace_ref[...] = trace
    gap_sq = col_gap_sq(cc_ref[...])
    cr, rad = cr_ref[...], rad_ref[...]
    total = jnp.zeros((8, comps), f32)
    for g in range(bands):
        fps[g].wait()
        for i in range(BAND):
            row = g * BAND + i
            keep = gap_sq <= disc_limit(cr, rad, count, row)
            foot = jnp.where(keep, fp_ref[pl.ds(row * SIDE, SIDE), :].astype(f32), 0.0)
            foot_ref[pl.ds(row * SIDE, SIDE), :] = foot.astype(bf16)
            total = total + jnp.sum((foot * foot).reshape(SIDE // 8, 8, comps), axis=0)
        movies[g].wait()
        resid_band(g, tile, movie_ref, foot_ref[pl.ds(g * band, band), :], trace, d_ref, r_ref, pay_ref)
    energy = jnp.sum(total, axis=0, keepdims=True) + RIDGE
    den_ref[...] = jnp.transpose(jnp.broadcast_to(energy, (LANES, comps)))


def banded(bands_ref, r_ref, x_ref):
    band = BAND * SIDE
    for g in range(SIDE // BAND):
        low = max(0, CYCLE - g * BAND)
        high = min(BAND + 2 * CYCLE, SIDE + CYCLE - g * BAND)
        first = (g * BAND + low - CYCLE) * SIDE
        x_ref[pl.ds(g * band, band), :] = dot(
            bands_ref[g, :, low * SIDE : high * SIDE], r_ref[pl.ds(first, (high - low) * SIDE), :])


def build_kernel(tile_ref, w_ref, own_ref, beside_ref, r_ref, bands_ref, sides_ref, x_ref, weights, wide):
    tile = tile_ref[0]
    bands = SIDE // BAND
    reach = bands_ref.shape[2]
    blocks = reach // LANES
    offs = w_ref.shape[0]
    eye = lax.broadcasted_iota(i32, (offs, LANES), 0) == lax.broadcasted_iota(i32, (offs, LANES), 1)
    weights[...] = lax.dot_general(w_ref[...], jnp.where(eye, 1.0, 0.0).astype(bf16), (((0,), (0,)), ((), ())),
                                   preferred_element_type=f32)
    pixel = lax.broadcasted_iota(i32, (SIDE, LANES), 0)
    lane = lax.broadcasted_iota(i32, (SIDE, LANES), 1)
    carried = lane < pixel
    period = 3
    inside = [jnp.abs(lax.rem(lane + v * LANES, SIDE) - pixel) <= CYCLE for v in range(period)]
    at = own_ref[...]
    target = lax.broadcasted_iota(i32, (OFFS_PAD, reach), 1)
    for i in range(BAND):
        moved = at + i * SIDE
        moved = jnp.where(moved >= reach, moved - reach, moved)
        pick = jnp.where(target == jnp.where(at < 0, -1, moved), 1.0, 0.0).astype(bf16)
        w = jnp.concatenate(
            [weights[(g * BAND + i) * SIDE : (g * BAND + i + 1) * SIDE, :OFFS_PAD] for g in range(bands)], axis=0)
        wide[...] = dot(w.astype(bf16), pick)
        for g in range(bands):
            turned = [pltpu.roll(wide[g * SIDE : (g + 1) * SIDE, v * LANES : (v + 1) * LANES], 0, 1,
                                 stride=1, stride_axis=0) for v in range(blocks)]
            for v in range(blocks):
                block = jnp.where(carried, turned[v - 1], turned[v])
                bands_ref[g, i * SIDE : (i + 1) * SIDE, v * LANES : (v + 1) * LANES] = jnp.where(
                    inside[v % period], block, 0.0).astype(bf16)
    beside = beside_ref[tile]
    for g in range(bands):
        edges = []
        for i in range(BAND):
            base = (g * BAND + i) * SIDE
            edges.append(jnp.where(tile == 0, weights[base + SIDE - CYCLE : base + SIDE, :],
                                   weights[base : base + CYCLE, :]))
        edge = jnp.concatenate(edges, axis=0)
        for v in range(2):
            lanes = slice(v * LANES, (v + 1) * LANES)
            sides_ref[g, :, lanes] = jnp.take_along_axis(edge, beside[:, lanes], axis=1).astype(bf16)
    banded(bands_ref, r_ref, x_ref)


def banded_kernel(bands_ref, r_ref, x_ref):
    banded(bands_ref, r_ref, x_ref)


def trace_step(tile, count, halo_ref, sides_ref, x_ref, d_ref, foot_ref, trace_ref, den_ref,
               wide_halo, err, back_ref=None):
    frames = x_ref.shape[1]
    band, edge = BAND * SIDE, CYCLE * SIDE
    pad = CYCLE * CYCLE
    wide_halo[:pad, :] = jnp.zeros((pad, frames), bf16)
    wide_halo[pl.ds(pad, edge), :] = halo_ref[...]
    tail = wide_halo.shape[0] - pad - edge
    wide_halo[pl.ds(pad + edge, tail), :] = jnp.zeros((tail, frames), bf16)
    for g in range(SIDE // BAND):
        rows = pl.ds(g * band, band)
        reach = sides_ref.shape[2]
        side = dot(sides_ref[g], wide_halo[pl.ds(g * BAND * CYCLE, reach), :]).reshape(BAND, CYCLE, frames)
        left = jnp.where(tile == 0, 0.0, side)
        right = jnp.where(tile == 0, side, 0.0)
        x = x_ref[rows, :].reshape(BAND, SIDE, frames)
        x = jnp.concatenate(
            [x[:, :CYCLE] + left, x[:, CYCLE : SIDE - CYCLE], x[:, SIDE - CYCLE :] + right], axis=1)
        back = x.reshape(band, frames).astype(bf16)
        if back_ref is not None:
            back_ref[rows, :] = back
        err[rows, :] = (back.astype(f32) - d_ref[rows, :]).astype(bf16)
    grad = lax.dot_general(foot_ref[...], err[...], (((0,), (0,)), ((), ())), preferred_element_type=f32)
    comps = grad.shape[0]
    live = lax.broadcasted_iota(i32, (comps, 1), 0) < count
    moved = jnp.maximum(trace_ref[...].astype(f32) - grad / den_ref[:, :1], 0.0)
    return jnp.where(live, moved, 0.0)


def pass_kernel(tile_ref, count_ref, halo_ref, sides_ref, x_ref, d_ref, foot_ref, trace_ref, den_ref,
                movie_ref, new_trace_ref, new_d_ref, new_r_ref, pay_ref, wide_halo, err):
    tile, count = tile_ref[0], count_ref[0]
    trace = trace_step(tile, count, halo_ref, sides_ref, x_ref, d_ref, foot_ref, trace_ref, den_ref,
                       wide_halo, err).astype(bf16)
    new_trace_ref[...] = trace
    for g in range(SIDE // BAND):
        resid_band(g, tile, movie_ref, foot_ref[pl.ds(g * BAND * SIDE, BAND * SIDE), :], trace,
                   new_d_ref, new_r_ref, pay_ref)


def last_kernel(block, share, tile_ref, count_ref, halo_ref, sides_ref, x_ref, d_ref, foot_ref, trace_ref,
                den_ref, movie_ref, cr_ref, cc_ref, rad_ref, slot_ref,
                trace_hbm, part_ref, fold_ref, wide_halo, err, back, masked, new_trace, sem):
    tile, count = tile_ref[0], count_ref[0]
    trace = trace_step(tile, count, halo_ref, sides_ref, x_ref, d_ref, foot_ref, trace_ref, den_ref,
                       wide_halo, err, back).astype(bf16)
    new_trace[...] = trace
    store = pltpu.make_async_copy(new_trace, trace_hbm, sem)
    store.start()
    comps = trace.shape[0]
    tf = trace.astype(f32)
    energy = jnp.sum(tf * tf, axis=1, keepdims=True)
    energy = jnp.transpose(jnp.broadcast_to(energy, (comps, LANES)))[:1]
    high = energy.astype(bf16).astype(f32)
    low = energy - high
    gap_sq = col_gap_sq(cc_ref[...])
    cr, rad = cr_ref[...], rad_ref[...]
    band = BAND * SIDE
    for g in range(SIDE // BAND):
        rows = pl.ds(g * band, band)
        prod = dot(foot_ref[rows, :], trace)
        ferr = (prod + back[rows, :].astype(f32) - movie_ref[rows, :].astype(f32)).astype(bf16)
        grad = lax.dot_general(ferr, trace, (((1,), (1,)), ((), ())), preferred_element_type=f32)
        for i in range(BAND):
            row = g * BAND + i
            keep = gap_sq <= disc_limit(cr, rad, count, row)
            masked[g % 2, pl.ds(g // 2 * band + i * SIDE, SIDE), :] = jnp.where(
                keep, grad[i * SIDE : (i + 1) * SIDE], 0.0).astype(bf16)
    half, taken = fold_ref.shape
    at = lax.broadcasted_iota(i32, (half, taken), 0)
    fold = jnp.where(at == slot_ref[...], 1.0, 0.0).astype(bf16)
    fold_ref[...] = fold
    inner = lax.rem(lax.broadcasted_iota(i32, (half, comps), 0), block)
    for h in range(2):
        part = dot(fold, masked[h])
        part = jnp.where(inner == share, high, jnp.where(inner == share + 1, low, part))
        part_ref[h * half : (h + 1) * half, :] = part.astype(bf16)
    store.wait()


def foot_fold_kernel(fold_ref, foot_ref, out_ref):
    half = fold_ref.shape[0]
    band = BAND * SIDE
    for h in range(2):
        foot = jnp.concatenate(
            [foot_ref[g * band : (g + 1) * band, :] for g in range(h, SIDE // BAND, 2)], axis=0)
        out_ref[h * half : (h + 1) * half, :] = dot(fold_ref[...], foot)


def share_kernel(share, me_ref, parts_ref, ffold_ref, out_ref):
    parts, block, comps = parts_ref.shape
    total = jnp.zeros((block, comps), f32)
    for j in range(parts):
        total = total + parts_ref[j].astype(f32)
    den = total[share : share + 1] + total[share + 1 : share + 2] + RIDGE
    foot = ffold_ref[pl.ds(pl.multiple_of(me_ref[0] * block, 8), block), :]
    moved = jnp.maximum(foot - total / den, 0.0).astype(bf16)
    for j in range(parts):
        out_ref[j] = moved


def unfold_kernel(count_ref, all_ref, fold_ref, cr_ref, cc_ref, rad_ref, out_hbm, buf, sems):
    count = count_ref[0]
    half = fold_ref.shape[0]
    gap_sq = col_gap_sq(cc_ref[...])
    cr, rad = cr_ref[...], rad_ref[...]
    band = BAND * SIDE
    stores = []
    for g in range(SIDE // BAND):
        h, b = g % 2, g // 2
        wide = lax.dot_general(fold_ref[:, b * band : (b + 1) * band], all_ref[h * half : (h + 1) * half, :],
                               (((0,), (0,)), ((), ())), preferred_element_type=f32)
        for i in range(BAND):
            row = g * BAND + i
            keep = gap_sq <= disc_limit(cr, rad, count, row)
            buf[pl.ds(row * SIDE, SIDE), :] = jnp.where(keep, wide[i * SIDE : (i + 1) * SIDE], 0.0).astype(bf16)
        rows = pl.ds(g * band, band)
        stores.append(pltpu.make_async_copy(buf.at[rows, :], out_hbm.at[rows, :], sems.at[g]))
        stores[-1].start()
    for store in stores:
        store.wait()


def swap(x):
    count = lax.axis_size("tile")
    return lax.ppermute(x, "tile", [(i, count - 1 - i) for i in range(count)])


def shards(movie, cycle_weights, footprints, traces, centre_row, centre_col, radius, comp_count):
    assert lax.axis_size("tile") == 2
    parts = lax.axis_size("tm")
    movie, fp, tr = movie[0], footprints[0], traces[0]
    weights = jnp.swapaxes(cycle_weights[0], 0, 1)
    pixels, frames = movie.shape
    comps = tr.shape[0]
    band = BAND * SIDE
    bands = SIDE // BAND
    edge = SIDE * CYCLE
    reach = (BAND + 2 * CYCLE) * SIDE
    tile = lax.axis_index("tile").astype(i32).reshape(1)
    me = lax.axis_index("tm").astype(i32).reshape(1)
    own, beside = band_tables()
    slots, share, block = fold_rows(parts)
    packed = parts * block
    sds = jax.ShapeDtypeStruct
    halo_pad = pltpu.VMEM((edge + 3 * CYCLE * CYCLE, frames), bf16)
    err_buf = pltpu.VMEM((pixels, frames), bf16)
    one_row = pltpu.VMEM((1, comps), i32)

    foot, trace, den, d, r, pay, movie = pl.pallas_call(
        start_kernel,
        out_shape=(sds((pixels, comps), bf16), sds((comps, frames), bf16), sds((comps, LANES), f32),
                   sds((pixels, frames), f32), sds((pixels, frames), bf16), sds((edge, frames), bf16),
                   sds((pixels, frames), bf16)),
        in_specs=[SM, SM] + [HB] * 6, out_specs=[VM] * 7,
        scratch_shapes=[pltpu.VMEM((pixels, comps), bf16), pltpu.VMEM((comps, frames), bf16),
                        one_row, one_row, one_row, pltpu.SemaphoreType.DMA((2 * bands + 4,))],
        compiler_params=params(),
    )(tile, comp_count, *[pltpu.with_memory_space_constraint(v, pltpu.HBM) for v in (movie, fp, tr, centre_row, centre_col, radius)])
    halo = swap(pay)
    banded_cost = pl.CostEstimate(flops=4_000_000_000, bytes_accessed=20_000_000, transcendentals=0)
    band_w, side_w, x = pl.pallas_call(
        build_kernel,
        out_shape=(sds((bands, band, reach), bf16), sds((bands, CYCLE * BAND, beside.shape[2]), bf16),
                   sds((pixels, frames), f32)),
        in_specs=[SM] + [VM] * 4, out_specs=[VM] * 3,
        scratch_shapes=[pltpu.VMEM((pixels, LANES), f32), pltpu.VMEM((bands * SIDE, reach), f32)],
        compiler_params=params(), cost_estimate=banded_cost,
    )(tile, weights, jnp.asarray(own), jnp.asarray(beside), r)
    trace, d, r, pay = pl.pallas_call(
        pass_kernel,
        out_shape=(sds((comps, frames), bf16), sds((pixels, frames), f32), sds((pixels, frames), bf16),
                   sds((edge, frames), bf16)),
        in_specs=[SM, SM] + [VM] * 8, out_specs=[VM] * 4,
        scratch_shapes=[halo_pad, err_buf], compiler_params=params(),
    )(tile, comp_count, halo, side_w, x, d, foot, trace, den, movie)
    halo = swap(pay)
    x = pl.pallas_call(
        banded_kernel,
        out_shape=sds((pixels, frames), f32),
        in_specs=[VM, VM], out_specs=VM, compiler_params=params(), cost_estimate=banded_cost,
    )(band_w, r)
    trace, part, fold = pl.pallas_call(
        functools.partial(last_kernel, block, share),
        out_shape=(sds((comps, frames), bf16), sds((packed, comps), bf16), sds((packed // 2, slots.shape[1]), bf16)),
        in_specs=[SM, SM] + [VM] * 12, out_specs=[HB, VM, VM],
        scratch_shapes=[halo_pad, err_buf, pltpu.VMEM((pixels, frames), bf16), pltpu.VMEM((2, pixels // 2, comps), bf16),
                        pltpu.VMEM((comps, frames), bf16), pltpu.SemaphoreType.DMA],
        compiler_params=params(14),
    )(tile, comp_count, halo, side_w, x, d, foot, trace, den, movie, centre_row, centre_col, radius, jnp.asarray(slots))
    received = lax.all_to_all(part.reshape(parts, block, comps), "tm", 0, 0, tiled=False)
    ffold = pl.pallas_call(
        foot_fold_kernel,
        out_shape=sds((packed, comps), f32),
        in_specs=[VM, VM], out_specs=VM, compiler_params=params(),
    )(fold, foot)
    moved = pl.pallas_call(
        functools.partial(share_kernel, share),
        out_shape=sds((parts, block, comps), bf16),
        in_specs=[SM, VM, VM], out_specs=VM, compiler_params=params(),
    )(me, received, ffold)
    every = lax.all_to_all(moved, "tm", 0, 0, tiled=False).reshape(packed, comps)
    new_foot = pl.pallas_call(
        unfold_kernel,
        out_shape=sds((pixels, comps), bf16),
        in_specs=[SM] + [VM] * 5, out_specs=HB,
        scratch_shapes=[pltpu.VMEM((pixels, comps), bf16), pltpu.SemaphoreType.DMA((bands,))],
        compiler_params=params(),
    )(comp_count, every, fold, centre_row, centre_col, radius)
    return (new_foot[None], trace[None])


def solution(mesh):
    in_specs = (
        P(("groups", "tile"), None, "tm"),
        P(("groups", "tile"), None, None),
        P(("groups", "tile"), None, None),
        P(("groups", "tile"), None, "tm"),
        P(("groups", "tile"), None),
        P(("groups", "tile"), None),
        P(("groups", "tile"), None),
        P(("groups", "tile")),
    )
    out_specs = (P(("groups", "tile"), None, None), P(("groups", "tile"), None, "tm"))
    return jax.shard_map(shards, mesh=mesh, in_specs=in_specs, out_specs=out_specs, check_vma=False)
```

```python
import functools

import jax
import jax.numpy as jnp
import numpy as np
from jax import lax
from jax.experimental import pallas as pl
from jax.experimental.pallas import tpu as pltpu
from jax.sharding import PartitionSpec as P

SIDE = 48
CYCLE = 8
PASSES = 2
RIDGE = 1.0
MAX_RADIUS = 9
BAND = 8
LANES = 128
OFFS_PAD = 64
HALF = SIDE // 2
REACH = HALF + CYCLE
COL_STEP = SIDE - REACH
RANGE = (BAND + 2 * CYCLE) * REACH

FOLD_R = 16
FOLD_C = 19
FOLD_SHIFT = 9
SLOTS = FOLD_R * FOLD_C

f32 = jnp.float32
bf16 = jnp.bfloat16
i32 = jnp.int32


def cycle_offsets():
    found = []
    for dy in range(-CYCLE, CYCLE + 1):
        for dx in range(-CYCLE, CYCLE + 1):
            if CYCLE * CYCLE <= dy * dy + dx * dx < (CYCLE + 1) * (CYCLE + 1):
                found.append((dy, dx))
    return found


def band_tables():
    offsets = cycle_offsets()
    none = len(offsets)
    own = np.full((OFFS_PAD, LANES), -1, np.int32)
    beside = np.full((2, BAND, CYCLE, 32, CYCLE), none, np.int32)
    for o, (dy, dx) in enumerate(offsets):
        own[o] = ((CYCLE + dy) * REACH + dx) % RANGE
        for i in range(BAND):
            for q in range(CYCLE):
                h = q + dx - CYCLE
                if 0 <= h < CYCLE:
                    beside[0, i, q, i + CYCLE + dy, h] = o
                h = q + dx + CYCLE
                if 0 <= h < CYCLE:
                    beside[1, i, q, i + CYCLE + dy, h] = o
    return own, beside.reshape(2, BAND * CYCLE, 32 * CYCLE)


def fold_rows(parts):
    share = -(-SLOTS // parts)
    block = -(-(share + 2) // 8) * 8
    assert SLOTS // 2 % share == 0 and FOLD_R == 2 * BAND
    low = np.arange(SIDE // FOLD_R)[:, None, None]
    row, col = np.arange(BAND)[:, None], np.arange(SIDE)
    slot = row * FOLD_C + (col + FOLD_SHIFT * low) % FOLD_C
    return (slot // share * block + slot % share).astype(np.int32).reshape(1, -1), share, block


def params(mib=12):
    return pltpu.CompilerParams(vmem_limit_bytes=mib * 2**20)


VM = pl.BlockSpec(memory_space=pltpu.VMEM)
HB = pl.BlockSpec(memory_space=pltpu.HBM)
SM = pl.BlockSpec(memory_space=pltpu.SMEM)


def dot(a, b):
    return jnp.dot(a, b, preferred_element_type=f32)


def disc_limit(centre_row, radius, count, row):
    gap = row - centre_row
    live = lax.broadcasted_iota(i32, centre_row.shape, 1) < count
    return jnp.where(live, radius * radius - gap * gap, -1)


def col_gap_sq(centre_col):
    gap = lax.broadcasted_iota(i32, (SIDE, centre_col.shape[1]), 0) - centre_col
    return gap * gap


def resid_band(g, tile, movie_ref, foot, trace, d_ref, r_ref, pay_ref):
    band = BAND * SIDE
    d = movie_ref[pl.ds(g * band, band), :].astype(f32) - dot(foot, trace)
    d3 = d.reshape(BAND, SIDE, d.shape[1])
    d_ref[pl.ds(g * BAND, BAND)] = d3
    r_ref[pl.ds(g * BAND, BAND)] = d3.astype(bf16)
    edge = jnp.where(tile == 0, d3[:, SIDE - CYCLE :], d3[:, :CYCLE])
    pay_ref[pl.ds(g * BAND * CYCLE, BAND * CYCLE), :] = edge.reshape(BAND * CYCLE, d.shape[1]).astype(bf16)


def build_bands(tile, w, at, beside, bands_ref, sides_ref, weights, wide):
    bands = SIDE // BAND
    blocks = RANGE // LANES
    offs = w.shape[0]
    eye = lax.broadcasted_iota(i32, (offs, LANES), 0) == lax.broadcasted_iota(i32, (offs, LANES), 1)
    weights[...] = lax.dot_general(w, jnp.where(eye, 1.0, 0.0).astype(bf16), (((0,), (0,)), ((), ())),
                                   preferred_element_type=f32)
    column = lax.broadcasted_iota(i32, (HALF, LANES), 0)
    lane = lax.broadcasted_iota(i32, (HALF, LANES), 1)
    shifts = [(HALF - COL_STEP) * h for h in range(2)]
    carried = [lane < column + shift for shift in shifts]
    inside = [jnp.abs(lax.rem(lane, REACH) - column - shift) <= CYCLE for shift in shifts]
    target = lax.broadcasted_iota(i32, (OFFS_PAD, RANGE), 1)
    for i in range(0, BAND, 2):
        for k in range(2):
            moved = at + (i + k) * REACH
            moved = jnp.where(moved >= RANGE, moved - RANGE, moved)
            pick = jnp.where(target == jnp.where(at < 0, -1, moved), 1.0, 0.0).astype(bf16)
            rows = [weights[(g * BAND + i + k) * SIDE : (g * BAND + i + k + 1) * SIDE, :OFFS_PAD] for g in range(bands)]
            wide[k] = dot(jnp.concatenate(rows, axis=0).astype(bf16), pick)
        for g in range(bands):
            for h in range(2):
                start = g * SIDE + h * HALF
                turned = [[pltpu.roll(wide[k, start : start + HALF, v * LANES : (v + 1) * LANES], shifts[h], 1,
                                      stride=1, stride_axis=0) for v in range(blocks)] for k in range(2)]
                for v in range(blocks):
                    pair = [jnp.where(inside[h], jnp.where(carried[h], turned[k][v - 1], turned[k][v]), 0.0)
                            for k in range(2)]
                    bands_ref[g, h, i * HALF : (i + 2) * HALF, v * LANES : (v + 1) * LANES] = jnp.concatenate(
                        pair, axis=0).astype(bf16)
    for g in range(bands):
        edges = []
        for i in range(BAND):
            base = (g * BAND + i) * SIDE
            edges.append(jnp.where(tile == 0, weights[base + SIDE - CYCLE : base + SIDE, :],
                                   weights[base : base + CYCLE, :]))
        edge = jnp.concatenate(edges, axis=0)
        for v in range(2):
            lanes = slice(v * LANES, (v + 1) * LANES)
            sides_ref[g, :, lanes] = jnp.take_along_axis(edge, beside[:, lanes], axis=1).astype(bf16)


def start_kernel(tile_ref, count_ref, movie_hbm, fp_hbm, tr_hbm, cr_hbm, cc_hbm, rad_hbm,
                 w_hbm, own_hbm, beside_hbm,
                 foot_ref, trace_ref, den_ref, d_ref, r_ref, pay_ref, movie_ref, bands_ref, sides_ref,
                 fp_ref, tr_ref, cr_ref, cc_ref, rad_ref, w_ref, own_ref, beside_ref, weights, wide, sems):
    count, tile = count_ref[0], tile_ref[0]
    comps = tr_ref.shape[0]
    band = BAND * SIDE
    bands = SIDE // BAND
    small = [pltpu.make_async_copy(src, dst, sems.at[2 * bands + n]) for n, (src, dst) in enumerate(
        ((w_hbm, w_ref), (own_hbm, own_ref), (beside_hbm.at[tile], beside_ref),
         (cr_hbm, cr_ref), (cc_hbm, cc_ref), (rad_hbm, rad_ref), (tr_hbm, tr_ref)))]
    fps, movies = [], []
    for g in range(bands):
        rows = pl.ds(g * band, band)
        fps.append(pltpu.make_async_copy(fp_hbm.at[rows, :], fp_ref.at[rows, :], sems.at[g]))
        movies.append(pltpu.make_async_copy(movie_hbm.at[rows, :], movie_ref.at[rows, :], sems.at[bands + g]))
    for copy in small:
        copy.start()
    for g in range(bands):
        fps[g].start()
        movies[g].start()
    for copy in small:
        copy.wait()
    build_bands(tile, w_ref[...], own_ref[:, :1], beside_ref[...], bands_ref, sides_ref, weights, wide)
    live = lax.broadcasted_iota(i32, (comps, 1), 0) < count
    trace = jnp.where(live, tr_ref[...].astype(f32), 0.0).astype(bf16)
    trace_ref[...] = trace
    gap_sq = col_gap_sq(cc_ref[...])
    cr, rad = cr_ref[...], rad_ref[...]
    total = jnp.zeros((8, comps), f32)
    for g in range(bands):
        fps[g].wait()
        for i in range(BAND):
            row = g * BAND + i
            keep = gap_sq <= disc_limit(cr, rad, count, row)
            foot = jnp.where(keep, fp_ref[pl.ds(row * SIDE, SIDE), :].astype(f32), 0.0)
            foot_ref[pl.ds(row * SIDE, SIDE), :] = foot.astype(bf16)
            total = total + jnp.sum((foot * foot).reshape(SIDE // 8, 8, comps), axis=0)
        movies[g].wait()
        resid_band(g, tile, movie_ref, foot_ref[pl.ds(g * band, band), :], trace, d_ref, r_ref, pay_ref)
    energy = jnp.sum(total, axis=0, keepdims=True) + RIDGE
    den_ref[...] = jnp.transpose(jnp.broadcast_to(energy, (LANES, comps)))


def banded_kernel(bands_ref, r_ref, x_ref):
    frames = r_ref.shape[2]
    for g in range(SIDE // BAND):
        low = max(0, CYCLE - g * BAND)
        high = min(BAND + 2 * CYCLE, SIDE + CYCLE - g * BAND)
        first = g * BAND + low - CYCLE
        for h in range(2):
            r = r_ref[first : first + high - low, h * COL_STEP : h * COL_STEP + REACH, :]
            x = dot(bands_ref[g, h, :, low * REACH : high * REACH], r.reshape((high - low) * REACH, frames))
            x_ref[g * BAND : (g + 1) * BAND, h * HALF : (h + 1) * HALF, :] = x.reshape(BAND, HALF, frames)


def trace_step(tile, count, halo_ref, sides_ref, x_ref, d_ref, foot_ref, trace_ref, den_ref,
               wide_halo, err, back_ref=None):
    frames = x_ref.shape[2]
    band, edge = BAND * SIDE, CYCLE * SIDE
    pad = CYCLE * CYCLE
    wide_halo[:pad, :] = jnp.zeros((pad, frames), bf16)
    wide_halo[pl.ds(pad, edge), :] = halo_ref[...]
    tail = wide_halo.shape[0] - pad - edge
    wide_halo[pl.ds(pad + edge, tail), :] = jnp.zeros((tail, frames), bf16)
    for g in range(SIDE // BAND):
        rows = pl.ds(g * band, band)
        reach = sides_ref.shape[2]
        side = dot(sides_ref[g], wide_halo[pl.ds(g * BAND * CYCLE, reach), :]).reshape(BAND, CYCLE, frames)
        left = jnp.where(tile == 0, 0.0, side)
        right = jnp.where(tile == 0, side, 0.0)
        x = x_ref[pl.ds(g * BAND, BAND)]
        x = jnp.concatenate(
            [x[:, :CYCLE] + left, x[:, CYCLE : SIDE - CYCLE], x[:, SIDE - CYCLE :] + right], axis=1)
        back = x.reshape(band, frames).astype(bf16)
        if back_ref is not None:
            back_ref[rows, :] = back
        d = d_ref[pl.ds(g * BAND, BAND)].reshape(band, frames)
        err[rows, :] = (back.astype(f32) - d).astype(bf16)
    grad = lax.dot_general(foot_ref[...], err[...], (((0,), (0,)), ((), ())), preferred_element_type=f32)
    comps = grad.shape[0]
    live = lax.broadcasted_iota(i32, (comps, 1), 0) < count
    moved = jnp.maximum(trace_ref[...].astype(f32) - grad / den_ref[:, :1], 0.0)
    return jnp.where(live, moved, 0.0)


def pass_kernel(tile_ref, count_ref, halo_ref, sides_ref, x_ref, d_ref, foot_ref, trace_ref, den_ref,
                movie_ref, new_trace_ref, new_d_ref, new_r_ref, pay_ref, wide_halo, err):
    tile, count = tile_ref[0], count_ref[0]
    trace = trace_step(tile, count, halo_ref, sides_ref, x_ref, d_ref, foot_ref, trace_ref, den_ref,
                       wide_halo, err).astype(bf16)
    new_trace_ref[...] = trace
    for g in range(SIDE // BAND):
        resid_band(g, tile, movie_ref, foot_ref[pl.ds(g * BAND * SIDE, BAND * SIDE), :], trace,
                   new_d_ref, new_r_ref, pay_ref)


def last_kernel(block, share, tile_ref, count_ref, halo_ref, sides_ref, x_ref, d_ref, foot_ref, trace_ref,
                den_ref, movie_ref, cr_ref, cc_ref, rad_ref, slot_ref,
                trace_hbm, part_ref, fold_ref, wide_halo, err, back, masked, new_trace, sem):
    tile, count = tile_ref[0], count_ref[0]
    trace = trace_step(tile, count, halo_ref, sides_ref, x_ref, d_ref, foot_ref, trace_ref, den_ref,
                       wide_halo, err, back).astype(bf16)
    new_trace[...] = trace
    store = pltpu.make_async_copy(new_trace, trace_hbm, sem)
    store.start()
    comps = trace.shape[0]
    tf = trace.astype(f32)
    energy = jnp.sum(tf * tf, axis=1, keepdims=True)
    energy = jnp.transpose(jnp.broadcast_to(energy, (comps, LANES)))[:1]
    high = energy.astype(bf16).astype(f32)
    low = energy - high
    gap_sq = col_gap_sq(cc_ref[...])
    cr, rad = cr_ref[...], rad_ref[...]
    band = BAND * SIDE
    for g in range(SIDE // BAND):
        rows = pl.ds(g * band, band)
        prod = dot(foot_ref[rows, :], trace)
        ferr = (prod + back[rows, :].astype(f32) - movie_ref[rows, :].astype(f32)).astype(bf16)
        grad = lax.dot_general(ferr, trace, (((1,), (1,)), ((), ())), preferred_element_type=f32)
        for i in range(BAND):
            row = g * BAND + i
            keep = gap_sq <= disc_limit(cr, rad, count, row)
            masked[g % 2, pl.ds(g // 2 * band + i * SIDE, SIDE), :] = jnp.where(
                keep, grad[i * SIDE : (i + 1) * SIDE], 0.0).astype(bf16)
    half, taken = fold_ref.shape
    at = lax.broadcasted_iota(i32, (half, taken), 0)
    fold = jnp.where(at == slot_ref[...], 1.0, 0.0).astype(bf16)
    fold_ref[...] = fold
    inner = lax.rem(lax.broadcasted_iota(i32, (half, comps), 0), block)
    for h in range(2):
        part = dot(fold, masked[h])
        part = jnp.where(inner == share, high, jnp.where(inner == share + 1, low, part))
        part_ref[h * half : (h + 1) * half, :] = part.astype(bf16)
    store.wait()


def foot_fold_kernel(fold_ref, foot_ref, out_ref):
    half = fold_ref.shape[0]
    band = BAND * SIDE
    for h in range(2):
        foot = jnp.concatenate(
            [foot_ref[g * band : (g + 1) * band, :] for g in range(h, SIDE // BAND, 2)], axis=0)
        out_ref[h * half : (h + 1) * half, :] = dot(fold_ref[...], foot)


def share_kernel(share, me_ref, parts_ref, ffold_ref, out_ref):
    parts, block, comps = parts_ref.shape
    total = jnp.zeros((block, comps), f32)
    for j in range(parts):
        total = total + parts_ref[j].astype(f32)
    den = total[share : share + 1] + total[share + 1 : share + 2] + RIDGE
    foot = ffold_ref[pl.ds(pl.multiple_of(me_ref[0] * block, 8), block), :]
    moved = jnp.maximum(foot - total / den, 0.0).astype(bf16)
    for j in range(parts):
        out_ref[j] = moved


def unfold_kernel(count_ref, all_ref, fold_ref, cr_ref, cc_ref, rad_ref, out_hbm, buf, sems):
    count = count_ref[0]
    half = fold_ref.shape[0]
    gap_sq = col_gap_sq(cc_ref[...])
    cr, rad = cr_ref[...], rad_ref[...]
    band = BAND * SIDE
    stores = []
    for g in range(SIDE // BAND):
        h, b = g % 2, g // 2
        wide = lax.dot_general(fold_ref[:, b * band : (b + 1) * band], all_ref[h * half : (h + 1) * half, :],
                               (((0,), (0,)), ((), ())), preferred_element_type=f32)
        for i in range(BAND):
            row = g * BAND + i
            keep = gap_sq <= disc_limit(cr, rad, count, row)
            buf[pl.ds(row * SIDE, SIDE), :] = jnp.where(keep, wide[i * SIDE : (i + 1) * SIDE], 0.0).astype(bf16)
        rows = pl.ds(g * band, band)
        stores.append(pltpu.make_async_copy(buf.at[rows, :], out_hbm.at[rows, :], sems.at[g]))
        stores[-1].start()
    for store in stores:
        store.wait()


def swap(x):
    count = lax.axis_size("tile")
    return lax.ppermute(x, "tile", [(i, count - 1 - i) for i in range(count)])


def shards(movie, cycle_weights, footprints, traces, centre_row, centre_col, radius, comp_count):
    assert lax.axis_size("tile") == 2
    parts = lax.axis_size("tm")
    movie, fp, tr = movie[0], footprints[0], traces[0]
    weights = jnp.swapaxes(cycle_weights[0], 0, 1)
    pixels, frames = movie.shape
    comps = tr.shape[0]
    band = BAND * SIDE
    bands = SIDE // BAND
    edge = SIDE * CYCLE
    tile = lax.axis_index("tile").astype(i32).reshape(1)
    me = lax.axis_index("tm").astype(i32).reshape(1)
    own, beside = band_tables()
    slots, share, block = fold_rows(parts)
    packed = parts * block
    sds = jax.ShapeDtypeStruct
    halo_pad = pltpu.VMEM((edge + 3 * CYCLE * CYCLE, frames), bf16)
    err_buf = pltpu.VMEM((pixels, frames), bf16)
    one_row = pltpu.VMEM((1, comps), i32)

    d_shape, r_shape = sds((SIDE, SIDE, frames), f32), sds((SIDE, SIDE, frames), bf16)
    inputs = [pltpu.with_memory_space_constraint(v, pltpu.HBM) for v in (
        movie, fp, tr, centre_row, centre_col, radius, weights, jnp.asarray(own), jnp.asarray(beside))]
    foot, trace, den, d, r, pay, movie, band_w, side_w = pl.pallas_call(
        start_kernel,
        out_shape=(sds((pixels, comps), bf16), sds((comps, frames), bf16), sds((comps, LANES), f32),
                   d_shape, r_shape, sds((edge, frames), bf16), sds((pixels, frames), bf16),
                   sds((bands, 2, BAND * HALF, RANGE), bf16), sds((bands, CYCLE * BAND, beside.shape[2]), bf16)),
        in_specs=[SM, SM] + [HB] * 9, out_specs=[VM] * 9,
        scratch_shapes=[pltpu.VMEM((pixels, comps), bf16), pltpu.VMEM((comps, frames), bf16),
                        one_row, one_row, one_row, pltpu.VMEM(weights.shape, bf16), pltpu.VMEM(own.shape, i32),
                        pltpu.VMEM(beside.shape[1:], i32), pltpu.VMEM((pixels, LANES), f32),
                        pltpu.VMEM((2, bands * SIDE, RANGE), f32), pltpu.SemaphoreType.DMA((2 * bands + 7,))],
        compiler_params=params(16),
    )(tile, comp_count, *inputs)
    banded = pl.pallas_call(
        banded_kernel,
        out_shape=d_shape, in_specs=[VM, VM], out_specs=VM, compiler_params=params(),
        cost_estimate=pl.CostEstimate(flops=4_000_000_000, bytes_accessed=20_000_000, transcendentals=0),
    )
    halo = swap(pay)
    x = banded(band_w, r)
    trace, d, r, pay = pl.pallas_call(
        pass_kernel,
        out_shape=(sds((comps, frames), bf16), d_shape, r_shape, sds((edge, frames), bf16)),
        in_specs=[SM, SM] + [VM] * 8, out_specs=[VM] * 4,
        scratch_shapes=[halo_pad, err_buf], compiler_params=params(),
    )(tile, comp_count, halo, side_w, x, d, foot, trace, den, movie)
    halo = swap(pay)
    x = banded(band_w, r)
    trace, part, fold = pl.pallas_call(
        functools.partial(last_kernel, block, share),
        out_shape=(sds((comps, frames), bf16), sds((packed, comps), bf16), sds((packed // 2, slots.shape[1]), bf16)),
        in_specs=[SM, SM] + [VM] * 12, out_specs=[HB, VM, VM],
        scratch_shapes=[halo_pad, err_buf, pltpu.VMEM((pixels, frames), bf16), pltpu.VMEM((2, pixels // 2, comps), bf16),
                        pltpu.VMEM((comps, frames), bf16), pltpu.SemaphoreType.DMA],
        compiler_params=params(14),
    )(tile, comp_count, halo, side_w, x, d, foot, trace, den, movie, centre_row, centre_col, radius, jnp.asarray(slots))
    received = lax.all_to_all(part.reshape(parts, block, comps), "tm", 0, 0, tiled=False)
    ffold = pl.pallas_call(
        foot_fold_kernel,
        out_shape=sds((packed, comps), f32),
        in_specs=[VM, VM], out_specs=VM, compiler_params=params(),
    )(fold, foot)
    moved = pl.pallas_call(
        functools.partial(share_kernel, share),
        out_shape=sds((parts, block, comps), bf16),
        in_specs=[SM, VM, VM], out_specs=VM, compiler_params=params(),
    )(me, received, ffold)
    every = lax.all_to_all(moved, "tm", 0, 0, tiled=False).reshape(packed, comps)
    new_foot = pl.pallas_call(
        unfold_kernel,
        out_shape=sds((pixels, comps), bf16),
        in_specs=[SM] + [VM] * 5, out_specs=HB,
        scratch_shapes=[pltpu.VMEM((pixels, comps), bf16), pltpu.SemaphoreType.DMA((bands,))],
        compiler_params=params(),
    )(comp_count, every, fold, centre_row, centre_col, radius)
    return (new_foot[None], trace[None])


def solution(mesh):
    in_specs = (
        P(("groups", "tile"), None, "tm"),
        P(("groups", "tile"), None, None),
        P(("groups", "tile"), None, None),
        P(("groups", "tile"), None, "tm"),
        P(("groups", "tile"), None),
        P(("groups", "tile"), None),
        P(("groups", "tile"), None),
        P(("groups", "tile")),
    )
    out_specs = (P(("groups", "tile"), None, None), P(("groups", "tile"), None, "tm"))
    return jax.shard_map(shards, mesh=mesh, in_specs=in_specs, out_specs=out_specs, check_vma=False)
```

```python
import functools

import jax
import jax.numpy as jnp
import numpy as np
from jax import lax
from jax.experimental import pallas as pl
from jax.experimental.pallas import tpu as pltpu
from jax.sharding import PartitionSpec as P

SIDE = 48
CYCLE = 8
PASSES = 2
RIDGE = 1.0
MAX_RADIUS = 9
BAND = 8
LANES = 128
OFFS_PAD = 64
HALF = SIDE // 2
REACH = HALF + CYCLE
COL_STEP = SIDE - REACH
RANGE = (BAND + 2 * CYCLE) * REACH

FOLD_R = 16
FOLD_C = 19
FOLD_SHIFT = 9
SLOTS = FOLD_R * FOLD_C

f32 = jnp.float32
bf16 = jnp.bfloat16
i32 = jnp.int32


def cycle_offsets():
    found = []
    for dy in range(-CYCLE, CYCLE + 1):
        for dx in range(-CYCLE, CYCLE + 1):
            if CYCLE * CYCLE <= dy * dy + dx * dx < (CYCLE + 1) * (CYCLE + 1):
                found.append((dy, dx))
    return found


def band_tables():
    offsets = cycle_offsets()
    none = len(offsets)
    own = np.full((OFFS_PAD, LANES), -1, np.int32)
    beside = np.full((2, BAND, CYCLE, 32, CYCLE), none, np.int32)
    for o, (dy, dx) in enumerate(offsets):
        own[o] = ((CYCLE + dy) * REACH + dx) % RANGE
        for i in range(BAND):
            for q in range(CYCLE):
                h = q + dx - CYCLE
                if 0 <= h < CYCLE:
                    beside[0, i, q, i + CYCLE + dy, h] = o
                h = q + dx + CYCLE
                if 0 <= h < CYCLE:
                    beside[1, i, q, i + CYCLE + dy, h] = o
    return own, beside.reshape(2, BAND * CYCLE, 32 * CYCLE)


def fold_rows(parts):
    share = -(-SLOTS // parts)
    block = -(-(share + 2) // 8) * 8
    assert SLOTS // 2 % share == 0 and FOLD_R == 2 * BAND
    low = np.arange(SIDE // FOLD_R)[:, None, None]
    row, col = np.arange(BAND)[:, None], np.arange(SIDE)
    slot = row * FOLD_C + (col + FOLD_SHIFT * low) % FOLD_C
    return (slot // share * block + slot % share).astype(np.int32).reshape(1, -1), share, block


def params(mib=12):
    return pltpu.CompilerParams(vmem_limit_bytes=mib * 2**20)


VM = pl.BlockSpec(memory_space=pltpu.VMEM)
HB = pl.BlockSpec(memory_space=pltpu.HBM)
SM = pl.BlockSpec(memory_space=pltpu.SMEM)


def dot(a, b):
    return jnp.dot(a, b, preferred_element_type=f32)


def disc_limit(centre_row, radius, count, row):
    gap = row - centre_row
    live = lax.broadcasted_iota(i32, centre_row.shape, 1) < count
    return jnp.where(live, radius * radius - gap * gap, -1)


def col_gap_sq(centre_col):
    gap = lax.broadcasted_iota(i32, (SIDE, centre_col.shape[1]), 0) - centre_col
    return gap * gap


def resid_band(g, tile, movie_ref, foot, trace, r_ref, pay_ref):
    band = BAND * SIDE
    d = movie_ref[pl.ds(g * band, band), :].astype(f32) - dot(foot, trace)
    d3 = d.reshape(BAND, SIDE, d.shape[1])
    r_ref[pl.ds(g * BAND, BAND)] = d3.astype(bf16)
    edge = jnp.where(tile == 0, d3[:, SIDE - CYCLE :], d3[:, :CYCLE])
    pay_ref[pl.ds(g * BAND * CYCLE, BAND * CYCLE), :] = edge.reshape(BAND * CYCLE, d.shape[1]).astype(bf16)


def build_bands(tile, w, at, beside, bands_ref, sides_ref, weights, wide):
    bands = SIDE // BAND
    blocks = RANGE // LANES
    offs = w.shape[0]
    eye = lax.broadcasted_iota(i32, (offs, LANES), 0) == lax.broadcasted_iota(i32, (offs, LANES), 1)
    weights[...] = lax.dot_general(w, jnp.where(eye, 1.0, 0.0).astype(bf16), (((0,), (0,)), ((), ())),
                                   preferred_element_type=f32)
    column = lax.broadcasted_iota(i32, (HALF, LANES), 0)
    lane = lax.broadcasted_iota(i32, (HALF, LANES), 1)
    shifts = [(HALF - COL_STEP) * h for h in range(2)]
    carried = [lane < column + shift for shift in shifts]
    inside = [jnp.abs(lax.rem(lane, REACH) - column - shift) <= CYCLE for shift in shifts]
    target = lax.broadcasted_iota(i32, (OFFS_PAD, RANGE), 1)
    for i in range(0, BAND, 2):
        for k in range(2):
            moved = at + (i + k) * REACH
            moved = jnp.where(moved >= RANGE, moved - RANGE, moved)
            pick = jnp.where(target == jnp.where(at < 0, -1, moved), 1.0, 0.0).astype(bf16)
            rows = [weights[(g * BAND + i + k) * SIDE : (g * BAND + i + k + 1) * SIDE, :OFFS_PAD] for g in range(bands)]
            wide[k] = dot(jnp.concatenate(rows, axis=0).astype(bf16), pick)
        for g in range(bands):
            for h in range(2):
                start = g * SIDE + h * HALF
                turned = [[pltpu.roll(wide[k, start : start + HALF, v * LANES : (v + 1) * LANES], shifts[h], 1,
                                      stride=1, stride_axis=0) for v in range(blocks)] for k in range(2)]
                for v in range(blocks):
                    pair = [jnp.where(inside[h], jnp.where(carried[h], turned[k][v - 1], turned[k][v]), 0.0)
                            for k in range(2)]
                    bands_ref[g, h, i * HALF : (i + 2) * HALF, v * LANES : (v + 1) * LANES] = jnp.concatenate(
                        pair, axis=0).astype(bf16)
    for g in range(bands):
        edges = []
        for i in range(BAND):
            base = (g * BAND + i) * SIDE
            edges.append(jnp.where(tile == 0, weights[base + SIDE - CYCLE : base + SIDE, :],
                                   weights[base : base + CYCLE, :]))
        edge = jnp.concatenate(edges, axis=0)
        for v in range(2):
            lanes = slice(v * LANES, (v + 1) * LANES)
            sides_ref[g, :, lanes] = jnp.take_along_axis(edge, beside[:, lanes], axis=1).astype(bf16)


def start_kernel(tile_ref, count_ref, movie_hbm, fp_hbm, tr_hbm, cr_hbm, cc_hbm, rad_hbm,
                 w_hbm, own_hbm, beside_hbm,
                 foot_ref, trace_ref, den_ref, r_ref, pay_ref, movie_ref, bands_ref, sides_ref,
                 fp_ref, tr_ref, cr_ref, cc_ref, rad_ref, w_ref, own_ref, beside_ref, weights, wide, sems):
    count, tile = count_ref[0], tile_ref[0]
    comps = tr_ref.shape[0]
    band = BAND * SIDE
    bands = SIDE // BAND
    small = [pltpu.make_async_copy(src, dst, sems.at[2 * bands + n]) for n, (src, dst) in enumerate(
        ((w_hbm, w_ref), (own_hbm, own_ref), (beside_hbm.at[tile], beside_ref),
         (cr_hbm, cr_ref), (cc_hbm, cc_ref), (rad_hbm, rad_ref), (tr_hbm, tr_ref)))]
    fps, movies = [], []
    for g in range(bands):
        rows = pl.ds(g * band, band)
        fps.append(pltpu.make_async_copy(fp_hbm.at[rows, :], fp_ref.at[rows, :], sems.at[g]))
        movies.append(pltpu.make_async_copy(movie_hbm.at[rows, :], movie_ref.at[rows, :], sems.at[bands + g]))
    for copy in small:
        copy.start()
    for g in range(bands):
        fps[g].start()
        movies[g].start()
    for copy in small[:3]:
        copy.wait()
    build_bands(tile, w_ref[...], own_ref[:, :1], beside_ref[...], bands_ref, sides_ref, weights, wide)
    for copy in small[3:] + fps + movies:
        copy.wait()
    live = lax.broadcasted_iota(i32, (comps, 1), 0) < count
    trace = jnp.where(live, tr_ref[...].astype(f32), 0.0).astype(bf16)
    trace_ref[...] = trace
    gap_sq = col_gap_sq(cc_ref[...])
    cr, rad = cr_ref[...], rad_ref[...]
    total = jnp.zeros((8, comps), f32)
    for g in range(bands):
        for i in range(BAND):
            row = g * BAND + i
            keep = gap_sq <= disc_limit(cr, rad, count, row)
            foot = jnp.where(keep, fp_ref[pl.ds(row * SIDE, SIDE), :].astype(f32), 0.0)
            foot_ref[pl.ds(row * SIDE, SIDE), :] = foot.astype(bf16)
            total = total + jnp.sum((foot * foot).reshape(SIDE // 8, 8, comps), axis=0)
        resid_band(g, tile, movie_ref, foot_ref[pl.ds(g * band, band), :], trace, r_ref, pay_ref)
    energy = jnp.sum(total, axis=0, keepdims=True) + RIDGE
    den_ref[...] = jnp.transpose(jnp.broadcast_to(1.0 / energy, (LANES, comps)))


def banded_kernel(tile_ref, bands_ref, r_ref, x_ref, edge_ref):
    tile = tile_ref[0]
    frames = r_ref.shape[2]
    for g in range(SIDE // BAND):
        low = max(0, CYCLE - g * BAND)
        high = min(BAND + 2 * CYCLE, SIDE + CYCLE - g * BAND)
        first = g * BAND + low - CYCLE
        halves = []
        for h in range(2):
            r = r_ref[first : first + high - low, h * COL_STEP : h * COL_STEP + REACH, :]
            x = dot(bands_ref[g, h, :, low * REACH : high * REACH], r.reshape((high - low) * REACH, frames))
            halves.append(x.reshape(BAND, HALF, frames))
        rows = pl.ds(g * BAND, BAND)
        edge_ref[rows] = jnp.where(tile == 0, halves[1][:, HALF - CYCLE :], halves[0][:, :CYCLE])
        x_ref[rows] = jnp.concatenate(halves, axis=1).astype(bf16)


def trace_step(tile, count, halo_ref, sides_ref, x_ref, edge_ref, r_ref, foot_ref, trace_ref, den_ref,
               wide_halo, err, back_ref=None):
    frames = x_ref.shape[2]
    band, edge = BAND * SIDE, CYCLE * SIDE
    pad = CYCLE * CYCLE
    wide_halo[:pad, :] = jnp.zeros((pad, frames), bf16)
    wide_halo[pl.ds(pad, edge), :] = halo_ref[...]
    tail = wide_halo.shape[0] - pad - edge
    wide_halo[pl.ds(pad + edge, tail), :] = jnp.zeros((tail, frames), bf16)
    for g in range(SIDE // BAND):
        rows = pl.ds(g * BAND, BAND)
        reach = sides_ref.shape[2]
        side = dot(sides_ref[g], wide_halo[pl.ds(g * BAND * CYCLE, reach), :]).reshape(BAND, CYCLE, frames)
        side = (edge_ref[rows] + side).astype(bf16).astype(f32)
        x = x_ref[rows].astype(f32)
        left = jnp.where(tile == 0, x[:, :CYCLE], side)
        right = jnp.where(tile == 0, side, x[:, SIDE - CYCLE :])
        back = jnp.concatenate([left, x[:, CYCLE : SIDE - CYCLE], right], axis=1)
        if back_ref is not None:
            back_ref[rows] = back.astype(bf16)
        err[pl.ds(g * band, band), :] = (back - r_ref[rows].astype(f32)).reshape(band, frames).astype(bf16)
    grad = lax.dot_general(foot_ref[...], err[...], (((0,), (0,)), ((), ())), preferred_element_type=f32)
    comps = grad.shape[0]
    live = lax.broadcasted_iota(i32, (comps, 1), 0) < count
    moved = jnp.maximum(trace_ref[...].astype(f32) - grad * den_ref[:, :1], 0.0)
    return jnp.where(live, moved, 0.0)


def pass_kernel(tile_ref, count_ref, halo_ref, sides_ref, x_ref, edge_ref, r_ref, foot_ref, trace_ref, den_ref,
                movie_ref, new_trace_ref, new_r_ref, pay_ref, wide_halo, err):
    tile, count = tile_ref[0], count_ref[0]
    trace = trace_step(tile, count, halo_ref, sides_ref, x_ref, edge_ref, r_ref, foot_ref, trace_ref, den_ref,
                       wide_halo, err).astype(bf16)
    new_trace_ref[...] = trace
    for g in range(SIDE // BAND):
        resid_band(g, tile, movie_ref, foot_ref[pl.ds(g * BAND * SIDE, BAND * SIDE), :], trace,
                   new_r_ref, pay_ref)


def last_kernel(block, share, tile_ref, count_ref, halo_ref, sides_ref, x_ref, edge_ref, r_ref, foot_ref, trace_ref,
                den_ref, movie_ref, cr_ref, cc_ref, rad_ref, slot_ref,
                trace_hbm, part_hbm, fold_ref, wide_halo, err, back, masked, new_trace, part_ref, sems):
    tile, count = tile_ref[0], count_ref[0]
    trace = trace_step(tile, count, halo_ref, sides_ref, x_ref, edge_ref, r_ref, foot_ref, trace_ref, den_ref,
                       wide_halo, err, back).astype(bf16)
    new_trace[...] = trace
    stores = [pltpu.make_async_copy(new_trace, trace_hbm, sems.at[2])]
    stores[0].start()
    comps = trace.shape[0]
    tf = trace.astype(f32)
    energy = jnp.sum(tf * tf, axis=1, keepdims=True)
    energy = jnp.transpose(jnp.broadcast_to(energy, (comps, LANES)))[:1]
    high = energy.astype(bf16).astype(f32)
    low = energy - high
    half, taken = fold_ref.shape
    at = lax.broadcasted_iota(i32, (half, taken), 0)
    fold = jnp.where(at == slot_ref[...], 1.0, 0.0).astype(bf16)
    fold_ref[...] = fold
    inner = lax.rem(lax.broadcasted_iota(i32, (half, comps), 0), block)
    gap_sq = col_gap_sq(cc_ref[...])
    cr, rad = cr_ref[...], rad_ref[...]
    band = BAND * SIDE
    for h in range(2):
        for g in range(h, SIDE // BAND, 2):
            rows = pl.ds(g * band, band)
            prod = dot(foot_ref[rows, :], trace)
            old = back[pl.ds(g * BAND, BAND)].reshape(band, prod.shape[1]).astype(f32)
            ferr = (prod + old - movie_ref[rows, :].astype(f32)).astype(bf16)
            grad = lax.dot_general(ferr, trace, (((1,), (1,)), ((), ())), preferred_element_type=f32)
            for i in range(BAND):
                keep = gap_sq <= disc_limit(cr, rad, count, g * BAND + i)
                masked[h, pl.ds(g // 2 * band + i * SIDE, SIDE), :] = jnp.where(
                    keep, grad[i * SIDE : (i + 1) * SIDE], 0.0).astype(bf16)
        part = dot(fold, masked[h])
        part = jnp.where(inner == share, high, jnp.where(inner == share + 1, low, part))
        rows = pl.ds(h * half, half)
        part_ref[rows, :] = part.astype(bf16)
        stores.append(pltpu.make_async_copy(part_ref.at[rows, :], part_hbm.at[rows, :], sems.at[h]))
        stores[-1].start()
    for store in stores:
        store.wait()


def foot_fold_kernel(fold_ref, foot_ref, out_ref):
    half = fold_ref.shape[0]
    band = BAND * SIDE
    for h in range(2):
        foot = jnp.concatenate(
            [foot_ref[g * band : (g + 1) * band, :] for g in range(h, SIDE // BAND, 2)], axis=0)
        out_ref[h * half : (h + 1) * half, :] = dot(fold_ref[...], foot)


def share_kernel(share, me_ref, parts_ref, ffold_ref, out_ref):
    parts, block, comps = parts_ref.shape
    total = jnp.zeros((block, comps), f32)
    for j in range(parts):
        total = total + parts_ref[j].astype(f32)
    den = total[share : share + 1] + total[share + 1 : share + 2] + RIDGE
    foot = ffold_ref[pl.ds(pl.multiple_of(me_ref[0] * block, 8), block), :]
    moved = jnp.maximum(foot - total / den, 0.0).astype(bf16)
    for j in range(parts):
        out_ref[j] = moved


def unfold_kernel(count_ref, all_ref, fold_ref, cr_ref, cc_ref, rad_ref, out_hbm, buf, sems):
    count = count_ref[0]
    half = fold_ref.shape[0]
    gap_sq = col_gap_sq(cc_ref[...])
    cr, rad = cr_ref[...], rad_ref[...]
    band = BAND * SIDE
    stores = []
    for g in range(SIDE // BAND):
        h, b = g % 2, g // 2
        wide = lax.dot_general(fold_ref[:, b * band : (b + 1) * band], all_ref[h * half : (h + 1) * half, :],
                               (((0,), (0,)), ((), ())), preferred_element_type=f32)
        for i in range(BAND):
            row = g * BAND + i
            keep = gap_sq <= disc_limit(cr, rad, count, row)
            buf[pl.ds(row * SIDE, SIDE), :] = jnp.where(keep, wide[i * SIDE : (i + 1) * SIDE], 0.0).astype(bf16)
        rows = pl.ds(g * band, band)
        stores.append(pltpu.make_async_copy(buf.at[rows, :], out_hbm.at[rows, :], sems.at[g]))
        stores[-1].start()
    for store in stores:
        store.wait()


def swap(x):
    count = lax.axis_size("tile")
    return lax.ppermute(x, "tile", [(i, count - 1 - i) for i in range(count)])


def shards(movie, cycle_weights, footprints, traces, centre_row, centre_col, radius, comp_count):
    assert lax.axis_size("tile") == 2
    parts = lax.axis_size("tm")
    movie, fp, tr = movie[0], footprints[0], traces[0]
    weights = jnp.swapaxes(cycle_weights[0], 0, 1)
    pixels, frames = movie.shape
    comps = tr.shape[0]
    band = BAND * SIDE
    bands = SIDE // BAND
    edge = SIDE * CYCLE
    tile = lax.axis_index("tile").astype(i32).reshape(1)
    me = lax.axis_index("tm").astype(i32).reshape(1)
    own, beside = band_tables()
    slots, share, block = fold_rows(parts)
    packed = parts * block
    sds = jax.ShapeDtypeStruct
    halo_pad = pltpu.VMEM((edge + 3 * CYCLE * CYCLE, frames), bf16)
    err_buf = pltpu.VMEM((pixels, frames), bf16)
    one_row = pltpu.VMEM((1, comps), i32)

    r_shape = sds((SIDE, SIDE, frames), bf16)
    inputs = [pltpu.with_memory_space_constraint(v, pltpu.HBM) for v in (
        movie, fp, tr, centre_row, centre_col, radius, weights, jnp.asarray(own), jnp.asarray(beside))]
    foot, trace, den, r, pay, movie, band_w, side_w = pl.pallas_call(
        start_kernel,
        out_shape=(sds((pixels, comps), bf16), sds((comps, frames), bf16), sds((comps, LANES), f32),
                   r_shape, sds((edge, frames), bf16), sds((pixels, frames), bf16),
                   sds((bands, 2, BAND * HALF, RANGE), bf16), sds((bands, CYCLE * BAND, beside.shape[2]), bf16)),
        in_specs=[SM, SM] + [HB] * 9, out_specs=[VM] * 8,
        scratch_shapes=[pltpu.VMEM((pixels, comps), bf16), pltpu.VMEM((comps, frames), bf16),
                        one_row, one_row, one_row, pltpu.VMEM(weights.shape, bf16), pltpu.VMEM(own.shape, i32),
                        pltpu.VMEM(beside.shape[1:], i32), pltpu.VMEM((pixels, LANES), f32),
                        pltpu.VMEM((2, bands * SIDE, RANGE), f32), pltpu.SemaphoreType.DMA((2 * bands + 7,))],
        compiler_params=params(16),
    )(tile, comp_count, *inputs)
    banded = pl.pallas_call(
        banded_kernel,
        out_shape=(r_shape, sds((SIDE, CYCLE, frames), f32)), in_specs=[SM, VM, VM], out_specs=[VM, VM],
        compiler_params=params(),
        cost_estimate=pl.CostEstimate(flops=4_000_000_000, bytes_accessed=20_000_000, transcendentals=0),
    )
    halo = swap(pay)
    x, beyond = banded(tile, band_w, r)
    trace, new_r, pay = pl.pallas_call(
        pass_kernel,
        out_shape=(sds((comps, frames), bf16), r_shape, sds((edge, frames), bf16)),
        in_specs=[SM, SM] + [VM] * 9, out_specs=[VM] * 3,
        scratch_shapes=[halo_pad, err_buf], compiler_params=params(),
    )(tile, comp_count, halo, side_w, x, beyond, r, foot, trace, den, movie)
    r = new_r
    halo = swap(pay)
    x, beyond = banded(tile, band_w, r)
    trace, part, fold = pl.pallas_call(
        functools.partial(last_kernel, block, share),
        out_shape=(sds((comps, frames), bf16), sds((packed, comps), bf16), sds((packed // 2, slots.shape[1]), bf16)),
        in_specs=[SM, SM] + [VM] * 13, out_specs=[HB, HB, VM],
        scratch_shapes=[halo_pad, err_buf, pltpu.VMEM(r_shape.shape, bf16), pltpu.VMEM((2, pixels // 2, comps), bf16),
                        pltpu.VMEM((comps, frames), bf16), pltpu.VMEM((packed, comps), bf16),
                        pltpu.SemaphoreType.DMA((3,))],
        compiler_params=params(14),
    )(tile, comp_count, halo, side_w, x, beyond, r, foot, trace, den, movie, centre_row, centre_col, radius, jnp.asarray(slots))
    received = lax.all_to_all(part.reshape(parts, block, comps), "tm", 0, 0, tiled=False)
    ffold = pl.pallas_call(
        foot_fold_kernel,
        out_shape=sds((packed, comps), f32),
        in_specs=[VM, VM], out_specs=VM, compiler_params=params(),
    )(fold, foot)
    moved = pl.pallas_call(
        functools.partial(share_kernel, share),
        out_shape=sds((parts, block, comps), bf16),
        in_specs=[SM, VM, VM], out_specs=VM, compiler_params=params(),
    )(me, received, ffold)
    every = lax.all_to_all(moved, "tm", 0, 0, tiled=False).reshape(packed, comps)
    new_foot = pl.pallas_call(
        unfold_kernel,
        out_shape=sds((pixels, comps), bf16),
        in_specs=[SM] + [VM] * 5, out_specs=HB,
        scratch_shapes=[pltpu.VMEM((pixels, comps), bf16), pltpu.SemaphoreType.DMA((bands,))],
        compiler_params=params(),
    )(comp_count, every, fold, centre_row, centre_col, radius)
    return (new_foot[None], trace[None])


def solution(mesh):
    in_specs = (
        P(("groups", "tile"), None, "tm"),
        P(("groups", "tile"), None, None),
        P(("groups", "tile"), None, None),
        P(("groups", "tile"), None, "tm"),
        P(("groups", "tile"), None),
        P(("groups", "tile"), None),
        P(("groups", "tile"), None),
        P(("groups", "tile")),
    )
    out_specs = (P(("groups", "tile"), None, None), P(("groups", "tile"), None, "tm"))
    return jax.shard_map(shards, mesh=mesh, in_specs=in_specs, out_specs=out_specs, check_vma=False)
```

```python
import functools

import jax
import jax.numpy as jnp
import numpy as np
from jax import lax
from jax.experimental import pallas as pl
from jax.experimental.pallas import tpu as pltpu
from jax.sharding import PartitionSpec as P

SIDE = 48
CYCLE = 8
PASSES = 2
RIDGE = 1.0
MAX_RADIUS = 9
BAND = 8
LANES = 128
OFFS_PAD = 64
HALF = SIDE // 2
REACH = HALF + CYCLE
COL_STEP = SIDE - REACH
RANGE = (BAND + 2 * CYCLE) * REACH

FOLD_R = 16
FOLD_C = 19
FOLD_SHIFT = 9
SLOTS = FOLD_R * FOLD_C

f32 = jnp.float32
bf16 = jnp.bfloat16
i32 = jnp.int32


def cycle_offsets():
    found = []
    for dy in range(-CYCLE, CYCLE + 1):
        for dx in range(-CYCLE, CYCLE + 1):
            if CYCLE * CYCLE <= dy * dy + dx * dx < (CYCLE + 1) * (CYCLE + 1):
                found.append((dy, dx))
    return found


def band_tables():
    offsets = cycle_offsets()
    none = len(offsets)
    own = np.full((OFFS_PAD + 8, LANES), -1, np.int32)
    own[OFFS_PAD] = SIDE
    beside = np.full((2, BAND, CYCLE, 32, CYCLE), none, np.int32)
    for o, (dy, dx) in enumerate(offsets):
        own[o] = (CYCLE + dy) * REACH + dx + CYCLE
        own[OFFS_PAD, o] = dx
        for i in range(BAND):
            for q in range(CYCLE):
                h = q + dx - CYCLE
                if 0 <= h < CYCLE:
                    beside[0, i, q, i + CYCLE + dy, h] = o
                h = q + dx + CYCLE
                if 0 <= h < CYCLE:
                    beside[1, i, q, i + CYCLE + dy, h] = o
    return own, beside.reshape(2, BAND * CYCLE, 32 * CYCLE)


def fold_rows(parts):
    share = -(-SLOTS // parts)
    block = -(-(share + 2) // 8) * 8
    assert SLOTS // 2 % share == 0 and FOLD_R == 2 * BAND
    low = np.arange(SIDE // FOLD_R)[:, None, None]
    row, col = np.arange(BAND)[:, None], np.arange(SIDE)
    slot = row * FOLD_C + (col + FOLD_SHIFT * low) % FOLD_C
    return (slot // share * block + slot % share).astype(np.int32).reshape(1, -1), share, block


def params(mib=12):
    return pltpu.CompilerParams(vmem_limit_bytes=mib * 2**20)


VM = pl.BlockSpec(memory_space=pltpu.VMEM)
HB = pl.BlockSpec(memory_space=pltpu.HBM)
SM = pl.BlockSpec(memory_space=pltpu.SMEM)


def dot(a, b):
    return jnp.dot(a, b, preferred_element_type=f32)


def disc_limit(centre_row, radius, count, row):
    gap = row - centre_row
    live = lax.broadcasted_iota(i32, centre_row.shape, 1) < count
    return jnp.where(live, radius * radius - gap * gap, -1)


def col_gap_sq(centre_col):
    gap = lax.broadcasted_iota(i32, (SIDE, centre_col.shape[1]), 0) - centre_col
    return gap * gap


def resid_band(g, tile, movie_ref, foot, trace, r_ref, pay_ref):
    band = BAND * SIDE
    d = movie_ref[pl.ds(g * band, band), :].astype(f32) - dot(foot, trace)
    d3 = d.reshape(BAND, SIDE, d.shape[1])
    r_ref[pl.ds(g * BAND, BAND)] = d3.astype(bf16)
    edge = jnp.where(tile == 0, d3[:, SIDE - CYCLE :], d3[:, :CYCLE])
    pay_ref[pl.ds(g * BAND * CYCLE, BAND * CYCLE), :] = edge.reshape(BAND * CYCLE, d.shape[1]).astype(bf16)


def build_bands(tile, w, own_ref, beside, bands_ref, sides_ref, weights, wide):
    bands = SIDE // BAND
    blocks = RANGE // LANES
    offs = w.shape[0]
    eye = lax.broadcasted_iota(i32, (offs, LANES), 0) == lax.broadcasted_iota(i32, (offs, LANES), 1)
    weights[...] = lax.dot_general(w, jnp.where(eye, 1.0, 0.0).astype(bf16), (((0,), (0,)), ((), ())),
                                   preferred_element_type=f32)
    at = own_ref[:OFFS_PAD, :1]
    from_col = lax.broadcasted_iota(i32, (SIDE, LANES), 0) + own_ref[OFFS_PAD : OFFS_PAD + 1, :]
    inside = (from_col >= 0) & (from_col < SIDE)
    per = LANES // REACH
    taken = wide.shape[2]
    target = lax.broadcasted_iota(i32, (OFFS_PAD, taken), 1)
    nothing = jnp.zeros((8, LANES), f32)
    for b in range(per):
        pick = jnp.where(target == jnp.where(at < 0, -1, at + b * REACH), 1.0, 0.0).astype(bf16)
        for k in range(BAND // per):
            rows = [weights[pl.ds((g * BAND + b + k * per) * SIDE, SIDE), :] for g in range(bands)]
            rows = [jnp.where(inside, row, 0.0)[:, :OFFS_PAD].astype(bf16) for row in rows]
            wide[k] = dot(jnp.concatenate(rows, axis=0), pick)
        for g in range(bands):
            for h in range(2):
                start = g * SIDE + h * HALF
                shift = (h * (HALF - COL_STEP) - CYCLE) % LANES
                turned = [[pltpu.roll(wide[k, start : start + HALF, v * LANES : (v + 1) * LANES], shift, 1,
                                      stride=1, stride_axis=0) for v in range(taken // LANES)]
                          for k in range(BAND // per)]
                for v in range(blocks):
                    for t in range(HALF // 8):
                        pieces = [turned[k][v - k][t * 8 : (t + 1) * 8] if 0 <= v - k < taken // LANES else nothing
                                  for k in range(BAND // per)]
                        first = t * BAND * 8 + b * len(pieces) * 8
                        bands_ref[g, h, first : first + len(pieces) * 8, v * LANES : (v + 1) * LANES] = (
                            jnp.concatenate(pieces, axis=0).astype(bf16))
    for g in range(bands):
        edges = []
        for i in range(BAND):
            base = (g * BAND + i) * SIDE
            edges.append(jnp.where(tile == 0, weights[base + SIDE - CYCLE : base + SIDE, :],
                                   weights[base : base + CYCLE, :]))
        edge = jnp.concatenate(edges, axis=0)
        for v in range(2):
            lanes = slice(v * LANES, (v + 1) * LANES)
            sides_ref[g, :, lanes] = jnp.take_along_axis(edge, beside[:, lanes], axis=1).astype(bf16)


def start_kernel(tile_ref, count_ref, movie_hbm, fp_hbm, tr_hbm, cr_hbm, cc_hbm, rad_hbm,
                 w_hbm, own_hbm, beside_hbm,
                 foot_ref, trace_ref, den_ref, r_ref, pay_ref, movie_ref, bands_ref, sides_ref,
                 fp_ref, tr_ref, cr_ref, cc_ref, rad_ref, w_ref, own_ref, beside_ref, weights, wide, sems):
    count, tile = count_ref[0], tile_ref[0]
    comps = tr_ref.shape[0]
    band = BAND * SIDE
    bands = SIDE // BAND
    small = [pltpu.make_async_copy(src, dst, sems.at[2 * bands + n]) for n, (src, dst) in enumerate(
        ((w_hbm, w_ref), (own_hbm, own_ref), (beside_hbm.at[tile], beside_ref),
         (cr_hbm, cr_ref), (cc_hbm, cc_ref), (rad_hbm, rad_ref), (tr_hbm, tr_ref)))]
    fps, movies = [], []
    for g in range(bands):
        rows = pl.ds(g * band, band)
        fps.append(pltpu.make_async_copy(fp_hbm.at[rows, :], fp_ref.at[rows, :], sems.at[g]))
        movies.append(pltpu.make_async_copy(movie_hbm.at[rows, :], movie_ref.at[rows, :], sems.at[bands + g]))
    for copy in small:
        copy.start()
    for g in range(bands):
        fps[g].start()
        movies[g].start()
    for copy in small[:3]:
        copy.wait()
    build_bands(tile, w_ref[...], own_ref, beside_ref[...], bands_ref, sides_ref, weights, wide)
    for copy in small[3:] + fps + movies:
        copy.wait()
    live = lax.broadcasted_iota(i32, (comps, 1), 0) < count
    trace = jnp.where(live, tr_ref[...].astype(f32), 0.0).astype(bf16)
    trace_ref[...] = trace
    gap_sq = col_gap_sq(cc_ref[...])
    cr, rad = cr_ref[...], rad_ref[...]
    total = jnp.zeros((8, comps), f32)
    for g in range(bands):
        for i in range(BAND):
            row = g * BAND + i
            keep = gap_sq <= disc_limit(cr, rad, count, row)
            foot = jnp.where(keep, fp_ref[pl.ds(row * SIDE, SIDE), :].astype(f32), 0.0)
            foot_ref[pl.ds(row * SIDE, SIDE), :] = foot.astype(bf16)
            total = total + jnp.sum((foot * foot).reshape(SIDE // 8, 8, comps), axis=0)
        resid_band(g, tile, movie_ref, foot_ref[pl.ds(g * band, band), :], trace, r_ref, pay_ref)
    energy = jnp.sum(total, axis=0, keepdims=True) + RIDGE
    den_ref[...] = jnp.transpose(jnp.broadcast_to(1.0 / energy, (LANES, comps)))


def banded_kernel(tile_ref, bands_ref, r_ref, x_ref, edge_ref):
    tile = tile_ref[0]
    frames = r_ref.shape[2]
    for g in range(SIDE // BAND):
        low = max(0, CYCLE - g * BAND)
        high = min(BAND + 2 * CYCLE, SIDE + CYCLE - g * BAND)
        first = g * BAND + low - CYCLE
        halves = []
        for h in range(2):
            r = r_ref[first : first + high - low, h * COL_STEP : h * COL_STEP + REACH, :]
            x = dot(bands_ref[g, h, :, low * REACH : high * REACH], r.reshape((high - low) * REACH, frames))
            per = LANES // REACH
            x = x.reshape(HALF // 8, per, BAND // per, 8, frames)
            rows = [jnp.concatenate([x[t, i % per, i // per] for t in range(HALF // 8)], axis=0) for i in range(BAND)]
            halves.append(jnp.stack(rows))
        rows = pl.ds(g * BAND, BAND)
        edge_ref[rows] = jnp.where(tile == 0, halves[1][:, HALF - CYCLE :], halves[0][:, :CYCLE])
        x_ref[rows] = jnp.concatenate(halves, axis=1).astype(bf16)


def trace_step(tile, count, halo_ref, sides_ref, x_ref, edge_ref, r_ref, foot_ref, trace_ref, den_ref,
               wide_halo, err, back_ref=None):
    frames = x_ref.shape[2]
    band, edge = BAND * SIDE, CYCLE * SIDE
    pad = CYCLE * CYCLE
    wide_halo[:pad, :] = jnp.zeros((pad, frames), bf16)
    wide_halo[pl.ds(pad, edge), :] = halo_ref[...]
    tail = wide_halo.shape[0] - pad - edge
    wide_halo[pl.ds(pad + edge, tail), :] = jnp.zeros((tail, frames), bf16)
    for g in range(SIDE // BAND):
        rows = pl.ds(g * BAND, BAND)
        reach = sides_ref.shape[2]
        side = dot(sides_ref[g], wide_halo[pl.ds(g * BAND * CYCLE, reach), :]).reshape(BAND, CYCLE, frames)
        side = (edge_ref[rows] + side).astype(bf16).astype(f32)
        x = x_ref[rows].astype(f32)
        left = jnp.where(tile == 0, x[:, :CYCLE], side)
        right = jnp.where(tile == 0, side, x[:, SIDE - CYCLE :])
        back = jnp.concatenate([left, x[:, CYCLE : SIDE - CYCLE], right], axis=1)
        if back_ref is not None:
            back_ref[rows] = back.astype(bf16)
        err[pl.ds(g * band, band), :] = (back - r_ref[rows].astype(f32)).reshape(band, frames).astype(bf16)
    grad = lax.dot_general(foot_ref[...], err[...], (((0,), (0,)), ((), ())), preferred_element_type=f32)
    comps = grad.shape[0]
    live = lax.broadcasted_iota(i32, (comps, 1), 0) < count
    moved = jnp.maximum(trace_ref[...].astype(f32) - grad * den_ref[:, :1], 0.0)
    return jnp.where(live, moved, 0.0)


def pass_kernel(tile_ref, count_ref, halo_ref, sides_ref, x_ref, edge_ref, r_ref, foot_ref, trace_ref, den_ref,
                movie_ref, new_trace_ref, new_r_ref, pay_ref, wide_halo, err):
    tile, count = tile_ref[0], count_ref[0]
    trace = trace_step(tile, count, halo_ref, sides_ref, x_ref, edge_ref, r_ref, foot_ref, trace_ref, den_ref,
                       wide_halo, err).astype(bf16)
    new_trace_ref[...] = trace
    for g in range(SIDE // BAND):
        resid_band(g, tile, movie_ref, foot_ref[pl.ds(g * BAND * SIDE, BAND * SIDE), :], trace,
                   new_r_ref, pay_ref)


def last_kernel(block, share, tile_ref, count_ref, halo_ref, sides_ref, x_ref, edge_ref, r_ref, foot_ref, trace_ref,
                den_ref, movie_ref, cr_ref, cc_ref, rad_ref, slot_ref,
                trace_hbm, part_hbm, fold_ref, wide_halo, err, back, masked, new_trace, part_ref, sems):
    tile, count = tile_ref[0], count_ref[0]
    trace = trace_step(tile, count, halo_ref, sides_ref, x_ref, edge_ref, r_ref, foot_ref, trace_ref, den_ref,
                       wide_halo, err, back).astype(bf16)
    new_trace[...] = trace
    stores = [pltpu.make_async_copy(new_trace, trace_hbm, sems.at[2])]
    stores[0].start()
    comps = trace.shape[0]
    tf = trace.astype(f32)
    energy = jnp.sum(tf * tf, axis=1, keepdims=True)
    energy = jnp.transpose(jnp.broadcast_to(energy, (comps, LANES)))[:1]
    high = energy.astype(bf16).astype(f32)
    low = energy - high
    half, taken = fold_ref.shape
    at = lax.broadcasted_iota(i32, (half, taken), 0)
    fold = jnp.where(at == slot_ref[...], 1.0, 0.0).astype(bf16)
    fold_ref[...] = fold
    inner = lax.rem(lax.broadcasted_iota(i32, (half, comps), 0), block)
    gap_sq = col_gap_sq(cc_ref[...])
    cr, rad = cr_ref[...], rad_ref[...]
    band = BAND * SIDE
    for h in range(2):
        for g in range(h, SIDE // BAND, 2):
            rows = pl.ds(g * band, band)
            prod = dot(foot_ref[rows, :], trace)
            old = back[pl.ds(g * BAND, BAND)].reshape(band, prod.shape[1]).astype(f32)
            ferr = (prod + old - movie_ref[rows, :].astype(f32)).astype(bf16)
            grad = lax.dot_general(ferr, trace, (((1,), (1,)), ((), ())), preferred_element_type=f32)
            for i in range(BAND):
                keep = gap_sq <= disc_limit(cr, rad, count, g * BAND + i)
                masked[h, pl.ds(g // 2 * band + i * SIDE, SIDE), :] = jnp.where(
                    keep, grad[i * SIDE : (i + 1) * SIDE], 0.0).astype(bf16)
        part = dot(fold, masked[h])
        part = jnp.where(inner == share, high, jnp.where(inner == share + 1, low, part))
        rows = pl.ds(h * half, half)
        part_ref[rows, :] = part.astype(bf16)
        stores.append(pltpu.make_async_copy(part_ref.at[rows, :], part_hbm.at[rows, :], sems.at[h]))
        stores[-1].start()
    for store in stores:
        store.wait()


def foot_fold_kernel(fold_ref, foot_ref, out_ref):
    half = fold_ref.shape[0]
    band = BAND * SIDE
    for h in range(2):
        foot = jnp.concatenate(
            [foot_ref[g * band : (g + 1) * band, :] for g in range(h, SIDE // BAND, 2)], axis=0)
        out_ref[h * half : (h + 1) * half, :] = dot(fold_ref[...], foot)


def share_kernel(share, me_ref, parts_ref, ffold_ref, out_ref):
    parts, block, comps = parts_ref.shape
    total = jnp.zeros((block, comps), f32)
    for j in range(parts):
        total = total + parts_ref[j].astype(f32)
    den = total[share : share + 1] + total[share + 1 : share + 2] + RIDGE
    foot = ffold_ref[pl.ds(pl.multiple_of(me_ref[0] * block, 8), block), :]
    moved = jnp.maximum(foot - total / den, 0.0).astype(bf16)
    for j in range(parts):
        out_ref[j] = moved


def unfold_kernel(count_ref, all_ref, fold_ref, cr_ref, cc_ref, rad_ref, out_hbm, buf, sems):
    count = count_ref[0]
    half = fold_ref.shape[0]
    gap_sq = col_gap_sq(cc_ref[...])
    cr, rad = cr_ref[...], rad_ref[...]
    band = BAND * SIDE
    stores = []
    for g in range(SIDE // BAND):
        h, b = g % 2, g // 2
        wide = lax.dot_general(fold_ref[:, b * band : (b + 1) * band], all_ref[h * half : (h + 1) * half, :],
                               (((0,), (0,)), ((), ())), preferred_element_type=f32)
        for i in range(BAND):
            row = g * BAND + i
            keep = gap_sq <= disc_limit(cr, rad, count, row)
            buf[pl.ds(row * SIDE, SIDE), :] = jnp.where(keep, wide[i * SIDE : (i + 1) * SIDE], 0.0).astype(bf16)
        rows = pl.ds(g * band, band)
        stores.append(pltpu.make_async_copy(buf.at[rows, :], out_hbm.at[rows, :], sems.at[g]))
        stores[-1].start()
    for store in stores:
        store.wait()


def swap(x):
    count = lax.axis_size("tile")
    return lax.ppermute(x, "tile", [(i, count - 1 - i) for i in range(count)])


def shards(movie, cycle_weights, footprints, traces, centre_row, centre_col, radius, comp_count):
    assert lax.axis_size("tile") == 2
    parts = lax.axis_size("tm")
    movie, fp, tr = movie[0], footprints[0], traces[0]
    weights = jnp.swapaxes(cycle_weights[0], 0, 1)
    pixels, frames = movie.shape
    comps = tr.shape[0]
    band = BAND * SIDE
    bands = SIDE // BAND
    edge = SIDE * CYCLE
    tile = lax.axis_index("tile").astype(i32).reshape(1)
    me = lax.axis_index("tm").astype(i32).reshape(1)
    own, beside = band_tables()
    slots, share, block = fold_rows(parts)
    packed = parts * block
    sds = jax.ShapeDtypeStruct
    halo_pad = pltpu.VMEM((edge + 3 * CYCLE * CYCLE, frames), bf16)
    err_buf = pltpu.VMEM((pixels, frames), bf16)
    one_row = pltpu.VMEM((1, comps), i32)

    r_shape = sds((SIDE, SIDE, frames), bf16)
    inputs = [pltpu.with_memory_space_constraint(v, pltpu.HBM) for v in (
        movie, fp, tr, centre_row, centre_col, radius, weights, jnp.asarray(own), jnp.asarray(beside))]
    foot, trace, den, r, pay, movie, band_w, side_w = pl.pallas_call(
        start_kernel,
        out_shape=(sds((pixels, comps), bf16), sds((comps, frames), bf16), sds((comps, LANES), f32),
                   r_shape, sds((edge, frames), bf16), sds((pixels, frames), bf16),
                   sds((bands, 2, BAND * HALF, RANGE), bf16), sds((bands, CYCLE * BAND, beside.shape[2]), bf16)),
        in_specs=[SM, SM] + [HB] * 9, out_specs=[VM] * 8,
        scratch_shapes=[pltpu.VMEM((pixels, comps), bf16), pltpu.VMEM((comps, frames), bf16),
                        one_row, one_row, one_row, pltpu.VMEM(weights.shape, bf16), pltpu.VMEM(own.shape, i32),
                        pltpu.VMEM(beside.shape[1:], i32), pltpu.VMEM((pixels, LANES), f32),
                        pltpu.VMEM((2, bands * SIDE, RANGE - LANES), f32), pltpu.SemaphoreType.DMA((2 * bands + 7,))],
        compiler_params=params(16),
    )(tile, comp_count, *inputs)
    banded = pl.pallas_call(
        banded_kernel,
        out_shape=(r_shape, sds((SIDE, CYCLE, frames), f32)), in_specs=[SM, VM, VM], out_specs=[VM, VM],
        compiler_params=params(),
        cost_estimate=pl.CostEstimate(flops=4_000_000_000, bytes_accessed=20_000_000, transcendentals=0),
    )
    halo = swap(pay)
    x, beyond = banded(tile, band_w, r)
    trace, new_r, pay = pl.pallas_call(
        pass_kernel,
        out_shape=(sds((comps, frames), bf16), r_shape, sds((edge, frames), bf16)),
        in_specs=[SM, SM] + [VM] * 9, out_specs=[VM] * 3,
        scratch_shapes=[halo_pad, err_buf], compiler_params=params(),
    )(tile, comp_count, halo, side_w, x, beyond, r, foot, trace, den, movie)
    r = new_r
    halo = swap(pay)
    x, beyond = banded(tile, band_w, r)
    trace, part, fold = pl.pallas_call(
        functools.partial(last_kernel, block, share),
        out_shape=(sds((comps, frames), bf16), sds((packed, comps), bf16), sds((packed // 2, slots.shape[1]), bf16)),
        in_specs=[SM, SM] + [VM] * 13, out_specs=[HB, HB, VM],
        scratch_shapes=[halo_pad, err_buf, pltpu.VMEM(r_shape.shape, bf16), pltpu.VMEM((2, pixels // 2, comps), bf16),
                        pltpu.VMEM((comps, frames), bf16), pltpu.VMEM((packed, comps), bf16),
                        pltpu.SemaphoreType.DMA((3,))],
        compiler_params=params(14),
    )(tile, comp_count, halo, side_w, x, beyond, r, foot, trace, den, movie, centre_row, centre_col, radius, jnp.asarray(slots))
    received = lax.all_to_all(part.reshape(parts, block, comps), "tm", 0, 0, tiled=False)
    ffold = pl.pallas_call(
        foot_fold_kernel,
        out_shape=sds((packed, comps), f32),
        in_specs=[VM, VM], out_specs=VM, compiler_params=params(),
    )(fold, foot)
    moved = pl.pallas_call(
        functools.partial(share_kernel, share),
        out_shape=sds((parts, block, comps), bf16),
        in_specs=[SM, VM, VM], out_specs=VM, compiler_params=params(),
    )(me, received, ffold)
    every = lax.all_to_all(moved, "tm", 0, 0, tiled=False).reshape(packed, comps)
    new_foot = pl.pallas_call(
        unfold_kernel,
        out_shape=sds((pixels, comps), bf16),
        in_specs=[SM] + [VM] * 5, out_specs=HB,
        scratch_shapes=[pltpu.VMEM((pixels, comps), bf16), pltpu.SemaphoreType.DMA((bands,))],
        compiler_params=params(),
    )(comp_count, every, fold, centre_row, centre_col, radius)
    return (new_foot[None], trace[None])


def solution(mesh):
    in_specs = (
        P(("groups", "tile"), None, "tm"),
        P(("groups", "tile"), None, None),
        P(("groups", "tile"), None, None),
        P(("groups", "tile"), None, "tm"),
        P(("groups", "tile"), None),
        P(("groups", "tile"), None),
        P(("groups", "tile"), None),
        P(("groups", "tile")),
    )
    out_specs = (P(("groups", "tile"), None, None), P(("groups", "tile"), None, "tm"))
    return jax.shard_map(shards, mesh=mesh, in_specs=in_specs, out_specs=out_specs, check_vma=False)
```

```python
import functools

import jax
import jax.numpy as jnp
import numpy as np
from jax import lax
from jax.experimental import pallas as pl
from jax.experimental.pallas import tpu as pltpu
from jax.sharding import PartitionSpec as P

SIDE = 48
CYCLE = 8
PASSES = 2
RIDGE = 1.0
MAX_RADIUS = 9
BAND = 8
LANES = 128
OFFS_PAD = 64
GROUP = 256
HALF = SIDE // 2
REACH = HALF + CYCLE
COL_STEP = SIDE - REACH
RANGE = (BAND + 2 * CYCLE) * REACH

FOLD_R = 16
FOLD_C = 19
FOLD_SHIFT = 9
SLOTS = FOLD_R * FOLD_C

f32 = jnp.float32
bf16 = jnp.bfloat16
i32 = jnp.int32


def cycle_offsets():
    found = []
    for dy in range(-CYCLE, CYCLE + 1):
        for dx in range(-CYCLE, CYCLE + 1):
            if CYCLE * CYCLE <= dy * dy + dx * dx < (CYCLE + 1) * (CYCLE + 1):
                found.append((dy, dx))
    return found


def band_tables():
    offsets = cycle_offsets()
    none = len(offsets)
    own = np.full((OFFS_PAD + 8, LANES), -1, np.int32)
    own[OFFS_PAD] = SIDE
    beside = np.full((2, BAND, CYCLE, 32, CYCLE), none, np.int32)
    for o, (dy, dx) in enumerate(offsets):
        own[o] = (CYCLE + dy) * REACH + dx + CYCLE
        own[OFFS_PAD, o] = dx
        for i in range(BAND):
            for q in range(CYCLE):
                h = q + dx - CYCLE
                if 0 <= h < CYCLE:
                    beside[0, i, q, i + CYCLE + dy, h] = o
                h = q + dx + CYCLE
                if 0 <= h < CYCLE:
                    beside[1, i, q, i + CYCLE + dy, h] = o
    return own, beside.reshape(2, BAND * CYCLE, 32 * CYCLE)


def fold_rows(parts):
    share = -(-SLOTS // parts)
    block = -(-(share + 2) // 8) * 8
    assert SLOTS // 2 % share == 0 and FOLD_R == 2 * BAND
    low = np.arange(SIDE // FOLD_R)[:, None, None]
    row, col = np.arange(BAND)[:, None], np.arange(SIDE)
    slot = row * FOLD_C + (col + FOLD_SHIFT * low) % FOLD_C
    return (slot // share * block + slot % share).astype(np.int32).reshape(1, -1), share, block


def params(mib=12):
    return pltpu.CompilerParams(vmem_limit_bytes=mib * 2**20)


VM = pl.BlockSpec(memory_space=pltpu.VMEM)
HB = pl.BlockSpec(memory_space=pltpu.HBM)
SM = pl.BlockSpec(memory_space=pltpu.SMEM)


def dot(a, b):
    return jnp.dot(a, b, preferred_element_type=f32)


def disc_limit(centre_row, radius, count, row):
    gap = row - centre_row
    live = lax.broadcasted_iota(i32, centre_row.shape, 1) < count
    return jnp.where(live, radius * radius - gap * gap, -1)


def col_gap_sq(centre_col):
    gap = lax.broadcasted_iota(i32, (SIDE, centre_col.shape[1]), 0) - centre_col
    return gap * gap


def resid_band(g, tile, movie_ref, foot, trace, r_ref, pay_ref):
    band = BAND * SIDE
    d = movie_ref[pl.ds(g * band, band), :].astype(f32) - dot(foot, trace)
    d3 = d.reshape(BAND, SIDE, d.shape[1])
    r_ref[pl.ds(g * BAND, BAND)] = d3.astype(bf16)
    edge = jnp.where(tile == 0, d3[:, SIDE - CYCLE :], d3[:, :CYCLE])
    pay_ref[pl.ds(g * BAND * CYCLE, BAND * CYCLE), :] = edge.reshape(BAND * CYCLE, d.shape[1]).astype(bf16)


def build_bands(tile, w, own_ref, beside, bands_ref, sides_ref, weights, wide):
    bands = SIDE // BAND
    blocks = RANGE // LANES
    offs = w.shape[0]
    eye = lax.broadcasted_iota(i32, (offs, LANES), 0) == lax.broadcasted_iota(i32, (offs, LANES), 1)
    weights[...] = lax.dot_general(w, jnp.where(eye, 1.0, 0.0).astype(bf16), (((0,), (0,)), ((), ())),
                                   preferred_element_type=f32)
    at = own_ref[:OFFS_PAD, :1]
    from_col = lax.broadcasted_iota(i32, (SIDE, LANES), 0) + own_ref[OFFS_PAD : OFFS_PAD + 1, :]
    inside = (from_col >= 0) & (from_col < SIDE)
    per = LANES // REACH
    taken = wide.shape[2]
    target = lax.broadcasted_iota(i32, (OFFS_PAD, taken), 1)
    nothing = jnp.zeros((8, LANES), f32)
    for b in range(per):
        pick = jnp.where(target == jnp.where(at < 0, -1, at + b * REACH), 1.0, 0.0).astype(bf16)
        for k in range(BAND // per):
            rows = [weights[pl.ds((g * BAND + b + k * per) * SIDE, SIDE), :] for g in range(bands)]
            rows = [jnp.where(inside, row, 0.0)[:, :OFFS_PAD].astype(bf16) for row in rows]
            wide[k] = dot(jnp.concatenate(rows, axis=0), pick)
        for g in range(bands):
            for h in range(2):
                start = g * SIDE + h * HALF
                shift = (h * (HALF - COL_STEP) - CYCLE) % LANES
                turned = [[pltpu.roll(wide[k, start : start + HALF, v * LANES : (v + 1) * LANES], shift, 1,
                                      stride=1, stride_axis=0) for v in range(taken // LANES)]
                          for k in range(BAND // per)]
                for v in range(blocks):
                    for t in range(HALF // 8):
                        pieces = [turned[k][v - k][t * 8 : (t + 1) * 8] if 0 <= v - k < taken // LANES else nothing
                                  for k in range(BAND // per)]
                        first = t * BAND * 8 + b * len(pieces) * 8
                        bands_ref[g, h, first : first + len(pieces) * 8, v * LANES : (v + 1) * LANES] = (
                            jnp.concatenate(pieces, axis=0).astype(bf16))
    for g in range(bands):
        edges = []
        for i in range(BAND):
            base = (g * BAND + i) * SIDE
            edges.append(jnp.where(tile == 0, weights[base + SIDE - CYCLE : base + SIDE, :],
                                   weights[base : base + CYCLE, :]))
        edge = jnp.concatenate(edges, axis=0)
        for v in range(2):
            lanes = slice(v * LANES, (v + 1) * LANES)
            sides_ref[g, :, lanes] = jnp.take_along_axis(edge, beside[:, lanes], axis=1).astype(bf16)


def start_kernel(tile_ref, count_ref, movie_hbm, fp_hbm, tr_hbm, cr_hbm, cc_hbm, rad_hbm,
                 w_hbm, own_hbm, beside_hbm,
                 foot_ref, trace_ref, den_ref, r_ref, pay_ref, movie_ref, bands_ref, sides_ref,
                 fp_ref, tr_ref, cr_ref, cc_ref, rad_ref, w_ref, own_ref, beside_ref, weights, wide, sems):
    count, tile = count_ref[0], tile_ref[0]
    comps = tr_ref.shape[0]
    band = BAND * SIDE
    bands = SIDE // BAND
    small = [pltpu.make_async_copy(src, dst, sems.at[n]) for n, (src, dst) in enumerate(
        ((w_hbm, w_ref), (own_hbm, own_ref), (beside_hbm.at[tile], beside_ref),
         (cr_hbm, cr_ref), (cc_hbm, cc_ref), (rad_hbm, rad_ref), (tr_hbm, tr_ref)))]
    large = [pltpu.make_async_copy(fp_hbm, fp_ref, sems.at[len(small)])]
    half = movie_ref.shape[0] // 2
    for h in range(2):
        rows = pl.ds(h * half, half)
        large.append(pltpu.make_async_copy(movie_hbm.at[rows, :], movie_ref.at[rows, :], sems.at[len(small) + 1 + h]))
    for copy in small + large:
        copy.start()
    for copy in small[:3]:
        copy.wait()
    build_bands(tile, w_ref[...], own_ref, beside_ref[...], bands_ref, sides_ref, weights, wide)
    for copy in small[3:] + large[:2]:
        copy.wait()
    live = lax.broadcasted_iota(i32, (comps, 1), 0) < count
    trace = jnp.where(live, tr_ref[...].astype(f32), 0.0).astype(bf16)
    trace_ref[...] = trace
    gap_sq = col_gap_sq(cc_ref[...])
    cr, rad = cr_ref[...], rad_ref[...]
    total = jnp.zeros((8, comps), f32)
    for g in range(bands):
        if g == bands // 2:
            large[2].wait()
        for i in range(BAND):
            row = g * BAND + i
            keep = gap_sq <= disc_limit(cr, rad, count, row)
            foot = jnp.where(keep, fp_ref[pl.ds(row * SIDE, SIDE), :].astype(f32), 0.0)
            foot_ref[pl.ds(row * SIDE, SIDE), :] = foot.astype(bf16)
            total = total + jnp.sum((foot * foot).reshape(SIDE // 8, 8, comps), axis=0)
        resid_band(g, tile, movie_ref, foot_ref[pl.ds(g * band, band), :], trace, r_ref, pay_ref)
    energy = jnp.sum(total, axis=0, keepdims=True) + RIDGE
    den_ref[...] = jnp.transpose(jnp.broadcast_to(1.0 / energy, (LANES, comps)))


def banded_kernel(tile_ref, bands_ref, r_ref, x_ref, edge_ref):
    tile = tile_ref[0]
    frames = r_ref.shape[2]
    for g in range(SIDE // BAND):
        low = max(0, CYCLE - g * BAND)
        high = min(BAND + 2 * CYCLE, SIDE + CYCLE - g * BAND)
        first = g * BAND + low - CYCLE
        halves = []
        for h in range(2):
            r = r_ref[first : first + high - low, h * COL_STEP : h * COL_STEP + REACH, :]
            x = dot(bands_ref[g, h, :, low * REACH : high * REACH], r.reshape((high - low) * REACH, frames))
            per = LANES // REACH
            x = x.reshape(HALF // 8, per, BAND // per, 8, frames)
            rows = [jnp.concatenate([x[t, i % per, i // per] for t in range(HALF // 8)], axis=0) for i in range(BAND)]
            halves.append(jnp.stack(rows))
        rows = pl.ds(g * BAND, BAND)
        edge_ref[rows] = jnp.where(tile == 0, halves[1][:, HALF - CYCLE :], halves[0][:, :CYCLE])
        x_ref[rows] = jnp.concatenate(halves, axis=1).astype(bf16)


def trace_step(tile, count, halo_ref, sides_ref, x_ref, edge_ref, r_ref, foot_ref, trace_ref, den_ref,
               wide_halo, err, back_ref=None):
    frames = x_ref.shape[2]
    band, edge = BAND * SIDE, CYCLE * SIDE
    pad = CYCLE * CYCLE
    wide_halo[:pad, :] = jnp.zeros((pad, frames), bf16)
    wide_halo[pl.ds(pad, edge), :] = halo_ref[...]
    tail = wide_halo.shape[0] - pad - edge
    wide_halo[pl.ds(pad + edge, tail), :] = jnp.zeros((tail, frames), bf16)
    for g in range(SIDE // BAND):
        rows = pl.ds(g * BAND, BAND)
        reach = sides_ref.shape[2]
        side = dot(sides_ref[g], wide_halo[pl.ds(g * BAND * CYCLE, reach), :]).reshape(BAND, CYCLE, frames)
        side = (edge_ref[rows] + side).astype(bf16).astype(f32)
        x = x_ref[rows].astype(f32)
        left = jnp.where(tile == 0, x[:, :CYCLE], side)
        right = jnp.where(tile == 0, side, x[:, SIDE - CYCLE :])
        back = jnp.concatenate([left, x[:, CYCLE : SIDE - CYCLE], right], axis=1)
        if back_ref is not None:
            back_ref[rows] = back.astype(bf16)
        err[pl.ds(g * band, band), :] = (back - r_ref[rows].astype(f32)).reshape(band, frames).astype(bf16)
    comps = trace_ref.shape[0]
    moved = []
    for low in range(0, comps, GROUP):
        some = slice(low, min(low + GROUP, comps))
        grad = lax.dot_general(foot_ref[:, some], err[...], (((0,), (0,)), ((), ())), preferred_element_type=f32)
        live = lax.broadcasted_iota(i32, (grad.shape[0], 1), 0) < count - low
        new = jnp.maximum(trace_ref[some, :].astype(f32) - grad * den_ref[some, :1], 0.0)
        moved.append(jnp.where(live, new, 0.0).astype(bf16))
    return jnp.concatenate(moved, axis=0)


def pass_kernel(tile_ref, count_ref, halo_ref, sides_ref, x_ref, edge_ref, r_ref, foot_ref, trace_ref, den_ref,
                movie_ref, new_trace_ref, new_r_ref, pay_ref, wide_halo, err):
    tile, count = tile_ref[0], count_ref[0]
    trace = trace_step(tile, count, halo_ref, sides_ref, x_ref, edge_ref, r_ref, foot_ref, trace_ref, den_ref,
                       wide_halo, err)
    new_trace_ref[...] = trace
    for g in range(SIDE // BAND):
        resid_band(g, tile, movie_ref, foot_ref[pl.ds(g * BAND * SIDE, BAND * SIDE), :], trace,
                   new_r_ref, pay_ref)


def last_kernel(block, share, tile_ref, count_ref, halo_ref, sides_ref, x_ref, edge_ref, r_ref, foot_ref, trace_ref,
                den_ref, movie_ref, cr_ref, cc_ref, rad_ref, slot_ref,
                trace_hbm, part_hbm, fold_ref, wide_halo, err, back, masked, new_trace, part_ref, sems):
    tile, count = tile_ref[0], count_ref[0]
    trace = trace_step(tile, count, halo_ref, sides_ref, x_ref, edge_ref, r_ref, foot_ref, trace_ref, den_ref,
                       wide_halo, err, back)
    new_trace[...] = trace
    stores = [pltpu.make_async_copy(new_trace, trace_hbm, sems.at[2])]
    stores[0].start()
    comps = trace.shape[0]
    tf = trace.astype(f32)
    energy = jnp.sum(tf * tf, axis=1, keepdims=True)
    energy = jnp.transpose(jnp.broadcast_to(energy, (comps, LANES)))[:1]
    high = energy.astype(bf16).astype(f32)
    low = energy - high
    half, taken = fold_ref.shape
    at = lax.broadcasted_iota(i32, (half, taken), 0)
    fold = jnp.where(at == slot_ref[...], 1.0, 0.0).astype(bf16)
    fold_ref[...] = fold
    inner = lax.rem(lax.broadcasted_iota(i32, (half, comps), 0), block)
    gap_sq = col_gap_sq(cc_ref[...])
    cr, rad = cr_ref[...], rad_ref[...]
    band = BAND * SIDE
    for h in range(2):
        for g in range(h, SIDE // BAND, 2):
            rows = pl.ds(g * band, band)
            prod = dot(foot_ref[rows, :], trace)
            old = back[pl.ds(g * BAND, BAND)].reshape(band, prod.shape[1]).astype(f32)
            ferr = (prod + old - movie_ref[rows, :].astype(f32)).astype(bf16)
            grad = lax.dot_general(ferr, trace, (((1,), (1,)), ((), ())), preferred_element_type=f32)
            for i in range(BAND):
                keep = gap_sq <= disc_limit(cr, rad, count, g * BAND + i)
                masked[h, pl.ds(g // 2 * band + i * SIDE, SIDE), :] = jnp.where(
                    keep, grad[i * SIDE : (i + 1) * SIDE], 0.0).astype(bf16)
        part = dot(fold, masked[h])
        part = jnp.where(inner == share, high, jnp.where(inner == share + 1, low, part))
        rows = pl.ds(h * half, half)
        part_ref[rows, :] = part.astype(bf16)
        stores.append(pltpu.make_async_copy(part_ref.at[rows, :], part_hbm.at[rows, :], sems.at[h]))
        stores[-1].start()
    for store in stores:
        store.wait()


def foot_fold_kernel(fold_ref, foot_ref, out_ref):
    half = fold_ref.shape[0]
    band = BAND * SIDE
    for h in range(2):
        foot = jnp.concatenate(
            [foot_ref[g * band : (g + 1) * band, :] for g in range(h, SIDE // BAND, 2)], axis=0)
        out_ref[h * half : (h + 1) * half, :] = dot(fold_ref[...], foot)


def share_kernel(share, me_ref, parts_ref, ffold_ref, out_ref):
    parts, block, comps = parts_ref.shape
    total = jnp.zeros((block, comps), f32)
    for j in range(parts):
        total = total + parts_ref[j].astype(f32)
    den = total[share : share + 1] + total[share + 1 : share + 2] + RIDGE
    foot = ffold_ref[pl.ds(pl.multiple_of(me_ref[0] * block, 8), block), :]
    moved = jnp.maximum(foot - total / den, 0.0).astype(bf16)
    for j in range(parts):
        out_ref[j] = moved


def unfold_kernel(count_ref, all_ref, fold_ref, cr_ref, cc_ref, rad_ref, out_hbm, buf, sems):
    count = count_ref[0]
    half = fold_ref.shape[0]
    gap_sq = col_gap_sq(cc_ref[...])
    cr, rad = cr_ref[...], rad_ref[...]
    band = BAND * SIDE
    stores = []
    for g in range(SIDE // BAND):
        h, b = g % 2, g // 2
        wide = lax.dot_general(fold_ref[:, b * band : (b + 1) * band], all_ref[h * half : (h + 1) * half, :],
                               (((0,), (0,)), ((), ())), preferred_element_type=f32)
        for i in range(BAND):
            row = g * BAND + i
            keep = gap_sq <= disc_limit(cr, rad, count, row)
            buf[pl.ds(row * SIDE, SIDE), :] = jnp.where(keep, wide[i * SIDE : (i + 1) * SIDE], 0.0).astype(bf16)
        rows = pl.ds(g * band, band)
        stores.append(pltpu.make_async_copy(buf.at[rows, :], out_hbm.at[rows, :], sems.at[g]))
        stores[-1].start()
    for store in stores:
        store.wait()


def swap(x):
    count = lax.axis_size("tile")
    return lax.ppermute(x, "tile", [(i, count - 1 - i) for i in range(count)])


def shards(movie, cycle_weights, footprints, traces, centre_row, centre_col, radius, comp_count):
    assert lax.axis_size("tile") == 2
    parts = lax.axis_size("tm")
    movie, fp, tr = movie[0], footprints[0], traces[0]
    weights = jnp.swapaxes(cycle_weights[0], 0, 1)
    pixels, frames = movie.shape
    comps = tr.shape[0]
    band = BAND * SIDE
    bands = SIDE // BAND
    edge = SIDE * CYCLE
    tile = lax.axis_index("tile").astype(i32).reshape(1)
    me = lax.axis_index("tm").astype(i32).reshape(1)
    own, beside = band_tables()
    slots, share, block = fold_rows(parts)
    packed = parts * block
    sds = jax.ShapeDtypeStruct
    halo_pad = pltpu.VMEM((edge + 3 * CYCLE * CYCLE, frames), bf16)
    err_buf = pltpu.VMEM((pixels, frames), bf16)
    one_row = pltpu.VMEM((1, comps), i32)

    r_shape = sds((SIDE, SIDE, frames), bf16)
    inputs = [pltpu.with_memory_space_constraint(v, pltpu.HBM) for v in (
        movie, fp, tr, centre_row, centre_col, radius, weights, jnp.asarray(own), jnp.asarray(beside))]
    foot, trace, den, r, pay, movie, band_w, side_w = pl.pallas_call(
        start_kernel,
        out_shape=(sds((pixels, comps), bf16), sds((comps, frames), bf16), sds((comps, LANES), f32),
                   r_shape, sds((edge, frames), bf16), sds((pixels, frames), bf16),
                   sds((bands, 2, BAND * HALF, RANGE), bf16), sds((bands, CYCLE * BAND, beside.shape[2]), bf16)),
        in_specs=[SM, SM] + [HB] * 9, out_specs=[VM] * 8,
        scratch_shapes=[pltpu.VMEM((pixels, comps), bf16), pltpu.VMEM((comps, frames), bf16),
                        one_row, one_row, one_row, pltpu.VMEM(weights.shape, bf16), pltpu.VMEM(own.shape, i32),
                        pltpu.VMEM(beside.shape[1:], i32), pltpu.VMEM((pixels, LANES), f32),
                        pltpu.VMEM((2, bands * SIDE, RANGE - LANES), f32), pltpu.SemaphoreType.DMA((10,))],
        compiler_params=params(16),
    )(tile, comp_count, *inputs)
    banded = pl.pallas_call(
        banded_kernel,
        out_shape=(r_shape, sds((SIDE, CYCLE, frames), f32)), in_specs=[SM, VM, VM], out_specs=[VM, VM],
        compiler_params=params(),
        cost_estimate=pl.CostEstimate(flops=4_000_000_000, bytes_accessed=20_000_000, transcendentals=0),
    )
    halo = swap(pay)
    x, beyond = banded(tile, band_w, r)
    trace, new_r, pay = pl.pallas_call(
        pass_kernel,
        out_shape=(sds((comps, frames), bf16), r_shape, sds((edge, frames), bf16)),
        in_specs=[SM, SM] + [VM] * 9, out_specs=[VM] * 3,
        scratch_shapes=[halo_pad, err_buf], compiler_params=params(),
    )(tile, comp_count, halo, side_w, x, beyond, r, foot, trace, den, movie)
    r = new_r
    halo = swap(pay)
    x, beyond = banded(tile, band_w, r)
    trace, part, fold = pl.pallas_call(
        functools.partial(last_kernel, block, share),
        out_shape=(sds((comps, frames), bf16), sds((packed, comps), bf16), sds((packed // 2, slots.shape[1]), bf16)),
        in_specs=[SM, SM] + [VM] * 13, out_specs=[HB, HB, VM],
        scratch_shapes=[halo_pad, err_buf, pltpu.VMEM(r_shape.shape, bf16), pltpu.VMEM((2, pixels // 2, comps), bf16),
                        pltpu.VMEM((comps, frames), bf16), pltpu.VMEM((packed, comps), bf16),
                        pltpu.SemaphoreType.DMA((3,))],
        compiler_params=params(14),
    )(tile, comp_count, halo, side_w, x, beyond, r, foot, trace, den, movie, centre_row, centre_col, radius, jnp.asarray(slots))
    received = lax.all_to_all(part.reshape(parts, block, comps), "tm", 0, 0, tiled=False)
    ffold = pl.pallas_call(
        foot_fold_kernel,
        out_shape=sds((packed, comps), f32),
        in_specs=[VM, VM], out_specs=VM, compiler_params=params(),
    )(fold, foot)
    moved = pl.pallas_call(
        functools.partial(share_kernel, share),
        out_shape=sds((parts, block, comps), bf16),
        in_specs=[SM, VM, VM], out_specs=VM, compiler_params=params(),
    )(me, received, ffold)
    every = lax.all_to_all(moved, "tm", 0, 0, tiled=False).reshape(packed, comps)
    new_foot = pl.pallas_call(
        unfold_kernel,
        out_shape=sds((pixels, comps), bf16),
        in_specs=[SM] + [VM] * 5, out_specs=HB,
        scratch_shapes=[pltpu.VMEM((pixels, comps), bf16), pltpu.SemaphoreType.DMA((bands,))],
        compiler_params=params(),
    )(comp_count, every, fold, centre_row, centre_col, radius)
    return (new_foot[None], trace[None])


def solution(mesh):
    in_specs = (
        P(("groups", "tile"), None, "tm"),
        P(("groups", "tile"), None, None),
        P(("groups", "tile"), None, None),
        P(("groups", "tile"), None, "tm"),
        P(("groups", "tile"), None),
        P(("groups", "tile"), None),
        P(("groups", "tile"), None),
        P(("groups", "tile")),
    )
    out_specs = (P(("groups", "tile"), None, None), P(("groups", "tile"), None, "tm"))
    return jax.shard_map(shards, mesh=mesh, in_specs=in_specs, out_specs=out_specs, check_vma=False)
```

```python
import functools

import jax
import jax.numpy as jnp
import numpy as np
from jax import lax
from jax.experimental import pallas as pl
from jax.experimental.pallas import tpu as pltpu
from jax.sharding import PartitionSpec as P

SIDE = 48
CYCLE = 8
PASSES = 2
RIDGE = 1.0
MAX_RADIUS = 9
BAND = 8
LANES = 128
OFFS_PAD = 64
TALL = 2
HALF = SIDE // 2
REACH = HALF + CYCLE
COL_STEP = SIDE - REACH
RANGE = (BAND + 2 * CYCLE) * REACH

FOLD_R = 16
FOLD_C = 19
FOLD_SHIFT = 9
SLOTS = FOLD_R * FOLD_C

f32 = jnp.float32
bf16 = jnp.bfloat16
i32 = jnp.int32


def cycle_offsets():
    found = []
    for dy in range(-CYCLE, CYCLE + 1):
        for dx in range(-CYCLE, CYCLE + 1):
            if CYCLE * CYCLE <= dy * dy + dx * dx < (CYCLE + 1) * (CYCLE + 1):
                found.append((dy, dx))
    return found


def band_tables():
    offsets = cycle_offsets()
    none = len(offsets)
    own = np.full((OFFS_PAD + 8, LANES), -1, np.int32)
    own[OFFS_PAD] = SIDE
    beside = np.full((2, TALL * BAND, CYCLE, TALL * BAND + 2 * CYCLE, CYCLE), none, np.int32)
    for o, (dy, dx) in enumerate(offsets):
        own[o] = (CYCLE + dy) * REACH + dx + CYCLE
        own[OFFS_PAD, o] = dx
        for i in range(TALL * BAND):
            for q in range(CYCLE):
                h = q + dx - CYCLE
                if 0 <= h < CYCLE:
                    beside[0, i, q, i + CYCLE + dy, h] = o
                h = q + dx + CYCLE
                if 0 <= h < CYCLE:
                    beside[1, i, q, i + CYCLE + dy, h] = o
    return own, beside.reshape(2, TALL * BAND * CYCLE, -1)


def fold_rows(parts):
    share = -(-SLOTS // parts)
    block = -(-(share + 2) // 8) * 8
    assert SLOTS // 2 % share == 0 and FOLD_R == 2 * BAND
    low = np.arange(SIDE // FOLD_R)[:, None, None]
    row, col = np.arange(BAND)[:, None], np.arange(SIDE)
    slot = row * FOLD_C + (col + FOLD_SHIFT * low) % FOLD_C
    return (slot // share * block + slot % share).astype(np.int32).reshape(1, -1), share, block


def params(mib=12):
    return pltpu.CompilerParams(vmem_limit_bytes=mib * 2**20)


VM = pl.BlockSpec(memory_space=pltpu.VMEM)
HB = pl.BlockSpec(memory_space=pltpu.HBM)
SM = pl.BlockSpec(memory_space=pltpu.SMEM)


def dot(a, b):
    return jnp.dot(a, b, preferred_element_type=f32)


def disc_limit(centre_row, radius, count, row):
    gap = row - centre_row
    live = lax.broadcasted_iota(i32, centre_row.shape, 1) < count
    return jnp.where(live, radius * radius - gap * gap, -1)


def col_gap_sq(centre_col):
    gap = lax.broadcasted_iota(i32, (SIDE, centre_col.shape[1]), 0) - centre_col
    return gap * gap


def resid_bands(g, tile, movie_ref, foot_ref, trace, r_ref, pay_ref):
    rows, wide = pl.ds(g * BAND, TALL * BAND), pl.ds(g * BAND * SIDE, TALL * BAND * SIDE)
    d = movie_ref[wide, :].astype(f32) - dot(foot_ref[wide, :], trace)
    d3 = d.reshape(TALL * BAND, SIDE, d.shape[1])
    r_ref[rows] = d3.astype(bf16)
    edge = jnp.where(tile == 0, d3[:, SIDE - CYCLE :], d3[:, :CYCLE])
    edge = edge.reshape(TALL * BAND * CYCLE, d.shape[1]).astype(bf16)
    pay_ref[pl.ds(g * BAND * CYCLE, TALL * BAND * CYCLE), :] = edge


def build_bands(tile, w, own_ref, beside, bands_ref, sides_ref, weights, wide):
    bands = SIDE // BAND
    blocks = RANGE // LANES
    offs = w.shape[0]
    eye = lax.broadcasted_iota(i32, (offs, LANES), 0) == lax.broadcasted_iota(i32, (offs, LANES), 1)
    weights[...] = lax.dot_general(w, jnp.where(eye, 1.0, 0.0).astype(bf16), (((0,), (0,)), ((), ())),
                                   preferred_element_type=f32)
    at = own_ref[:OFFS_PAD, :1]
    from_col = lax.broadcasted_iota(i32, (SIDE, LANES), 0) + own_ref[OFFS_PAD : OFFS_PAD + 1, :]
    inside = (from_col >= 0) & (from_col < SIDE)
    per = LANES // REACH
    taken = wide.shape[2]
    target = lax.broadcasted_iota(i32, (OFFS_PAD, taken), 1)
    nothing = jnp.zeros((8, LANES), f32)
    for b in range(per):
        pick = jnp.where(target == jnp.where(at < 0, -1, at + b * REACH), 1.0, 0.0).astype(bf16)
        for k in range(BAND // per):
            rows = [weights[pl.ds((g * BAND + b + k * per) * SIDE, SIDE), :] for g in range(bands)]
            rows = [jnp.where(inside, row, 0.0)[:, :OFFS_PAD].astype(bf16) for row in rows]
            wide[k] = dot(jnp.concatenate(rows, axis=0), pick)
        for g in range(bands):
            for h in range(2):
                start = g * SIDE + h * HALF
                shift = (h * (HALF - COL_STEP) - CYCLE) % LANES
                turned = [[pltpu.roll(wide[k, start : start + HALF, v * LANES : (v + 1) * LANES], shift, 1,
                                      stride=1, stride_axis=0) for v in range(taken // LANES)]
                          for k in range(BAND // per)]
                for v in range(blocks):
                    for t in range(HALF // 8):
                        pieces = [turned[k][v - k][t * 8 : (t + 1) * 8] if 0 <= v - k < taken // LANES else nothing
                                  for k in range(BAND // per)]
                        first = t * BAND * 8 + b * len(pieces) * 8
                        bands_ref[g, h, first : first + len(pieces) * 8, v * LANES : (v + 1) * LANES] = (
                            jnp.concatenate(pieces, axis=0).astype(bf16))
    for g in range(bands // TALL):
        edges = []
        for i in range(TALL * BAND):
            base = (g * TALL * BAND + i) * SIDE
            edges.append(jnp.where(tile == 0, weights[base + SIDE - CYCLE : base + SIDE, :],
                                   weights[base : base + CYCLE, :]))
        edge = jnp.concatenate(edges, axis=0)
        for v in range(beside.shape[1] // LANES):
            lanes = slice(v * LANES, (v + 1) * LANES)
            sides_ref[g, :, lanes] = jnp.take_along_axis(edge, beside[:, lanes], axis=1).astype(bf16)


def start_kernel(tile_ref, count_ref, movie_hbm, fp_hbm, tr_hbm, cr_hbm, cc_hbm, rad_hbm,
                 w_hbm, own_hbm, beside_hbm,
                 foot_ref, trace_ref, den_ref, r_ref, pay_ref, movie_ref, bands_ref, sides_ref,
                 fp_ref, tr_ref, cr_ref, cc_ref, rad_ref, w_ref, own_ref, beside_ref, weights, wide, sems):
    count, tile = count_ref[0], tile_ref[0]
    comps = tr_ref.shape[0]
    band = BAND * SIDE
    bands = SIDE // BAND
    small = [pltpu.make_async_copy(src, dst, sems.at[2 * bands + n]) for n, (src, dst) in enumerate(
        ((w_hbm, w_ref), (own_hbm, own_ref), (beside_hbm.at[tile], beside_ref),
         (cr_hbm, cr_ref), (cc_hbm, cc_ref), (rad_hbm, rad_ref), (tr_hbm, tr_ref)))]
    fps, movies = [], []
    for g in range(bands):
        rows = pl.ds(g * band, band)
        fps.append(pltpu.make_async_copy(fp_hbm.at[rows, :], fp_ref.at[rows, :], sems.at[g]))
        movies.append(pltpu.make_async_copy(movie_hbm.at[rows, :], movie_ref.at[rows, :], sems.at[bands + g]))
    for copy in small:
        copy.start()
    for g in range(bands):
        fps[g].start()
        movies[g].start()
    for copy in small[:3]:
        copy.wait()
    build_bands(tile, w_ref[...], own_ref, beside_ref[...], bands_ref, sides_ref, weights, wide)
    for copy in small[3:] + fps + movies:
        copy.wait()
    live = lax.broadcasted_iota(i32, (comps, 1), 0) < count
    trace = jnp.where(live, tr_ref[...].astype(f32), 0.0).astype(bf16)
    trace_ref[...] = trace
    gap_sq = col_gap_sq(cc_ref[...])
    cr, rad = cr_ref[...], rad_ref[...]
    total = jnp.zeros((8, comps), f32)
    for g in range(bands):
        for i in range(BAND):
            row = g * BAND + i
            keep = gap_sq <= disc_limit(cr, rad, count, row)
            foot = jnp.where(keep, fp_ref[pl.ds(row * SIDE, SIDE), :].astype(f32), 0.0)
            foot_ref[pl.ds(row * SIDE, SIDE), :] = foot.astype(bf16)
            total = total + jnp.sum((foot * foot).reshape(SIDE // 8, 8, comps), axis=0)
        if g % TALL == TALL - 1:
            resid_bands(g + 1 - TALL, tile, movie_ref, foot_ref, trace, r_ref, pay_ref)
    energy = jnp.sum(total, axis=0, keepdims=True) + RIDGE
    den_ref[...] = jnp.transpose(jnp.broadcast_to(1.0 / energy, (LANES, comps)))


def banded_kernel(tile_ref, bands_ref, r_ref, x_ref, edge_ref):
    tile = tile_ref[0]
    frames = r_ref.shape[2]
    for g in range(SIDE // BAND):
        low = max(0, CYCLE - g * BAND)
        high = min(BAND + 2 * CYCLE, SIDE + CYCLE - g * BAND)
        first = g * BAND + low - CYCLE
        halves = []
        for h in range(2):
            r = r_ref[first : first + high - low, h * COL_STEP : h * COL_STEP + REACH, :]
            x = dot(bands_ref[g, h, :, low * REACH : high * REACH], r.reshape((high - low) * REACH, frames))
            per = LANES // REACH
            x = x.reshape(HALF // 8, per, BAND // per, 8, frames)
            rows = [jnp.concatenate([x[t, i % per, i // per] for t in range(HALF // 8)], axis=0) for i in range(BAND)]
            halves.append(jnp.stack(rows))
        rows = pl.ds(g * BAND, BAND)
        edge_ref[rows] = jnp.where(tile == 0, halves[1][:, HALF - CYCLE :], halves[0][:, :CYCLE])
        x_ref[rows] = jnp.concatenate(halves, axis=1).astype(bf16)


def trace_step(tile, count, halo_ref, sides_ref, x_ref, edge_ref, r_ref, foot_ref, trace_ref, den_ref,
               wide_halo, err, back_ref=None):
    frames = x_ref.shape[2]
    edge = CYCLE * SIDE
    pad = CYCLE * CYCLE
    wide_halo[:pad, :] = jnp.zeros((pad, frames), bf16)
    wide_halo[pl.ds(pad, edge), :] = halo_ref[...]
    tail = wide_halo.shape[0] - pad - edge
    wide_halo[pl.ds(pad + edge, tail), :] = jnp.zeros((tail, frames), bf16)
    tall = TALL * BAND
    for g in range(SIDE // tall):
        rows = pl.ds(g * tall, tall)
        reach = sides_ref.shape[2]
        side = dot(sides_ref[g], wide_halo[pl.ds(g * tall * CYCLE, reach), :]).reshape(tall, CYCLE, frames)
        side = (edge_ref[rows] + side).astype(bf16).astype(f32)
        x = x_ref[rows].astype(f32)
        left = jnp.where(tile == 0, x[:, :CYCLE], side)
        right = jnp.where(tile == 0, side, x[:, SIDE - CYCLE :])
        back = jnp.concatenate([left, x[:, CYCLE : SIDE - CYCLE], right], axis=1)
        if back_ref is not None:
            back_ref[rows] = back.astype(bf16)
        wide = (back - r_ref[rows].astype(f32)).reshape(tall * SIDE, frames)
        err[pl.ds(g * tall * SIDE, tall * SIDE), :] = wide.astype(bf16)
    grad = lax.dot_general(foot_ref[...], err[...], (((0,), (0,)), ((), ())), preferred_element_type=f32)
    comps = grad.shape[0]
    live = lax.broadcasted_iota(i32, (comps, 1), 0) < count
    moved = jnp.maximum(trace_ref[...].astype(f32) - grad * den_ref[:, :1], 0.0)
    return jnp.where(live, moved, 0.0)


def pass_kernel(tile_ref, count_ref, halo_ref, sides_ref, x_ref, edge_ref, r_ref, foot_ref, trace_ref, den_ref,
                movie_ref, new_trace_ref, new_r_ref, pay_ref, wide_halo, err):
    tile, count = tile_ref[0], count_ref[0]
    trace = trace_step(tile, count, halo_ref, sides_ref, x_ref, edge_ref, r_ref, foot_ref, trace_ref, den_ref,
                       wide_halo, err).astype(bf16)
    new_trace_ref[...] = trace
    for g in range(0, SIDE // BAND, TALL):
        resid_bands(g, tile, movie_ref, foot_ref, trace, new_r_ref, pay_ref)


def last_kernel(block, share, tile_ref, count_ref, halo_ref, sides_ref, x_ref, edge_ref, r_ref, foot_ref, trace_ref,
                den_ref, movie_ref, cr_ref, cc_ref, rad_ref, slot_ref,
                trace_hbm, part_hbm, fold_ref, wide_halo, err, back, masked, new_trace, part_ref, sems):
    tile, count = tile_ref[0], count_ref[0]
    trace = trace_step(tile, count, halo_ref, sides_ref, x_ref, edge_ref, r_ref, foot_ref, trace_ref, den_ref,
                       wide_halo, err, back).astype(bf16)
    new_trace[...] = trace
    stores = [pltpu.make_async_copy(new_trace, trace_hbm, sems.at[2])]
    stores[0].start()
    comps = trace.shape[0]
    tf = trace.astype(f32)
    energy = jnp.sum(tf * tf, axis=1, keepdims=True)
    energy = jnp.transpose(jnp.broadcast_to(energy, (comps, LANES)))[:1]
    high = energy.astype(bf16).astype(f32)
    low = energy - high
    half, taken = fold_ref.shape
    at = lax.broadcasted_iota(i32, (half, taken), 0)
    fold = jnp.where(at == slot_ref[...], 1.0, 0.0).astype(bf16)
    fold_ref[...] = fold
    inner = lax.rem(lax.broadcasted_iota(i32, (half, comps), 0), block)
    gap_sq = col_gap_sq(cc_ref[...])
    cr, rad = cr_ref[...], rad_ref[...]
    band = BAND * SIDE
    for h in range(2):
        for g in range(h, SIDE // BAND, 2):
            rows = pl.ds(g * band, band)
            prod = dot(foot_ref[rows, :], trace)
            old = back[pl.ds(g * BAND, BAND)].reshape(band, prod.shape[1]).astype(f32)
            ferr = (prod + old - movie_ref[rows, :].astype(f32)).astype(bf16)
            grad = lax.dot_general(ferr, trace, (((1,), (1,)), ((), ())), preferred_element_type=f32)
            for i in range(BAND):
                keep = gap_sq <= disc_limit(cr, rad, count, g * BAND + i)
                masked[h, pl.ds(g // 2 * band + i * SIDE, SIDE), :] = jnp.where(
                    keep, grad[i * SIDE : (i + 1) * SIDE], 0.0).astype(bf16)
        part = dot(fold, masked[h])
        part = jnp.where(inner == share, high, jnp.where(inner == share + 1, low, part))
        rows = pl.ds(h * half, half)
        part_ref[rows, :] = part.astype(bf16)
        stores.append(pltpu.make_async_copy(part_ref.at[rows, :], part_hbm.at[rows, :], sems.at[h]))
        stores[-1].start()
    for store in stores:
        store.wait()


def foot_fold_kernel(fold_ref, foot_ref, out_ref):
    half = fold_ref.shape[0]
    band = BAND * SIDE
    for h in range(2):
        foot = jnp.concatenate(
            [foot_ref[g * band : (g + 1) * band, :] for g in range(h, SIDE // BAND, 2)], axis=0)
        out_ref[h * half : (h + 1) * half, :] = dot(fold_ref[...], foot)


def share_kernel(share, me_ref, parts_ref, ffold_ref, out_ref):
    parts, block, comps = parts_ref.shape
    total = jnp.zeros((block, comps), f32)
    for j in range(parts):
        total = total + parts_ref[j].astype(f32)
    den = total[share : share + 1] + total[share + 1 : share + 2] + RIDGE
    foot = ffold_ref[pl.ds(pl.multiple_of(me_ref[0] * block, 8), block), :]
    moved = jnp.maximum(foot - total / den, 0.0).astype(bf16)
    for j in range(parts):
        out_ref[j] = moved


def unfold_kernel(count_ref, all_ref, fold_ref, cr_ref, cc_ref, rad_ref, out_hbm, buf, sems):
    count = count_ref[0]
    half = fold_ref.shape[0]
    gap_sq = col_gap_sq(cc_ref[...])
    cr, rad = cr_ref[...], rad_ref[...]
    band = BAND * SIDE
    stores = []
    for g in range(SIDE // BAND):
        h, b = g % 2, g // 2
        wide = lax.dot_general(fold_ref[:, b * band : (b + 1) * band], all_ref[h * half : (h + 1) * half, :],
                               (((0,), (0,)), ((), ())), preferred_element_type=f32)
        for i in range(BAND):
            row = g * BAND + i
            keep = gap_sq <= disc_limit(cr, rad, count, row)
            buf[pl.ds(row * SIDE, SIDE), :] = jnp.where(keep, wide[i * SIDE : (i + 1) * SIDE], 0.0).astype(bf16)
        rows = pl.ds(g * band, band)
        stores.append(pltpu.make_async_copy(buf.at[rows, :], out_hbm.at[rows, :], sems.at[g]))
        stores[-1].start()
    for store in stores:
        store.wait()


def swap(x):
    count = lax.axis_size("tile")
    return lax.ppermute(x, "tile", [(i, count - 1 - i) for i in range(count)])


def shards(movie, cycle_weights, footprints, traces, centre_row, centre_col, radius, comp_count):
    assert lax.axis_size("tile") == 2
    parts = lax.axis_size("tm")
    movie, fp, tr = movie[0], footprints[0], traces[0]
    weights = jnp.swapaxes(cycle_weights[0], 0, 1)
    pixels, frames = movie.shape
    comps = tr.shape[0]
    band = BAND * SIDE
    bands = SIDE // BAND
    edge = SIDE * CYCLE
    tile = lax.axis_index("tile").astype(i32).reshape(1)
    me = lax.axis_index("tm").astype(i32).reshape(1)
    own, beside = band_tables()
    slots, share, block = fold_rows(parts)
    packed = parts * block
    sds = jax.ShapeDtypeStruct
    halo_pad = pltpu.VMEM((edge + 2 * CYCLE * CYCLE, frames), bf16)
    err_buf = pltpu.VMEM((pixels, frames), bf16)
    one_row = pltpu.VMEM((1, comps), i32)

    r_shape = sds((SIDE, SIDE, frames), bf16)
    inputs = [pltpu.with_memory_space_constraint(v, pltpu.HBM) for v in (
        movie, fp, tr, centre_row, centre_col, radius, weights, jnp.asarray(own), jnp.asarray(beside))]
    foot, trace, den, r, pay, movie, band_w, side_w = pl.pallas_call(
        start_kernel,
        out_shape=(sds((pixels, comps), bf16), sds((comps, frames), bf16), sds((comps, LANES), f32),
                   r_shape, sds((edge, frames), bf16), sds((pixels, frames), bf16),
                   sds((bands, 2, BAND * HALF, RANGE), bf16), sds((bands // TALL,) + beside.shape[1:], bf16)),
        in_specs=[SM, SM] + [HB] * 9, out_specs=[VM] * 8,
        scratch_shapes=[pltpu.VMEM((pixels, comps), bf16), pltpu.VMEM((comps, frames), bf16),
                        one_row, one_row, one_row, pltpu.VMEM(weights.shape, bf16), pltpu.VMEM(own.shape, i32),
                        pltpu.VMEM(beside.shape[1:], i32), pltpu.VMEM((pixels, LANES), f32),
                        pltpu.VMEM((2, bands * SIDE, RANGE - LANES), f32), pltpu.SemaphoreType.DMA((2 * bands + 7,))],
        compiler_params=params(16),
    )(tile, comp_count, *inputs)
    banded = pl.pallas_call(
        banded_kernel,
        out_shape=(r_shape, sds((SIDE, CYCLE, frames), f32)), in_specs=[SM, VM, VM], out_specs=[VM, VM],
        compiler_params=params(),
        cost_estimate=pl.CostEstimate(flops=4_000_000_000, bytes_accessed=20_000_000, transcendentals=0),
    )
    halo = swap(pay)
    x, beyond = banded(tile, band_w, r)
    trace, new_r, pay = pl.pallas_call(
        pass_kernel,
        out_shape=(sds((comps, frames), bf16), r_shape, sds((edge, frames), bf16)),
        in_specs=[SM, SM] + [VM] * 9, out_specs=[VM] * 3,
        scratch_shapes=[halo_pad, err_buf], compiler_params=params(),
    )(tile, comp_count, halo, side_w, x, beyond, r, foot, trace, den, movie)
    r = new_r
    halo = swap(pay)
    x, beyond = banded(tile, band_w, r)
    trace, part, fold = pl.pallas_call(
        functools.partial(last_kernel, block, share),
        out_shape=(sds((comps, frames), bf16), sds((packed, comps), bf16), sds((packed // 2, slots.shape[1]), bf16)),
        in_specs=[SM, SM] + [VM] * 13, out_specs=[HB, HB, VM],
        scratch_shapes=[halo_pad, err_buf, pltpu.VMEM(r_shape.shape, bf16), pltpu.VMEM((2, pixels // 2, comps), bf16),
                        pltpu.VMEM((comps, frames), bf16), pltpu.VMEM((packed, comps), bf16),
                        pltpu.SemaphoreType.DMA((3,))],
        compiler_params=params(14),
    )(tile, comp_count, halo, side_w, x, beyond, r, foot, trace, den, movie, centre_row, centre_col, radius, jnp.asarray(slots))
    received = lax.all_to_all(part.reshape(parts, block, comps), "tm", 0, 0, tiled=False)
    ffold = pl.pallas_call(
        foot_fold_kernel,
        out_shape=sds((packed, comps), f32),
        in_specs=[VM, VM], out_specs=VM, compiler_params=params(),
    )(fold, foot)
    moved = pl.pallas_call(
        functools.partial(share_kernel, share),
        out_shape=sds((parts, block, comps), bf16),
        in_specs=[SM, VM, VM], out_specs=VM, compiler_params=params(),
    )(me, received, ffold)
    every = lax.all_to_all(moved, "tm", 0, 0, tiled=False).reshape(packed, comps)
    new_foot = pl.pallas_call(
        unfold_kernel,
        out_shape=sds((pixels, comps), bf16),
        in_specs=[SM] + [VM] * 5, out_specs=HB,
        scratch_shapes=[pltpu.VMEM((pixels, comps), bf16), pltpu.SemaphoreType.DMA((bands,))],
        compiler_params=params(),
    )(comp_count, every, fold, centre_row, centre_col, radius)
    return (new_foot[None], trace[None])


def solution(mesh):
    in_specs = (
        P(("groups", "tile"), None, "tm"),
        P(("groups", "tile"), None, None),
        P(("groups", "tile"), None, None),
        P(("groups", "tile"), None, "tm"),
        P(("groups", "tile"), None),
        P(("groups", "tile"), None),
        P(("groups", "tile"), None),
        P(("groups", "tile")),
    )
    out_specs = (P(("groups", "tile"), None, None), P(("groups", "tile"), None, "tm"))
    return jax.shard_map(shards, mesh=mesh, in_specs=in_specs, out_specs=out_specs, check_vma=False)
```

```python
import functools

import jax
import jax.numpy as jnp
import numpy as np
from jax import lax
from jax.experimental import pallas as pl
from jax.experimental.pallas import tpu as pltpu
from jax.sharding import PartitionSpec as P

SIDE = 48
CYCLE = 8
PASSES = 2
RIDGE = 1.0
MAX_RADIUS = 9
BAND = 8
LANES = 128
OFFS_PAD = 64
TALL = 2
HALF = SIDE // 2
REACH = HALF + CYCLE
COL_STEP = SIDE - REACH
RANGE = (BAND + 2 * CYCLE) * REACH

FOLD_R = 16
FOLD_C = 19
FOLD_SHIFT = 9
SLOTS = FOLD_R * FOLD_C

f32 = jnp.float32
bf16 = jnp.bfloat16
i32 = jnp.int32


def cycle_offsets():
    found = []
    for dy in range(-CYCLE, CYCLE + 1):
        for dx in range(-CYCLE, CYCLE + 1):
            if CYCLE * CYCLE <= dy * dy + dx * dx < (CYCLE + 1) * (CYCLE + 1):
                found.append((dy, dx))
    return found


def band_tables():
    offsets = cycle_offsets()
    none = len(offsets)
    own = np.full((OFFS_PAD + 8, LANES), -1, np.int32)
    own[OFFS_PAD] = SIDE
    beside = np.full((2, TALL * BAND, CYCLE, TALL * BAND + 2 * CYCLE, CYCLE), none, np.int32)
    for o, (dy, dx) in enumerate(offsets):
        own[o] = (CYCLE + dy) * REACH + dx + CYCLE
        own[OFFS_PAD, o] = dx
        for i in range(TALL * BAND):
            for q in range(CYCLE):
                h = q + dx - CYCLE
                if 0 <= h < CYCLE:
                    beside[0, i, q, i + CYCLE + dy, h] = o
                h = q + dx + CYCLE
                if 0 <= h < CYCLE:
                    beside[1, i, q, i + CYCLE + dy, h] = o
    return own, beside.reshape(2, TALL * BAND * CYCLE, -1)


def fold_rows(parts):
    share = -(-SLOTS // parts)
    block = -(-(share + 2) // 8) * 8
    assert SLOTS // 2 % share == 0 and FOLD_R == 2 * BAND
    low = np.arange(SIDE // FOLD_R)[:, None, None]
    row, col = np.arange(BAND)[:, None], np.arange(SIDE)
    slot = row * FOLD_C + (col + FOLD_SHIFT * low) % FOLD_C
    return (slot // share * block + slot % share).astype(np.int32).reshape(1, -1), share, block


def params(mib=12):
    return pltpu.CompilerParams(vmem_limit_bytes=mib * 2**20)


VM = pl.BlockSpec(memory_space=pltpu.VMEM)
HB = pl.BlockSpec(memory_space=pltpu.HBM)
SM = pl.BlockSpec(memory_space=pltpu.SMEM)


def dot(a, b):
    return jnp.dot(a, b, preferred_element_type=f32)


def disc_limit(centre_row, radius, count, row):
    gap = row - centre_row
    live = lax.broadcasted_iota(i32, centre_row.shape, 1) < count
    return jnp.where(live, radius * radius - gap * gap, -1)


def col_gap_sq(centre_col):
    gap = lax.broadcasted_iota(i32, (SIDE, centre_col.shape[1]), 0) - centre_col
    return gap * gap


def resid_bands(g, tile, movie_ref, foot_ref, trace, r_ref, pay_ref):
    rows, wide = pl.ds(g * BAND, TALL * BAND), pl.ds(g * BAND * SIDE, TALL * BAND * SIDE)
    d = movie_ref[wide, :].astype(f32) - dot(foot_ref[wide, :], trace)
    d3 = d.reshape(TALL * BAND, SIDE, d.shape[1])
    r_ref[rows] = d3.astype(bf16)
    edge = jnp.where(tile == 0, d3[:, SIDE - CYCLE :], d3[:, :CYCLE])
    edge = edge.reshape(TALL * BAND * CYCLE, d.shape[1]).astype(bf16)
    pay_ref[pl.ds(g * BAND * CYCLE, TALL * BAND * CYCLE), :] = edge


def build_bands(tile, w, own_ref, beside, bands_ref, sides_ref, weights, wide):
    bands = SIDE // BAND
    blocks = RANGE // LANES
    offs = w.shape[0]
    eye = lax.broadcasted_iota(i32, (offs, LANES), 0) == lax.broadcasted_iota(i32, (offs, LANES), 1)
    weights[...] = lax.dot_general(w, jnp.where(eye, 1.0, 0.0).astype(bf16), (((0,), (0,)), ((), ())),
                                   preferred_element_type=f32)
    at = own_ref[:OFFS_PAD, :1]
    from_col = lax.broadcasted_iota(i32, (SIDE, LANES), 0) + own_ref[OFFS_PAD : OFFS_PAD + 1, :]
    inside = (from_col >= 0) & (from_col < SIDE)
    per = LANES // REACH
    taken = wide.shape[2]
    target = lax.broadcasted_iota(i32, (OFFS_PAD, taken), 1)
    nothing = jnp.zeros((8, LANES), f32)
    for b in range(per):
        pick = jnp.where(target == jnp.where(at < 0, -1, at + b * REACH), 1.0, 0.0).astype(bf16)
        for k in range(BAND // per):
            rows = [weights[pl.ds((g * BAND + b + k * per) * SIDE, SIDE), :] for g in range(bands)]
            rows = [jnp.where(inside, row, 0.0)[:, :OFFS_PAD].astype(bf16) for row in rows]
            wide[k] = dot(jnp.concatenate(rows, axis=0), pick)
        for g in range(bands):
            for h in range(2):
                start = g * SIDE + h * HALF
                shift = (h * (HALF - COL_STEP) - CYCLE) % LANES
                turned = [[pltpu.roll(wide[k, start : start + HALF, v * LANES : (v + 1) * LANES], shift, 1,
                                      stride=1, stride_axis=0) for v in range(taken // LANES)]
                          for k in range(BAND // per)]
                for v in range(blocks):
                    for t in range(HALF // 8):
                        pieces = [turned[k][v - k][t * 8 : (t + 1) * 8] if 0 <= v - k < taken // LANES else nothing
                                  for k in range(BAND // per)]
                        first = t * BAND * 8 + b * len(pieces) * 8
                        bands_ref[g, h, first : first + len(pieces) * 8, v * LANES : (v + 1) * LANES] = (
                            jnp.concatenate(pieces, axis=0).astype(bf16))
    for g in range(bands // TALL):
        edges = []
        for i in range(TALL * BAND):
            base = (g * TALL * BAND + i) * SIDE
            edges.append(jnp.where(tile == 0, weights[base + SIDE - CYCLE : base + SIDE, :],
                                   weights[base : base + CYCLE, :]))
        edge = jnp.concatenate(edges, axis=0)
        for v in range(beside.shape[1] // LANES):
            lanes = slice(v * LANES, (v + 1) * LANES)
            sides_ref[g, :, lanes] = jnp.take_along_axis(edge, beside[:, lanes], axis=1).astype(bf16)


def start_kernel(tile_ref, count_ref, movie_hbm, fp_hbm, tr_hbm, cr_hbm, cc_hbm, rad_hbm,
                 w_hbm, own_hbm, beside_hbm,
                 foot_ref, trace_ref, den_ref, r_ref, pay_ref, movie_ref, bands_ref, sides_ref,
                 fp_ref, tr_ref, cr_ref, cc_ref, rad_ref, w_ref, own_ref, beside_ref, weights, wide, sems):
    count, tile = count_ref[0], tile_ref[0]
    comps = tr_ref.shape[0]
    band = BAND * SIDE
    bands = SIDE // BAND
    small = [pltpu.make_async_copy(src, dst, sems.at[2 * bands + n]) for n, (src, dst) in enumerate(
        ((w_hbm, w_ref), (own_hbm, own_ref), (beside_hbm.at[tile], beside_ref),
         (cr_hbm, cr_ref), (cc_hbm, cc_ref), (rad_hbm, rad_ref), (tr_hbm, tr_ref)))]
    fps, movies = [], []
    for g in range(bands):
        rows = pl.ds(g * band, band)
        fps.append(pltpu.make_async_copy(fp_hbm.at[rows, :], fp_ref.at[rows, :], sems.at[g]))
        movies.append(pltpu.make_async_copy(movie_hbm.at[rows, :], movie_ref.at[rows, :], sems.at[bands + g]))
    for copy in small:
        copy.start()
    for g in range(bands):
        fps[g].start()
        movies[g].start()
    for copy in small[:3]:
        copy.wait()
    build_bands(tile, w_ref[...], own_ref, beside_ref[...], bands_ref, sides_ref, weights, wide)
    for copy in small[3:] + fps + movies:
        copy.wait()
    live = lax.broadcasted_iota(i32, (comps, 1), 0) < count
    trace = jnp.where(live, tr_ref[...].astype(f32), 0.0).astype(bf16)
    trace_ref[...] = trace
    gap_sq = col_gap_sq(cc_ref[...])
    cr, rad = cr_ref[...], rad_ref[...]
    total = jnp.zeros((8, comps), f32)
    for g in range(bands):
        for i in range(BAND):
            row = g * BAND + i
            keep = gap_sq <= disc_limit(cr, rad, count, row)
            foot = jnp.where(keep, fp_ref[pl.ds(row * SIDE, SIDE), :].astype(f32), 0.0)
            foot_ref[pl.ds(row * SIDE, SIDE), :] = foot.astype(bf16)
            total = total + jnp.sum((foot * foot).reshape(SIDE // 8, 8, comps), axis=0)
        if g % TALL == TALL - 1:
            resid_bands(g + 1 - TALL, tile, movie_ref, foot_ref, trace, r_ref, pay_ref)
    energy = jnp.sum(total, axis=0, keepdims=True) + RIDGE
    den_ref[...] = jnp.transpose(jnp.broadcast_to(1.0 / energy, (LANES, comps)))


def banded_kernel(tile_ref, bands_ref, r_ref, x_ref, edge_ref):
    tile = tile_ref[0]
    frames = r_ref.shape[2]
    for g in range(SIDE // BAND):
        low = max(0, CYCLE - g * BAND)
        high = min(BAND + 2 * CYCLE, SIDE + CYCLE - g * BAND)
        first = g * BAND + low - CYCLE
        halves = []
        for h in range(2):
            r = r_ref[first : first + high - low, h * COL_STEP : h * COL_STEP + REACH, :]
            x = dot(bands_ref[g, h, :, low * REACH : high * REACH], r.reshape((high - low) * REACH, frames))
            per = LANES // REACH
            x = x.reshape(HALF // 8, per, BAND // per, 8, frames)
            rows = [jnp.concatenate([x[t, i % per, i // per] for t in range(HALF // 8)], axis=0) for i in range(BAND)]
            halves.append(jnp.stack(rows))
        rows = pl.ds(g * BAND, BAND)
        edge_ref[rows] = jnp.where(tile == 0, halves[1][:, HALF - CYCLE :], halves[0][:, :CYCLE])
        x_ref[rows] = jnp.concatenate(halves, axis=1).astype(bf16)


def trace_step(tile, count, halo_ref, sides_ref, x_ref, edge_ref, r_ref, foot_ref, trace_ref, den_ref,
               wide_halo, err, back_ref=None):
    frames = x_ref.shape[2]
    edge = CYCLE * SIDE
    pad = CYCLE * CYCLE
    wide_halo[:pad, :] = jnp.zeros((pad, frames), bf16)
    wide_halo[pl.ds(pad, edge), :] = halo_ref[...]
    tail = wide_halo.shape[0] - pad - edge
    wide_halo[pl.ds(pad + edge, tail), :] = jnp.zeros((tail, frames), bf16)
    tall = TALL * BAND
    for g in range(SIDE // tall):
        rows = pl.ds(g * tall, tall)
        reach = sides_ref.shape[2]
        side = dot(sides_ref[g], wide_halo[pl.ds(g * tall * CYCLE, reach), :]).reshape(tall, CYCLE, frames)
        side = (edge_ref[rows] + side).astype(bf16).astype(f32)
        x = x_ref[rows].astype(f32)
        left = jnp.where(tile == 0, x[:, :CYCLE], side)
        right = jnp.where(tile == 0, side, x[:, SIDE - CYCLE :])
        back = jnp.concatenate([left, x[:, CYCLE : SIDE - CYCLE], right], axis=1)
        if back_ref is not None:
            back_ref[rows] = back.astype(bf16)
        wide = (back - r_ref[rows].astype(f32)).reshape(tall * SIDE, frames)
        err[pl.ds(g * tall * SIDE, tall * SIDE), :] = wide.astype(bf16)
    grad = lax.dot_general(foot_ref[...], err[...], (((0,), (0,)), ((), ())), preferred_element_type=f32)
    comps = grad.shape[0]
    live = lax.broadcasted_iota(i32, (comps, 1), 0) < count
    moved = jnp.maximum(trace_ref[...].astype(f32) - grad * den_ref[:, :1], 0.0)
    return jnp.where(live, moved, 0.0)


def pass_kernel(tile_ref, count_ref, halo_ref, sides_ref, x_ref, edge_ref, r_ref, foot_ref, trace_ref, den_ref,
                movie_ref, new_trace_ref, new_r_ref, pay_ref, wide_halo, err):
    tile, count = tile_ref[0], count_ref[0]
    trace = trace_step(tile, count, halo_ref, sides_ref, x_ref, edge_ref, r_ref, foot_ref, trace_ref, den_ref,
                       wide_halo, err).astype(bf16)
    new_trace_ref[...] = trace
    for g in range(0, SIDE // BAND, TALL):
        resid_bands(g, tile, movie_ref, foot_ref, trace, new_r_ref, pay_ref)


def last_kernel(block, share, tile_ref, count_ref, halo_ref, sides_ref, x_ref, edge_ref, r_ref, foot_ref, trace_ref,
                den_ref, movie_ref, cr_ref, cc_ref, rad_ref, slot_ref,
                trace_hbm, part_hbm, fold_ref, wide_halo, err, back, masked, new_trace, part_ref, sems):
    tile, count = tile_ref[0], count_ref[0]
    trace = trace_step(tile, count, halo_ref, sides_ref, x_ref, edge_ref, r_ref, foot_ref, trace_ref, den_ref,
                       wide_halo, err, back).astype(bf16)
    new_trace[...] = trace
    stores = [pltpu.make_async_copy(new_trace, trace_hbm, sems.at[2])]
    stores[0].start()
    comps = trace.shape[0]
    tf = trace.astype(f32)
    energy = jnp.sum(tf * tf, axis=1, keepdims=True)
    energy = jnp.transpose(jnp.broadcast_to(energy, (comps, LANES)))[:1]
    high = energy.astype(bf16).astype(f32)
    low = energy - high
    half, taken = fold_ref.shape
    at = lax.broadcasted_iota(i32, (half, taken), 0)
    fold = jnp.where(at == slot_ref[...], 1.0, 0.0).astype(bf16)
    fold_ref[...] = fold
    inner = lax.rem(lax.broadcasted_iota(i32, (half, comps), 0), block)
    gap_sq = col_gap_sq(cc_ref[...])
    cr, rad = cr_ref[...], rad_ref[...]
    band = BAND * SIDE
    for h in range(2):
        for g in range(h, SIDE // BAND, 2):
            rows = pl.ds(g * band, band)
            prod = dot(foot_ref[rows, :], trace)
            old = back[pl.ds(g * BAND, BAND)].reshape(band, prod.shape[1]).astype(f32)
            ferr = (prod + old - movie_ref[rows, :].astype(f32)).astype(bf16)
            grad = lax.dot_general(ferr, trace, (((1,), (1,)), ((), ())), preferred_element_type=f32)
            for i in range(BAND):
                keep = gap_sq <= disc_limit(cr, rad, count, g * BAND + i)
                masked[h, pl.ds(g // 2 * band + i * SIDE, SIDE), :] = jnp.where(
                    keep, grad[i * SIDE : (i + 1) * SIDE], 0.0).astype(bf16)
        part = dot(fold, masked[h])
        part = jnp.where(inner == share, high, jnp.where(inner == share + 1, low, part))
        rows = pl.ds(h * half, half)
        part_ref[rows, :] = part.astype(bf16)
        stores.append(pltpu.make_async_copy(part_ref.at[rows, :], part_hbm.at[rows, :], sems.at[h]))
        stores[-1].start()
    for store in stores:
        store.wait()


def foot_fold_kernel(fold_ref, foot_ref, out_ref):
    half = fold_ref.shape[0]
    band = BAND * SIDE
    for h in range(2):
        foot = jnp.concatenate(
            [foot_ref[g * band : (g + 1) * band, :] for g in range(h, SIDE // BAND, 2)], axis=0)
        out_ref[h * half : (h + 1) * half, :] = dot(fold_ref[...], foot)


def share_kernel(share, me_ref, parts_ref, ffold_ref, out_ref):
    parts, block, comps = parts_ref.shape
    total = jnp.zeros((block, comps), f32)
    for j in range(parts):
        total = total + parts_ref[j].astype(f32)
    den = total[share : share + 1] + total[share + 1 : share + 2] + RIDGE
    foot = ffold_ref[pl.ds(pl.multiple_of(me_ref[0] * block, 8), block), :]
    moved = jnp.maximum(foot - total / den, 0.0).astype(bf16)
    out_ref[...] = moved


def pair_kernel(me_ref, own_ref, other_ref, out_ref):
    odd = lax.rem(me_ref[0], 2) == 1
    block = own_ref.shape[0]
    own, other = own_ref[...].astype(f32), other_ref[...].astype(f32)
    both = jnp.concatenate([jnp.where(odd, other, own), jnp.where(odd, own, other)], axis=0)
    out_ref[...] = both.astype(bf16)


def unfold_kernel(steps, far, me_ref, count_ref, fold_ref, cr_ref, cc_ref, rad_ref, *refs):
    pairs, out_hbm, every, buf, sems = refs[: len(steps)], refs[-4], refs[-3], refs[-2], refs[-1]
    count, me = count_ref[0], me_ref[0]
    half = fold_ref.shape[0]
    pair = pairs[0].shape[0]
    in_half = half // pair
    mine = me // 2
    h = mine // in_half
    if far:
        h = 1 - h
    for step, ref in zip(steps, pairs):
        place = lax.rem(jnp.bitwise_xor(mine, step // 2), in_half)
        every[pl.ds(pl.multiple_of(place * pair, 16), pair), :] = ref[...]
    gap_sq = col_gap_sq(cc_ref[...])
    cr, rad = cr_ref[...], rad_ref[...]
    band = BAND * SIDE
    stores = []
    for b in range(SIDE // BAND // 2):
        wide = lax.dot_general(fold_ref[:, b * band : (b + 1) * band], every[...],
                               (((0,), (0,)), ((), ())), preferred_element_type=f32)
        for i in range(BAND):
            keep = gap_sq <= disc_limit(cr, rad, count, (2 * b + h) * BAND + i)
            buf[pl.ds(b * band + i * SIDE, SIDE), :] = jnp.where(keep, wide[i * SIDE : (i + 1) * SIDE], 0.0).astype(bf16)
        rows = pl.ds(pl.multiple_of((2 * b + h) * band, band), band)
        stores.append(pltpu.make_async_copy(buf.at[pl.ds(b * band, band), :], out_hbm.at[rows, :], sems.at[b]))
        stores[-1].start()
    for store in stores:
        store.wait()


def swap(x):
    count = lax.axis_size("tile")
    return lax.ppermute(x, "tile", [(i, count - 1 - i) for i in range(count)])


def from_xor(x, step):
    return lax.ppermute(x, "tm", [(i, i ^ step) for i in range(lax.axis_size("tm"))])


def shards(movie, cycle_weights, footprints, traces, centre_row, centre_col, radius, comp_count):
    assert lax.axis_size("tile") == 2
    parts = lax.axis_size("tm")
    movie, fp, tr = movie[0], footprints[0], traces[0]
    weights = jnp.swapaxes(cycle_weights[0], 0, 1)
    pixels, frames = movie.shape
    comps = tr.shape[0]
    band = BAND * SIDE
    bands = SIDE // BAND
    edge = SIDE * CYCLE
    tile = lax.axis_index("tile").astype(i32).reshape(1)
    me = lax.axis_index("tm").astype(i32).reshape(1)
    own, beside = band_tables()
    slots, share, block = fold_rows(parts)
    packed = parts * block
    sds = jax.ShapeDtypeStruct
    halo_pad = pltpu.VMEM((edge + 2 * CYCLE * CYCLE, frames), bf16)
    err_buf = pltpu.VMEM((pixels, frames), bf16)
    one_row = pltpu.VMEM((1, comps), i32)

    r_shape = sds((SIDE, SIDE, frames), bf16)
    inputs = [pltpu.with_memory_space_constraint(v, pltpu.HBM) for v in (
        movie, fp, tr, centre_row, centre_col, radius, weights, jnp.asarray(own), jnp.asarray(beside))]
    foot, trace, den, r, pay, movie, band_w, side_w = pl.pallas_call(
        start_kernel,
        out_shape=(sds((pixels, comps), bf16), sds((comps, frames), bf16), sds((comps, LANES), f32),
                   r_shape, sds((edge, frames), bf16), sds((pixels, frames), bf16),
                   sds((bands, 2, BAND * HALF, RANGE), bf16), sds((bands // TALL,) + beside.shape[1:], bf16)),
        in_specs=[SM, SM] + [HB] * 9, out_specs=[VM] * 8,
        scratch_shapes=[pltpu.VMEM((pixels, comps), bf16), pltpu.VMEM((comps, frames), bf16),
                        one_row, one_row, one_row, pltpu.VMEM(weights.shape, bf16), pltpu.VMEM(own.shape, i32),
                        pltpu.VMEM(beside.shape[1:], i32), pltpu.VMEM((pixels, LANES), f32),
                        pltpu.VMEM((2, bands * SIDE, RANGE - LANES), f32), pltpu.SemaphoreType.DMA((2 * bands + 7,))],
        compiler_params=params(16),
    )(tile, comp_count, *inputs)
    banded = pl.pallas_call(
        banded_kernel,
        out_shape=(r_shape, sds((SIDE, CYCLE, frames), f32)), in_specs=[SM, VM, VM], out_specs=[VM, VM],
        compiler_params=params(),
        cost_estimate=pl.CostEstimate(flops=4_000_000_000, bytes_accessed=20_000_000, transcendentals=0),
    )
    halo = swap(pay)
    x, beyond = banded(tile, band_w, r)
    trace, new_r, pay = pl.pallas_call(
        pass_kernel,
        out_shape=(sds((comps, frames), bf16), r_shape, sds((edge, frames), bf16)),
        in_specs=[SM, SM] + [VM] * 9, out_specs=[VM] * 3,
        scratch_shapes=[halo_pad, err_buf], compiler_params=params(),
    )(tile, comp_count, halo, side_w, x, beyond, r, foot, trace, den, movie)
    r = new_r
    halo = swap(pay)
    x, beyond = banded(tile, band_w, r)
    trace, part, fold = pl.pallas_call(
        functools.partial(last_kernel, block, share),
        out_shape=(sds((comps, frames), bf16), sds((packed, comps), bf16), sds((packed // 2, slots.shape[1]), bf16)),
        in_specs=[SM, SM] + [VM] * 13, out_specs=[HB, HB, VM],
        scratch_shapes=[halo_pad, err_buf, pltpu.VMEM(r_shape.shape, bf16), pltpu.VMEM((2, pixels // 2, comps), bf16),
                        pltpu.VMEM((comps, frames), bf16), pltpu.VMEM((packed, comps), bf16),
                        pltpu.SemaphoreType.DMA((3,))],
        compiler_params=params(14),
    )(tile, comp_count, halo, side_w, x, beyond, r, foot, trace, den, movie, centre_row, centre_col, radius, jnp.asarray(slots))
    received = lax.all_to_all(part.reshape(parts, block, comps), "tm", 0, 0, tiled=False)
    ffold = pl.pallas_call(
        foot_fold_kernel,
        out_shape=sds((packed, comps), f32),
        in_specs=[VM, VM], out_specs=VM, compiler_params=params(),
    )(fold, foot)
    moved = pl.pallas_call(
        functools.partial(share_kernel, share),
        out_shape=sds((block, comps), bf16),
        in_specs=[SM, VM, VM], out_specs=VM, compiler_params=params(),
    )(me, received, ffold)
    pair = pl.pallas_call(
        pair_kernel,
        out_shape=sds((2 * block, comps), bf16),
        in_specs=[SM, VM, VM], out_specs=VM, compiler_params=params(),
    )(me, moved, from_xor(moved, 1))
    pairs = [pair] + [from_xor(pair, step) for step in range(2, parts, 2)]
    new_foot = None
    for far in range(2):
        steps = list(range(far * parts // 2, (far + 1) * parts // 2, 2))
        args = [me, comp_count, fold, centre_row, centre_col, radius] + [pairs[step // 2] for step in steps]
        specs = [SM, SM] + [VM] * (len(args) - 2)
        if far:
            args, specs = args + [new_foot], specs + [HB]
        new_foot = pl.pallas_call(
            functools.partial(unfold_kernel, steps, far),
            out_shape=sds((pixels, comps), bf16),
            in_specs=specs, out_specs=HB,
            scratch_shapes=[pltpu.VMEM((packed // 2, comps), bf16), pltpu.VMEM((pixels // 2, comps), bf16),
                            pltpu.SemaphoreType.DMA((bands // 2,))],
            input_output_aliases={len(args) - 1: 0} if far else {},
            compiler_params=params(),
            cost_estimate=pl.CostEstimate(flops=1_000_000_000, bytes_accessed=1_000_000, transcendentals=0),
        )(*args)
    return (new_foot[None], trace[None])


def solution(mesh):
    in_specs = (
        P(("groups", "tile"), None, "tm"),
        P(("groups", "tile"), None, None),
        P(("groups", "tile"), None, None),
        P(("groups", "tile"), None, "tm"),
        P(("groups", "tile"), None),
        P(("groups", "tile"), None),
        P(("groups", "tile"), None),
        P(("groups", "tile")),
    )
    out_specs = (P(("groups", "tile"), None, None), P(("groups", "tile"), None, "tm"))
    return jax.shard_map(shards, mesh=mesh, in_specs=in_specs, out_specs=out_specs, check_vma=False)
```

```python
import functools

import jax
import jax.numpy as jnp
import numpy as np
from jax import lax
from jax.experimental import pallas as pl
from jax.experimental.pallas import tpu as pltpu
from jax.sharding import PartitionSpec as P

SIDE = 48
CYCLE = 8
PASSES = 2
RIDGE = 1.0
MAX_RADIUS = 9
BAND = 8
LANES = 128
OFFS_PAD = 64
GROUP = 256
TALL = 2
HALF = SIDE // 2
REACH = HALF + CYCLE
COL_STEP = SIDE - REACH
RANGE = (BAND + 2 * CYCLE) * REACH

FOLD_R = 16
FOLD_C = 19
FOLD_SHIFT = 9
SLOTS = FOLD_R * FOLD_C

f32 = jnp.float32
bf16 = jnp.bfloat16
i32 = jnp.int32


def cycle_offsets():
    found = []
    for dy in range(-CYCLE, CYCLE + 1):
        for dx in range(-CYCLE, CYCLE + 1):
            if CYCLE * CYCLE <= dy * dy + dx * dx < (CYCLE + 1) * (CYCLE + 1):
                found.append((dy, dx))
    return found


def band_tables():
    offsets = cycle_offsets()
    none = len(offsets)
    own = np.full((OFFS_PAD + 8, LANES), -1, np.int32)
    own[OFFS_PAD] = SIDE
    beside = np.full((2, TALL * BAND, CYCLE, TALL * BAND + 2 * CYCLE, CYCLE), none, np.int32)
    for o, (dy, dx) in enumerate(offsets):
        own[o] = (CYCLE + dy) * REACH + dx + CYCLE
        own[OFFS_PAD, o] = dx
        for i in range(TALL * BAND):
            for q in range(CYCLE):
                h = q + dx - CYCLE
                if 0 <= h < CYCLE:
                    beside[0, i, q, i + CYCLE + dy, h] = o
                h = q + dx + CYCLE
                if 0 <= h < CYCLE:
                    beside[1, i, q, i + CYCLE + dy, h] = o
    return own, beside.reshape(2, TALL * BAND * CYCLE, -1)


def fold_rows(parts):
    share = -(-SLOTS // parts)
    block = -(-(share + 2) // 8) * 8
    assert SLOTS // 2 % share == 0 and FOLD_R == 2 * BAND
    low = np.arange(SIDE // FOLD_R)[:, None, None]
    row, col = np.arange(BAND)[:, None], np.arange(SIDE)
    slot = row * FOLD_C + (col + FOLD_SHIFT * low) % FOLD_C
    return (slot // share * block + slot % share).astype(np.int32).reshape(1, -1), share, block


def params(mib=12):
    return pltpu.CompilerParams(vmem_limit_bytes=mib * 2**20)


VM = pl.BlockSpec(memory_space=pltpu.VMEM)
HB = pl.BlockSpec(memory_space=pltpu.HBM)
SM = pl.BlockSpec(memory_space=pltpu.SMEM)


def dot(a, b):
    return jnp.dot(a, b, preferred_element_type=f32)


def disc_limit(centre_row, radius, count, row):
    gap = row - centre_row
    live = lax.broadcasted_iota(i32, centre_row.shape, 1) < count
    return jnp.where(live, radius * radius - gap * gap, -1)


def col_gap_sq(centre_col):
    gap = lax.broadcasted_iota(i32, (SIDE, centre_col.shape[1]), 0) - centre_col
    return gap * gap


def by_live(count, comps, body):
    few = min(GROUP, comps)
    pl.when(count <= few)(functools.partial(body, few))
    if few < comps:
        pl.when(count > few)(functools.partial(body, comps))


def resid_bands(g, tile, movie_ref, foot_ref, trace, r_ref, pay_ref):
    rows, wide = pl.ds(g * BAND, TALL * BAND), pl.ds(g * BAND * SIDE, TALL * BAND * SIDE)
    d = movie_ref[wide, :].astype(f32) - dot(foot_ref[wide, : trace.shape[0]], trace)
    d3 = d.reshape(TALL * BAND, SIDE, d.shape[1])
    r_ref[rows] = d3.astype(bf16)
    edge = jnp.where(tile == 0, d3[:, SIDE - CYCLE :], d3[:, :CYCLE])
    edge = edge.reshape(TALL * BAND * CYCLE, d.shape[1]).astype(bf16)
    pay_ref[pl.ds(g * BAND * CYCLE, TALL * BAND * CYCLE), :] = edge


def build_bands(tile, w, own_ref, beside, bands_ref, sides_ref, weights, wide):
    bands = SIDE // BAND
    blocks = RANGE // LANES
    offs = w.shape[0]
    eye = lax.broadcasted_iota(i32, (offs, LANES), 0) == lax.broadcasted_iota(i32, (offs, LANES), 1)
    weights[...] = lax.dot_general(w, jnp.where(eye, 1.0, 0.0).astype(bf16), (((0,), (0,)), ((), ())),
                                   preferred_element_type=f32)
    at = own_ref[:OFFS_PAD, :1]
    from_col = lax.broadcasted_iota(i32, (SIDE, LANES), 0) + own_ref[OFFS_PAD : OFFS_PAD + 1, :]
    inside = (from_col >= 0) & (from_col < SIDE)
    per = LANES // REACH
    taken = wide.shape[2]
    target = lax.broadcasted_iota(i32, (OFFS_PAD, taken), 1)
    nothing = jnp.zeros((8, LANES), f32)
    for b in range(per):
        pick = jnp.where(target == jnp.where(at < 0, -1, at + b * REACH), 1.0, 0.0).astype(bf16)
        for k in range(BAND // per):
            rows = [weights[pl.ds((g * BAND + b + k * per) * SIDE, SIDE), :] for g in range(bands)]
            rows = [jnp.where(inside, row, 0.0)[:, :OFFS_PAD].astype(bf16) for row in rows]
            wide[k] = dot(jnp.concatenate(rows, axis=0), pick)
        for g in range(bands):
            for h in range(2):
                start = g * SIDE + h * HALF
                shift = (h * (HALF - COL_STEP) - CYCLE) % LANES
                turned = [[pltpu.roll(wide[k, start : start + HALF, v * LANES : (v + 1) * LANES], shift, 1,
                                      stride=1, stride_axis=0) for v in range(taken // LANES)]
                          for k in range(BAND // per)]
                for v in range(blocks):
                    for t in range(HALF // 8):
                        pieces = [turned[k][v - k][t * 8 : (t + 1) * 8] if 0 <= v - k < taken // LANES else nothing
                                  for k in range(BAND // per)]
                        first = t * BAND * 8 + b * len(pieces) * 8
                        bands_ref[g, h, first : first + len(pieces) * 8, v * LANES : (v + 1) * LANES] = (
                            jnp.concatenate(pieces, axis=0).astype(bf16))
    for g in range(bands // TALL):
        edges = []
        for i in range(TALL * BAND):
            base = (g * TALL * BAND + i) * SIDE
            edges.append(jnp.where(tile == 0, weights[base + SIDE - CYCLE : base + SIDE, :],
                                   weights[base : base + CYCLE, :]))
        edge = jnp.concatenate(edges, axis=0)
        for v in range(beside.shape[1] // LANES):
            lanes = slice(v * LANES, (v + 1) * LANES)
            sides_ref[g, :, lanes] = jnp.take_along_axis(edge, beside[:, lanes], axis=1).astype(bf16)


def start_kernel(tile_ref, count_ref, movie_hbm, fp_hbm, tr_hbm, cr_hbm, cc_hbm, rad_hbm,
                 w_hbm, own_hbm, beside_hbm,
                 foot_ref, trace_ref, den_ref, r_ref, pay_ref, movie_ref, bands_ref, sides_ref,
                 fp_ref, tr_ref, cr_ref, cc_ref, rad_ref, w_ref, own_ref, beside_ref, weights, wide, sems):
    count, tile = count_ref[0], tile_ref[0]
    comps = tr_ref.shape[0]
    band = BAND * SIDE
    bands = SIDE // BAND
    small = [pltpu.make_async_copy(src, dst, sems.at[2 * bands + n]) for n, (src, dst) in enumerate(
        ((w_hbm, w_ref), (own_hbm, own_ref), (beside_hbm.at[tile], beside_ref),
         (cr_hbm, cr_ref), (cc_hbm, cc_ref), (rad_hbm, rad_ref), (tr_hbm, tr_ref)))]
    fps, movies = [], []
    for g in range(bands):
        rows = pl.ds(g * band, band)
        fps.append(pltpu.make_async_copy(fp_hbm.at[rows, :], fp_ref.at[rows, :], sems.at[g]))
        movies.append(pltpu.make_async_copy(movie_hbm.at[rows, :], movie_ref.at[rows, :], sems.at[bands + g]))
    for copy in small:
        copy.start()
    for g in range(bands):
        fps[g].start()
        movies[g].start()
    for copy in small[:3]:
        copy.wait()
    build_bands(tile, w_ref[...], own_ref, beside_ref[...], bands_ref, sides_ref, weights, wide)
    for copy in small[3:] + fps + movies:
        copy.wait()

    def rest(n):
        live = lax.broadcasted_iota(i32, (n, 1), 0) < count
        trace = jnp.where(live, tr_ref[:n, :].astype(f32), 0.0).astype(bf16)
        trace_ref[:n, :] = trace
        gap_sq = col_gap_sq(cc_ref[:, :n])
        cr, rad = cr_ref[:, :n], rad_ref[:, :n]
        total = jnp.zeros((8, n), f32)
        for g in range(bands):
            for i in range(BAND):
                row = g * BAND + i
                keep = gap_sq <= disc_limit(cr, rad, count, row)
                foot = jnp.where(keep, fp_ref[pl.ds(row * SIDE, SIDE), :n].astype(f32), 0.0)
                foot_ref[pl.ds(row * SIDE, SIDE), :n] = foot.astype(bf16)
                total = total + jnp.sum((foot * foot).reshape(SIDE // 8, 8, n), axis=0)
            if g % TALL == TALL - 1:
                resid_bands(g + 1 - TALL, tile, movie_ref, foot_ref, trace, r_ref, pay_ref)
        energy = jnp.sum(total, axis=0, keepdims=True) + RIDGE
        den_ref[:n, :] = jnp.transpose(jnp.broadcast_to(1.0 / energy, (LANES, n)))
        if n < comps:
            trace_ref[n:, :] = jnp.zeros((comps - n, trace.shape[1]), bf16)
            foot_ref[:, n:] = jnp.zeros((foot_ref.shape[0], comps - n), bf16)

    by_live(count, comps, rest)


def banded_kernel(tile_ref, bands_ref, r_ref, x_ref, edge_ref):
    tile = tile_ref[0]
    frames = r_ref.shape[2]
    for g in range(SIDE // BAND):
        low = max(0, CYCLE - g * BAND)
        high = min(BAND + 2 * CYCLE, SIDE + CYCLE - g * BAND)
        first = g * BAND + low - CYCLE
        halves = []
        for h in range(2):
            r = r_ref[first : first + high - low, h * COL_STEP : h * COL_STEP + REACH, :]
            x = dot(bands_ref[g, h, :, low * REACH : high * REACH], r.reshape((high - low) * REACH, frames))
            per = LANES // REACH
            x = x.reshape(HALF // 8, per, BAND // per, 8, frames)
            rows = [jnp.concatenate([x[t, i % per, i // per] for t in range(HALF // 8)], axis=0) for i in range(BAND)]
            halves.append(jnp.stack(rows))
        rows = pl.ds(g * BAND, BAND)
        edge_ref[rows] = jnp.where(tile == 0, halves[1][:, HALF - CYCLE :], halves[0][:, :CYCLE])
        x_ref[rows] = jnp.concatenate(halves, axis=1).astype(bf16)


def trace_step(n, tile, count, halo_ref, sides_ref, x_ref, edge_ref, r_ref, foot_ref, trace_ref, den_ref,
               wide_halo, err, back_ref=None):
    frames = x_ref.shape[2]
    edge = CYCLE * SIDE
    pad = CYCLE * CYCLE
    wide_halo[:pad, :] = jnp.zeros((pad, frames), bf16)
    wide_halo[pl.ds(pad, edge), :] = halo_ref[...]
    tail = wide_halo.shape[0] - pad - edge
    wide_halo[pl.ds(pad + edge, tail), :] = jnp.zeros((tail, frames), bf16)
    tall = TALL * BAND
    for g in range(SIDE // tall):
        rows = pl.ds(g * tall, tall)
        reach = sides_ref.shape[2]
        side = dot(sides_ref[g], wide_halo[pl.ds(g * tall * CYCLE, reach), :]).reshape(tall, CYCLE, frames)
        side = (edge_ref[rows] + side).astype(bf16).astype(f32)
        x = x_ref[rows].astype(f32)
        left = jnp.where(tile == 0, x[:, :CYCLE], side)
        right = jnp.where(tile == 0, side, x[:, SIDE - CYCLE :])
        back = jnp.concatenate([left, x[:, CYCLE : SIDE - CYCLE], right], axis=1)
        if back_ref is not None:
            back_ref[rows] = back.astype(bf16)
        wide = (back - r_ref[rows].astype(f32)).reshape(tall * SIDE, frames)
        err[pl.ds(g * tall * SIDE, tall * SIDE), :] = wide.astype(bf16)
    grad = lax.dot_general(foot_ref[:, :n], err[...], (((0,), (0,)), ((), ())), preferred_element_type=f32)
    live = lax.broadcasted_iota(i32, (n, 1), 0) < count
    moved = jnp.maximum(trace_ref[:n, :].astype(f32) - grad * den_ref[:n, :1], 0.0)
    return jnp.where(live, moved, 0.0).astype(bf16)


def pass_kernel(tile_ref, count_ref, halo_ref, sides_ref, x_ref, edge_ref, r_ref, foot_ref, trace_ref, den_ref,
                movie_ref, new_trace_ref, new_r_ref, pay_ref, wide_halo, err):
    tile, count = tile_ref[0], count_ref[0]
    comps = trace_ref.shape[0]

    def body(n):
        trace = trace_step(n, tile, count, halo_ref, sides_ref, x_ref, edge_ref, r_ref, foot_ref, trace_ref, den_ref,
                           wide_halo, err)
        new_trace_ref[:n, :] = trace
        if n < comps:
            new_trace_ref[n:, :] = jnp.zeros((comps - n, trace.shape[1]), bf16)
        for g in range(0, SIDE // BAND, TALL):
            resid_bands(g, tile, movie_ref, foot_ref, trace, new_r_ref, pay_ref)

    by_live(count, comps, body)


def last_kernel(block, share, tile_ref, count_ref, halo_ref, sides_ref, x_ref, edge_ref, r_ref, foot_ref, trace_ref,
                den_ref, movie_ref, cr_ref, cc_ref, rad_ref, slot_ref,
                trace_hbm, part_hbm, fold_ref, wide_halo, err, back, masked, new_trace, part_ref, sems):
    tile, count = tile_ref[0], count_ref[0]
    comps = trace_ref.shape[0]
    half, taken = fold_ref.shape
    band = BAND * SIDE

    def body(n):
        trace = trace_step(n, tile, count, halo_ref, sides_ref, x_ref, edge_ref, r_ref, foot_ref, trace_ref, den_ref,
                           wide_halo, err, back)
        new_trace[:n, :] = trace
        if n < comps:
            new_trace[n:, :] = jnp.zeros((comps - n, trace.shape[1]), bf16)
        stores = [pltpu.make_async_copy(new_trace, trace_hbm, sems.at[2])]
        stores[0].start()
        tf = trace.astype(f32)
        energy = jnp.sum(tf * tf, axis=1, keepdims=True)
        energy = jnp.transpose(jnp.broadcast_to(energy, (n, LANES)))[:1]
        high = energy.astype(bf16).astype(f32)
        low = energy - high
        at = lax.broadcasted_iota(i32, (half, taken), 0)
        fold = jnp.where(at == slot_ref[...], 1.0, 0.0).astype(bf16)
        fold_ref[...] = fold
        inner = lax.rem(lax.broadcasted_iota(i32, (half, n), 0), block)
        gap_sq = col_gap_sq(cc_ref[:, :n])
        cr, rad = cr_ref[:, :n], rad_ref[:, :n]
        for h in range(2):
            for g in range(h, SIDE // BAND, 2):
                rows = pl.ds(g * band, band)
                prod = dot(foot_ref[rows, :n], trace)
                old = back[pl.ds(g * BAND, BAND)].reshape(band, prod.shape[1]).astype(f32)
                ferr = (prod + old - movie_ref[rows, :].astype(f32)).astype(bf16)
                grad = lax.dot_general(ferr, trace, (((1,), (1,)), ((), ())), preferred_element_type=f32)
                for i in range(BAND):
                    keep = gap_sq <= disc_limit(cr, rad, count, g * BAND + i)
                    masked[h, pl.ds(g // 2 * band + i * SIDE, SIDE), :n] = jnp.where(
                        keep, grad[i * SIDE : (i + 1) * SIDE], 0.0).astype(bf16)
            part = dot(fold, masked[h, :, :n])
            part = jnp.where(inner == share, high, jnp.where(inner == share + 1, low, part))
            rows = pl.ds(h * half, half)
            part_ref[rows, :n] = part.astype(bf16)
            if n < comps:
                part_ref[rows, n:] = jnp.zeros((half, comps - n), bf16)
            stores.append(pltpu.make_async_copy(part_ref.at[rows, :], part_hbm.at[rows, :], sems.at[h]))
            stores[-1].start()
        for store in stores:
            store.wait()

    by_live(count, comps, body)


def foot_fold_kernel(fold_ref, foot_ref, out_ref):
    half = fold_ref.shape[0]
    band = BAND * SIDE
    for h in range(2):
        foot = jnp.concatenate(
            [foot_ref[g * band : (g + 1) * band, :] for g in range(h, SIDE // BAND, 2)], axis=0)
        out_ref[h * half : (h + 1) * half, :] = dot(fold_ref[...], foot)


def share_kernel(share, me_ref, parts_ref, ffold_ref, out_ref):
    parts, block, comps = parts_ref.shape
    total = jnp.zeros((block, comps), f32)
    for j in range(parts):
        total = total + parts_ref[j].astype(f32)
    den = total[share : share + 1] + total[share + 1 : share + 2] + RIDGE
    foot = ffold_ref[pl.ds(pl.multiple_of(me_ref[0] * block, 8), block), :]
    moved = jnp.maximum(foot - total / den, 0.0).astype(bf16)
    for j in range(parts):
        out_ref[j] = moved


def unfold_kernel(count_ref, all_ref, fold_ref, cr_ref, cc_ref, rad_ref, out_hbm, buf, sems):
    count = count_ref[0]
    half = fold_ref.shape[0]
    gap_sq = col_gap_sq(cc_ref[...])
    cr, rad = cr_ref[...], rad_ref[...]
    band = BAND * SIDE
    stores = []
    for g in range(SIDE // BAND):
        h, b = g % 2, g // 2
        wide = lax.dot_general(fold_ref[:, b * band : (b + 1) * band], all_ref[h * half : (h + 1) * half, :],
                               (((0,), (0,)), ((), ())), preferred_element_type=f32)
        for i in range(BAND):
            row = g * BAND + i
            keep = gap_sq <= disc_limit(cr, rad, count, row)
            buf[pl.ds(row * SIDE, SIDE), :] = jnp.where(keep, wide[i * SIDE : (i + 1) * SIDE], 0.0).astype(bf16)
        rows = pl.ds(g * band, band)
        stores.append(pltpu.make_async_copy(buf.at[rows, :], out_hbm.at[rows, :], sems.at[g]))
        stores[-1].start()
    for store in stores:
        store.wait()


def swap(x):
    count = lax.axis_size("tile")
    return lax.ppermute(x, "tile", [(i, count - 1 - i) for i in range(count)])


def shards(movie, cycle_weights, footprints, traces, centre_row, centre_col, radius, comp_count):
    assert lax.axis_size("tile") == 2
    parts = lax.axis_size("tm")
    movie, fp, tr = movie[0], footprints[0], traces[0]
    weights = jnp.swapaxes(cycle_weights[0], 0, 1)
    pixels, frames = movie.shape
    comps = tr.shape[0]
    band = BAND * SIDE
    bands = SIDE // BAND
    edge = SIDE * CYCLE
    tile = lax.axis_index("tile").astype(i32).reshape(1)
    me = lax.axis_index("tm").astype(i32).reshape(1)
    own, beside = band_tables()
    slots, share, block = fold_rows(parts)
    packed = parts * block
    sds = jax.ShapeDtypeStruct
    halo_pad = pltpu.VMEM((edge + 2 * CYCLE * CYCLE, frames), bf16)
    err_buf = pltpu.VMEM((pixels, frames), bf16)
    one_row = pltpu.VMEM((1, comps), i32)

    r_shape = sds((SIDE, SIDE, frames), bf16)
    inputs = [pltpu.with_memory_space_constraint(v, pltpu.HBM) for v in (
        movie, fp, tr, centre_row, centre_col, radius, weights, jnp.asarray(own), jnp.asarray(beside))]
    foot, trace, den, r, pay, movie, band_w, side_w = pl.pallas_call(
        start_kernel,
        out_shape=(sds((pixels, comps), bf16), sds((comps, frames), bf16), sds((comps, LANES), f32),
                   r_shape, sds((edge, frames), bf16), sds((pixels, frames), bf16),
                   sds((bands, 2, BAND * HALF, RANGE), bf16), sds((bands // TALL,) + beside.shape[1:], bf16)),
        in_specs=[SM, SM] + [HB] * 9, out_specs=[VM] * 8,
        scratch_shapes=[pltpu.VMEM((pixels, comps), bf16), pltpu.VMEM((comps, frames), bf16),
                        one_row, one_row, one_row, pltpu.VMEM(weights.shape, bf16), pltpu.VMEM(own.shape, i32),
                        pltpu.VMEM(beside.shape[1:], i32), pltpu.VMEM((pixels, LANES), f32),
                        pltpu.VMEM((2, bands * SIDE, RANGE - LANES), f32), pltpu.SemaphoreType.DMA((2 * bands + 7,))],
        compiler_params=params(16),
    )(tile, comp_count, *inputs)
    banded = pl.pallas_call(
        banded_kernel,
        out_shape=(r_shape, sds((SIDE, CYCLE, frames), f32)), in_specs=[SM, VM, VM], out_specs=[VM, VM],
        compiler_params=params(),
        cost_estimate=pl.CostEstimate(flops=4_000_000_000, bytes_accessed=20_000_000, transcendentals=0),
    )
    halo = swap(pay)
    x, beyond = banded(tile, band_w, r)
    trace, new_r, pay = pl.pallas_call(
        pass_kernel,
        out_shape=(sds((comps, frames), bf16), r_shape, sds((edge, frames), bf16)),
        in_specs=[SM, SM] + [VM] * 9, out_specs=[VM] * 3,
        scratch_shapes=[halo_pad, err_buf], compiler_params=params(),
    )(tile, comp_count, halo, side_w, x, beyond, r, foot, trace, den, movie)
    r = new_r
    halo = swap(pay)
    x, beyond = banded(tile, band_w, r)
    trace, part, fold = pl.pallas_call(
        functools.partial(last_kernel, block, share),
        out_shape=(sds((comps, frames), bf16), sds((packed, comps), bf16), sds((packed // 2, slots.shape[1]), bf16)),
        in_specs=[SM, SM] + [VM] * 13, out_specs=[HB, HB, VM],
        scratch_shapes=[halo_pad, err_buf, pltpu.VMEM(r_shape.shape, bf16), pltpu.VMEM((2, pixels // 2, comps), bf16),
                        pltpu.VMEM((comps, frames), bf16), pltpu.VMEM((packed, comps), bf16),
                        pltpu.SemaphoreType.DMA((3,))],
        compiler_params=params(14),
    )(tile, comp_count, halo, side_w, x, beyond, r, foot, trace, den, movie, centre_row, centre_col, radius, jnp.asarray(slots))
    received = lax.all_to_all(part.reshape(parts, block, comps), "tm", 0, 0, tiled=False)
    ffold = pl.pallas_call(
        foot_fold_kernel,
        out_shape=sds((packed, comps), f32),
        in_specs=[VM, VM], out_specs=VM, compiler_params=params(),
    )(fold, foot)
    moved = pl.pallas_call(
        functools.partial(share_kernel, share),
        out_shape=sds((parts, block, comps), bf16),
        in_specs=[SM, VM, VM], out_specs=VM, compiler_params=params(),
    )(me, received, ffold)
    every = lax.all_to_all(moved, "tm", 0, 0, tiled=False).reshape(packed, comps)
    new_foot = pl.pallas_call(
        unfold_kernel,
        out_shape=sds((pixels, comps), bf16),
        in_specs=[SM] + [VM] * 5, out_specs=HB,
        scratch_shapes=[pltpu.VMEM((pixels, comps), bf16), pltpu.SemaphoreType.DMA((bands,))],
        compiler_params=params(),
    )(comp_count, every, fold, centre_row, centre_col, radius)
    return (new_foot[None], trace[None])


def solution(mesh):
    in_specs = (
        P(("groups", "tile"), None, "tm"),
        P(("groups", "tile"), None, None),
        P(("groups", "tile"), None, None),
        P(("groups", "tile"), None, "tm"),
        P(("groups", "tile"), None),
        P(("groups", "tile"), None),
        P(("groups", "tile"), None),
        P(("groups", "tile")),
    )
    out_specs = (P(("groups", "tile"), None, None), P(("groups", "tile"), None, "tm"))
    return jax.shard_map(shards, mesh=mesh, in_specs=in_specs, out_specs=out_specs, check_vma=False)
```

```python
import functools

import jax
import jax.numpy as jnp
import numpy as np
from jax import lax
from jax.experimental import pallas as pl
from jax.experimental.pallas import tpu as pltpu
from jax.sharding import PartitionSpec as P

SIDE = 48
CYCLE = 8
PASSES = 2
RIDGE = 1.0
MAX_RADIUS = 9
BAND = 8
LANES = 128
OFFS_PAD = 64
GROUP = 256
TALL = 2
HALF = SIDE // 2
REACH = HALF + CYCLE
COL_STEP = SIDE - REACH
RANGE = (BAND + 2 * CYCLE) * REACH

FOLD_R = 16
FOLD_C = 19
FOLD_SHIFT = 9
SLOTS = FOLD_R * FOLD_C

f32 = jnp.float32
bf16 = jnp.bfloat16
i32 = jnp.int32


def cycle_offsets():
    found = []
    for dy in range(-CYCLE, CYCLE + 1):
        for dx in range(-CYCLE, CYCLE + 1):
            if CYCLE * CYCLE <= dy * dy + dx * dx < (CYCLE + 1) * (CYCLE + 1):
                found.append((dy, dx))
    return found


def band_tables():
    offsets = cycle_offsets()
    none = len(offsets)
    own = np.full((OFFS_PAD + 8, LANES), -1, np.int32)
    own[OFFS_PAD] = SIDE
    beside = np.full((2, TALL * BAND, CYCLE, TALL * BAND + 2 * CYCLE, CYCLE), none, np.int32)
    for o, (dy, dx) in enumerate(offsets):
        own[o] = (CYCLE + dy) * REACH + dx + CYCLE
        own[OFFS_PAD, o] = dx
        for i in range(TALL * BAND):
            for q in range(CYCLE):
                h = q + dx - CYCLE
                if 0 <= h < CYCLE:
                    beside[0, i, q, i + CYCLE + dy, h] = o
                h = q + dx + CYCLE
                if 0 <= h < CYCLE:
                    beside[1, i, q, i + CYCLE + dy, h] = o
    return own, beside.reshape(2, TALL * BAND * CYCLE, -1)


def fold_rows(parts):
    share = -(-SLOTS // parts)
    block = -(-(share + 2) // 8) * 8
    assert SLOTS // 2 % share == 0 and FOLD_R == 2 * BAND
    low = np.arange(SIDE // FOLD_R)[:, None, None]
    row, col = np.arange(BAND)[:, None], np.arange(SIDE)
    slot = row * FOLD_C + (col + FOLD_SHIFT * low) % FOLD_C
    return (slot // share * block + slot % share).astype(np.int32).reshape(1, -1), share, block


def params(mib=12):
    return pltpu.CompilerParams(vmem_limit_bytes=mib * 2**20)


VM = pl.BlockSpec(memory_space=pltpu.VMEM)
HB = pl.BlockSpec(memory_space=pltpu.HBM)
SM = pl.BlockSpec(memory_space=pltpu.SMEM)


def dot(a, b):
    return jnp.dot(a, b, preferred_element_type=f32)


def disc_limit(centre_row, radius, count, row):
    gap = row - centre_row
    live = lax.broadcasted_iota(i32, centre_row.shape, 1) < count
    return jnp.where(live, radius * radius - gap * gap, -1)


def col_gap_sq(centre_col):
    gap = lax.broadcasted_iota(i32, (SIDE, centre_col.shape[1]), 0) - centre_col
    return gap * gap


def by_live(count, comps, body):
    few = min(GROUP, comps)
    pl.when(count <= few)(functools.partial(body, few))
    if few < comps:
        pl.when(count > few)(functools.partial(body, comps))


def resid_bands(g, tile, movie_ref, foot_ref, trace, d_ref, r_ref, pay_ref):
    rows, wide = pl.ds(g * BAND, TALL * BAND), pl.ds(g * BAND * SIDE, TALL * BAND * SIDE)
    d = movie_ref[wide, :].astype(f32) - dot(foot_ref[wide, : trace.shape[0]], trace)
    d3 = d.reshape(TALL * BAND, SIDE, d.shape[1])
    d_ref[rows] = d3
    r_ref[rows] = d3.astype(bf16)
    edge = jnp.where(tile == 0, d3[:, SIDE - CYCLE :], d3[:, :CYCLE])
    edge = edge.reshape(TALL * BAND * CYCLE, d.shape[1]).astype(bf16)
    pay_ref[pl.ds(g * BAND * CYCLE, TALL * BAND * CYCLE), :] = edge


def build_bands(tile, w, own_ref, beside, bands_ref, sides_ref, weights, wide):
    bands = SIDE // BAND
    blocks = RANGE // LANES
    offs = w.shape[0]
    eye = lax.broadcasted_iota(i32, (offs, LANES), 0) == lax.broadcasted_iota(i32, (offs, LANES), 1)
    weights[...] = lax.dot_general(w, jnp.where(eye, 1.0, 0.0).astype(bf16), (((0,), (0,)), ((), ())),
                                   preferred_element_type=f32)
    at = own_ref[:OFFS_PAD, :1]
    from_col = lax.broadcasted_iota(i32, (SIDE, LANES), 0) + own_ref[OFFS_PAD : OFFS_PAD + 1, :]
    inside = (from_col >= 0) & (from_col < SIDE)
    per = LANES // REACH
    taken = wide.shape[2]
    target = lax.broadcasted_iota(i32, (OFFS_PAD, taken), 1)
    nothing = jnp.zeros((8, LANES), f32)
    for b in range(per):
        pick = jnp.where(target == jnp.where(at < 0, -1, at + b * REACH), 1.0, 0.0).astype(bf16)
        for k in range(BAND // per):
            rows = [weights[pl.ds((g * BAND + b + k * per) * SIDE, SIDE), :] for g in range(bands)]
            rows = [jnp.where(inside, row, 0.0)[:, :OFFS_PAD].astype(bf16) for row in rows]
            wide[k] = dot(jnp.concatenate(rows, axis=0), pick)
        for g in range(bands):
            for h in range(2):
                start = g * SIDE + h * HALF
                shift = (h * (HALF - COL_STEP) - CYCLE) % LANES
                turned = [[pltpu.roll(wide[k, start : start + HALF, v * LANES : (v + 1) * LANES], shift, 1,
                                      stride=1, stride_axis=0) for v in range(taken // LANES)]
                          for k in range(BAND // per)]
                for v in range(blocks):
                    for t in range(HALF // 8):
                        pieces = [turned[k][v - k][t * 8 : (t + 1) * 8] if 0 <= v - k < taken // LANES else nothing
                                  for k in range(BAND // per)]
                        first = t * BAND * 8 + b * len(pieces) * 8
                        bands_ref[g, h, first : first + len(pieces) * 8, v * LANES : (v + 1) * LANES] = (
                            jnp.concatenate(pieces, axis=0).astype(bf16))
    for g in range(bands // TALL):
        edges = []
        for i in range(TALL * BAND):
            base = (g * TALL * BAND + i) * SIDE
            edges.append(jnp.where(tile == 0, weights[base + SIDE - CYCLE : base + SIDE, :],
                                   weights[base : base + CYCLE, :]))
        edge = jnp.concatenate(edges, axis=0)
        for v in range(beside.shape[1] // LANES):
            lanes = slice(v * LANES, (v + 1) * LANES)
            sides_ref[g, :, lanes] = jnp.take_along_axis(edge, beside[:, lanes], axis=1).astype(bf16)


def start_kernel(tile_ref, count_ref, movie_hbm, fp_hbm, tr_hbm, cr_hbm, cc_hbm, rad_hbm,
                 w_hbm, own_hbm, beside_hbm,
                 foot_ref, trace_ref, den_ref, d_ref, r_ref, pay_ref, movie_ref, bands_ref, sides_ref,
                 fp_ref, tr_ref, cr_ref, cc_ref, rad_ref, w_ref, own_ref, beside_ref, weights, wide, sems):
    count, tile = count_ref[0], tile_ref[0]
    comps = tr_ref.shape[0]
    band = BAND * SIDE
    bands = SIDE // BAND
    small = [pltpu.make_async_copy(src, dst, sems.at[2 * bands + n]) for n, (src, dst) in enumerate(
        ((w_hbm, w_ref), (own_hbm, own_ref), (beside_hbm.at[tile], beside_ref),
         (cr_hbm, cr_ref), (cc_hbm, cc_ref), (rad_hbm, rad_ref), (tr_hbm, tr_ref)))]
    fps, movies = [], []
    for g in range(bands):
        rows = pl.ds(g * band, band)
        fps.append(pltpu.make_async_copy(fp_hbm.at[rows, :], fp_ref.at[rows, :], sems.at[g]))
        movies.append(pltpu.make_async_copy(movie_hbm.at[rows, :], movie_ref.at[rows, :], sems.at[bands + g]))
    for copy in small:
        copy.start()
    for g in range(bands):
        fps[g].start()
        movies[g].start()
    for copy in small[:3]:
        copy.wait()
    build_bands(tile, w_ref[...], own_ref, beside_ref[...], bands_ref, sides_ref, weights, wide)
    for copy in small[3:] + fps + movies:
        copy.wait()

    def rest(n):
        live = lax.broadcasted_iota(i32, (n, 1), 0) < count
        trace = jnp.where(live, tr_ref[:n, :].astype(f32), 0.0).astype(bf16)
        trace_ref[:n, :] = trace
        gap_sq = col_gap_sq(cc_ref[:, :n])
        cr, rad = cr_ref[:, :n], rad_ref[:, :n]
        total = jnp.zeros((8, n), f32)
        for g in range(bands):
            for i in range(BAND):
                row = g * BAND + i
                keep = gap_sq <= disc_limit(cr, rad, count, row)
                foot = jnp.where(keep, fp_ref[pl.ds(row * SIDE, SIDE), :n].astype(f32), 0.0)
                foot_ref[pl.ds(row * SIDE, SIDE), :n] = foot.astype(bf16)
                total = total + jnp.sum((foot * foot).reshape(SIDE // 8, 8, n), axis=0)
            if g % TALL == TALL - 1:
                resid_bands(g + 1 - TALL, tile, movie_ref, foot_ref, trace, d_ref, r_ref, pay_ref)
        energy = jnp.sum(total, axis=0, keepdims=True) + RIDGE
        den_ref[:n, :] = jnp.transpose(jnp.broadcast_to(1.0 / energy, (LANES, n)))
        if n < comps:
            trace_ref[n:, :] = jnp.zeros((comps - n, trace.shape[1]), bf16)
            foot_ref[:, n:] = jnp.zeros((foot_ref.shape[0], comps - n), bf16)

    by_live(count, comps, rest)


def banded_kernel(tile_ref, bands_ref, r_ref, x_ref, edge_ref):
    tile = tile_ref[0]
    frames = r_ref.shape[2]
    for g in range(SIDE // BAND):
        low = max(0, CYCLE - g * BAND)
        high = min(BAND + 2 * CYCLE, SIDE + CYCLE - g * BAND)
        first = g * BAND + low - CYCLE
        halves = []
        for h in range(2):
            r = r_ref[first : first + high - low, h * COL_STEP : h * COL_STEP + REACH, :]
            x = dot(bands_ref[g, h, :, low * REACH : high * REACH], r.reshape((high - low) * REACH, frames))
            per = LANES // REACH
            x = x.reshape(HALF // 8, per, BAND // per, 8, frames)
            rows = [jnp.concatenate([x[t, i % per, i // per] for t in range(HALF // 8)], axis=0) for i in range(BAND)]
            halves.append(jnp.stack(rows))
        rows = pl.ds(g * BAND, BAND)
        edge_ref[rows] = jnp.where(tile == 0, halves[1][:, HALF - CYCLE :], halves[0][:, :CYCLE])
        x_ref[rows] = jnp.concatenate(halves, axis=1).astype(bf16)


def trace_step(n, tile, count, halo_ref, sides_ref, x_ref, edge_ref, d_ref, foot_ref, trace_ref, den_ref,
               wide_halo, err, back_ref=None):
    frames = x_ref.shape[2]
    edge = CYCLE * SIDE
    pad = CYCLE * CYCLE
    wide_halo[:pad, :] = jnp.zeros((pad, frames), bf16)
    wide_halo[pl.ds(pad, edge), :] = halo_ref[...]
    tail = wide_halo.shape[0] - pad - edge
    wide_halo[pl.ds(pad + edge, tail), :] = jnp.zeros((tail, frames), bf16)
    tall = TALL * BAND
    for g in range(SIDE // tall):
        rows = pl.ds(g * tall, tall)
        reach = sides_ref.shape[2]
        side = dot(sides_ref[g], wide_halo[pl.ds(g * tall * CYCLE, reach), :]).reshape(tall, CYCLE, frames)
        side = (edge_ref[rows] + side).astype(bf16).astype(f32)
        x = x_ref[rows].astype(f32)
        left = jnp.where(tile == 0, x[:, :CYCLE], side)
        right = jnp.where(tile == 0, side, x[:, SIDE - CYCLE :])
        back = jnp.concatenate([left, x[:, CYCLE : SIDE - CYCLE], right], axis=1)
        if back_ref is not None:
            back_ref[rows] = back.astype(bf16)
        wide = (back - d_ref[rows]).reshape(tall * SIDE, frames)
        err[pl.ds(g * tall * SIDE, tall * SIDE), :] = wide.astype(bf16)
    grad = lax.dot_general(foot_ref[:, :n], err[...], (((0,), (0,)), ((), ())), preferred_element_type=f32)
    live = lax.broadcasted_iota(i32, (n, 1), 0) < count
    moved = jnp.maximum(trace_ref[:n, :].astype(f32) - grad * den_ref[:n, :1], 0.0)
    return jnp.where(live, moved, 0.0).astype(bf16)


def pass_kernel(tile_ref, count_ref, halo_ref, sides_ref, x_ref, edge_ref, d_ref, foot_ref, trace_ref, den_ref,
                movie_ref, new_trace_ref, new_d_ref, new_r_ref, pay_ref, wide_halo, err):
    tile, count = tile_ref[0], count_ref[0]
    comps = trace_ref.shape[0]

    def body(n):
        trace = trace_step(n, tile, count, halo_ref, sides_ref, x_ref, edge_ref, d_ref, foot_ref, trace_ref, den_ref,
                           wide_halo, err)
        new_trace_ref[:n, :] = trace
        if n < comps:
            new_trace_ref[n:, :] = jnp.zeros((comps - n, trace.shape[1]), bf16)
        for g in range(0, SIDE // BAND, TALL):
            resid_bands(g, tile, movie_ref, foot_ref, trace, new_d_ref, new_r_ref, pay_ref)

    by_live(count, comps, body)


def last_kernel(block, share, tile_ref, count_ref, halo_ref, sides_ref, x_ref, edge_ref, d_ref, foot_ref, trace_ref,
                den_ref, movie_ref, cr_ref, cc_ref, rad_ref, slot_ref,
                trace_hbm, part_hbm, fold_ref, wide_halo, err, back, masked, new_trace, part_ref, sems):
    tile, count = tile_ref[0], count_ref[0]
    comps = trace_ref.shape[0]
    half, taken = fold_ref.shape
    band = BAND * SIDE

    def body(n):
        trace = trace_step(n, tile, count, halo_ref, sides_ref, x_ref, edge_ref, d_ref, foot_ref, trace_ref, den_ref,
                           wide_halo, err, back)
        new_trace[:n, :] = trace
        if n < comps:
            new_trace[n:, :] = jnp.zeros((comps - n, trace.shape[1]), bf16)
        stores = [pltpu.make_async_copy(new_trace, trace_hbm, sems.at[2])]
        stores[0].start()
        tf = trace.astype(f32)
        energy = jnp.sum(tf * tf, axis=1, keepdims=True)
        energy = jnp.transpose(jnp.broadcast_to(energy, (n, LANES)))[:1]
        high = energy.astype(bf16).astype(f32)
        low = energy - high
        at = lax.broadcasted_iota(i32, (half, taken), 0)
        fold = jnp.where(at == slot_ref[...], 1.0, 0.0).astype(bf16)
        fold_ref[...] = fold
        inner = lax.rem(lax.broadcasted_iota(i32, (half, n), 0), block)
        gap_sq = col_gap_sq(cc_ref[:, :n])
        cr, rad = cr_ref[:, :n], rad_ref[:, :n]
        for h in range(2):
            for g in range(h, SIDE // BAND, 2):
                rows = pl.ds(g * band, band)
                prod = dot(foot_ref[rows, :n], trace)
                old = back[pl.ds(g * BAND, BAND)].reshape(band, prod.shape[1]).astype(f32)
                ferr = (prod + old - movie_ref[rows, :].astype(f32)).astype(bf16)
                grad = lax.dot_general(ferr, trace, (((1,), (1,)), ((), ())), preferred_element_type=f32)
                for i in range(BAND):
                    keep = gap_sq <= disc_limit(cr, rad, count, g * BAND + i)
                    masked[h, pl.ds(g // 2 * band + i * SIDE, SIDE), :n] = jnp.where(
                        keep, grad[i * SIDE : (i + 1) * SIDE], 0.0).astype(bf16)
            part = dot(fold, masked[h, :, :n])
            part = jnp.where(inner == share, high, jnp.where(inner == share + 1, low, part))
            rows = pl.ds(h * half, half)
            part_ref[rows, :n] = part.astype(bf16)
            if n < comps:
                part_ref[rows, n:] = jnp.zeros((half, comps - n), bf16)
            stores.append(pltpu.make_async_copy(part_ref.at[rows, :], part_hbm.at[rows, :], sems.at[h]))
            stores[-1].start()
        for store in stores:
            store.wait()

    by_live(count, comps, body)


def foot_fold_kernel(fold_ref, foot_ref, out_ref):
    half = fold_ref.shape[0]
    band = BAND * SIDE
    for h in range(2):
        foot = jnp.concatenate(
            [foot_ref[g * band : (g + 1) * band, :] for g in range(h, SIDE // BAND, 2)], axis=0)
        out_ref[h * half : (h + 1) * half, :] = dot(fold_ref[...], foot)


def share_kernel(share, me_ref, parts_ref, ffold_ref, out_ref):
    parts, block, comps = parts_ref.shape
    total = jnp.zeros((block, comps), f32)
    for j in range(parts):
        total = total + parts_ref[j].astype(f32)
    den = total[share : share + 1] + total[share + 1 : share + 2] + RIDGE
    foot = ffold_ref[pl.ds(pl.multiple_of(me_ref[0] * block, 8), block), :]
    moved = jnp.maximum(foot - total / den, 0.0).astype(bf16)
    for j in range(parts):
        out_ref[j] = moved


def unfold_kernel(count_ref, all_ref, fold_ref, cr_ref, cc_ref, rad_ref, out_hbm, buf, sems):
    count = count_ref[0]
    half = fold_ref.shape[0]
    gap_sq = col_gap_sq(cc_ref[...])
    cr, rad = cr_ref[...], rad_ref[...]
    band = BAND * SIDE
    stores = []
    for g in range(SIDE // BAND):
        h, b = g % 2, g // 2
        wide = lax.dot_general(fold_ref[:, b * band : (b + 1) * band], all_ref[h * half : (h + 1) * half, :],
                               (((0,), (0,)), ((), ())), preferred_element_type=f32)
        for i in range(BAND):
            row = g * BAND + i
            keep = gap_sq <= disc_limit(cr, rad, count, row)
            buf[pl.ds(row * SIDE, SIDE), :] = jnp.where(keep, wide[i * SIDE : (i + 1) * SIDE], 0.0).astype(bf16)
        rows = pl.ds(g * band, band)
        stores.append(pltpu.make_async_copy(buf.at[rows, :], out_hbm.at[rows, :], sems.at[g]))
        stores[-1].start()
    for store in stores:
        store.wait()


def swap(x):
    count = lax.axis_size("tile")
    return lax.ppermute(x, "tile", [(i, count - 1 - i) for i in range(count)])


def shards(movie, cycle_weights, footprints, traces, centre_row, centre_col, radius, comp_count):
    assert lax.axis_size("tile") == 2
    parts = lax.axis_size("tm")
    movie, fp, tr = movie[0], footprints[0], traces[0]
    weights = jnp.swapaxes(cycle_weights[0], 0, 1)
    pixels, frames = movie.shape
    comps = tr.shape[0]
    band = BAND * SIDE
    bands = SIDE // BAND
    edge = SIDE * CYCLE
    tile = lax.axis_index("tile").astype(i32).reshape(1)
    me = lax.axis_index("tm").astype(i32).reshape(1)
    own, beside = band_tables()
    slots, share, block = fold_rows(parts)
    packed = parts * block
    sds = jax.ShapeDtypeStruct
    halo_pad = pltpu.VMEM((edge + 2 * CYCLE * CYCLE, frames), bf16)
    err_buf = pltpu.VMEM((pixels, frames), bf16)
    one_row = pltpu.VMEM((1, comps), i32)

    d_shape, r_shape = sds((SIDE, SIDE, frames), f32), sds((SIDE, SIDE, frames), bf16)
    inputs = [pltpu.with_memory_space_constraint(v, pltpu.HBM) for v in (
        movie, fp, tr, centre_row, centre_col, radius, weights, jnp.asarray(own), jnp.asarray(beside))]
    foot, trace, den, d, r, pay, movie, band_w, side_w = pl.pallas_call(
        start_kernel,
        out_shape=(sds((pixels, comps), bf16), sds((comps, frames), bf16), sds((comps, LANES), f32),
                   d_shape, r_shape, sds((edge, frames), bf16), sds((pixels, frames), bf16),
                   sds((bands, 2, BAND * HALF, RANGE), bf16), sds((bands // TALL,) + beside.shape[1:], bf16)),
        in_specs=[SM, SM] + [HB] * 9, out_specs=[VM] * 9,
        scratch_shapes=[pltpu.VMEM((pixels, comps), bf16), pltpu.VMEM((comps, frames), bf16),
                        one_row, one_row, one_row, pltpu.VMEM(weights.shape, bf16), pltpu.VMEM(own.shape, i32),
                        pltpu.VMEM(beside.shape[1:], i32), pltpu.VMEM((pixels, LANES), f32),
                        pltpu.VMEM((2, bands * SIDE, RANGE - LANES), f32), pltpu.SemaphoreType.DMA((2 * bands + 7,))],
        compiler_params=params(16),
    )(tile, comp_count, *inputs)
    banded = pl.pallas_call(
        banded_kernel,
        out_shape=(r_shape, sds((SIDE, CYCLE, frames), f32)), in_specs=[SM, VM, VM], out_specs=[VM, VM],
        compiler_params=params(),
        cost_estimate=pl.CostEstimate(flops=4_000_000_000, bytes_accessed=20_000_000, transcendentals=0),
    )
    halo = swap(pay)
    x, beyond = banded(tile, band_w, r)
    trace, new_d, r, pay = pl.pallas_call(
        pass_kernel,
        out_shape=(sds((comps, frames), bf16), d_shape, r_shape, sds((edge, frames), bf16)),
        in_specs=[SM, SM] + [VM] * 9, out_specs=[VM] * 4,
        scratch_shapes=[halo_pad, err_buf], compiler_params=params(),
    )(tile, comp_count, halo, side_w, x, beyond, d, foot, trace, den, movie)
    d = new_d
    halo = swap(pay)
    x, beyond = banded(tile, band_w, r)
    trace, part, fold = pl.pallas_call(
        functools.partial(last_kernel, block, share),
        out_shape=(sds((comps, frames), bf16), sds((packed, comps), bf16), sds((packed // 2, slots.shape[1]), bf16)),
        in_specs=[SM, SM] + [VM] * 13, out_specs=[HB, HB, VM],
        scratch_shapes=[halo_pad, err_buf, pltpu.VMEM(r_shape.shape, bf16), pltpu.VMEM((2, pixels // 2, comps), bf16),
                        pltpu.VMEM((comps, frames), bf16), pltpu.VMEM((packed, comps), bf16),
                        pltpu.SemaphoreType.DMA((3,))],
        compiler_params=params(14),
    )(tile, comp_count, halo, side_w, x, beyond, d, foot, trace, den, movie, centre_row, centre_col, radius, jnp.asarray(slots))
    received = lax.all_to_all(part.reshape(parts, block, comps), "tm", 0, 0, tiled=False)
    ffold = pl.pallas_call(
        foot_fold_kernel,
        out_shape=sds((packed, comps), f32),
        in_specs=[VM, VM], out_specs=VM, compiler_params=params(),
    )(fold, foot)
    moved = pl.pallas_call(
        functools.partial(share_kernel, share),
        out_shape=sds((parts, block, comps), bf16),
        in_specs=[SM, VM, VM], out_specs=VM, compiler_params=params(),
    )(me, received, ffold)
    every = lax.all_to_all(moved, "tm", 0, 0, tiled=False).reshape(packed, comps)
    new_foot = pl.pallas_call(
        unfold_kernel,
        out_shape=sds((pixels, comps), bf16),
        in_specs=[SM] + [VM] * 5, out_specs=HB,
        scratch_shapes=[pltpu.VMEM((pixels, comps), bf16), pltpu.SemaphoreType.DMA((bands,))],
        compiler_params=params(),
    )(comp_count, every, fold, centre_row, centre_col, radius)
    return (new_foot[None], trace[None])


def solution(mesh):
    in_specs = (
        P(("groups", "tile"), None, "tm"),
        P(("groups", "tile"), None, None),
        P(("groups", "tile"), None, None),
        P(("groups", "tile"), None, "tm"),
        P(("groups", "tile"), None),
        P(("groups", "tile"), None),
        P(("groups", "tile"), None),
        P(("groups", "tile")),
    )
    out_specs = (P(("groups", "tile"), None, None), P(("groups", "tile"), None, "tm"))
    return jax.shard_map(shards, mesh=mesh, in_specs=in_specs, out_specs=out_specs, check_vma=False)
```
